512 devices in a mesh: gx: 16 (over y_lo, z), gy: 8 (over y_hi, core), gz: 4 (over x).
Axes of the slice: x: 4, y: 8 (y_hi: 4, y_lo: 2; y = y_hi * 2 + y_lo), z: 8, core: 2. Of those that a mesh axis runs over, the one named last changes fastest.
Arguments:
- fields: float32 [4, 128, 256, 512], P(None, 'gx', 'gy', 'gz'), may hold values from -6 to 6
- velocity: float32 [3, 128, 256, 512], P(None, 'gx', 'gy', 'gz'), may hold values from -3 to 3
- diffusivity: float32 [4], replicated, may hold values from 0.05 to 0.5
- coupling: float32 [4, 4], replicated, may hold values from -1 to 1
- factor_x: float32 [128, 32], P('gx'), may hold values from -1 to 1, as said below
- factor_y: float32 [256, 32], P('gy'), may hold values from -1 to 1, as said below
- factor_z: float32 [512, 32], P('gz'), may hold values from -1 to 1, as said below
Outputs:
- core_tensor: float32 [4, 32, 32, 32], P(None, 'gx', 'gy', 'gz')
The draws below stay inside these ranges and needn't reach their ends.
Inputs may be any that keep to these rules, and one draw needn't show every extreme that they name: `factor_x`: the columns of each factor are orthonormal. `factor_y`: the columns of each factor are orthonormal. `factor_z`: the columns of each factor are orthonormal.
All inputs are finite; a program needn't handle non-finite values.
Results may differ from the reference program's by a relative error of at most 0.0003.
Values sent between devices are 32-bit elements; how exact they have to be, the bound alone decides.
No kernel may reach another device: no remote copies, remote signals or barrier semaphores. Data moves between devices by JAX's collectives and lax.ppermute only.
A program may use at most 64 MiB of HBM per device.

```python
import math
import jax
import jax.numpy as jnp
from jax import lax

VARS = 4
R = 32
STEPS = 2
NX = 128
NY = 256
NZ = 512


def orthonormal(key, rows, salt):
    normal_draw = jax.random.normal(jax.random.fold_in(key, salt), (rows, R), jnp.float32)
    basis, upper = jnp.linalg.qr(normal_draw)
    return basis


def draw_factor_x(key, part):
    return orthonormal(key, NX, 11)


def draw_factor_y(key, part):
    return orthonormal(key, NY, 23)


def draw_factor_z(key, part):
    return orthonormal(key, NZ, 37)


def draw_fields(key, part):
    base = jax.random.fold_in(key, 51)
    rough_key = jax.random.fold_in(base, 1)
    phase_key = jax.random.fold_in(base, 2)
    shape = (VARS, NX, NY, NZ)
    rough = 0.8 * jnp.clip(jax.random.normal(rough_key, shape, jnp.float32), -3.5, 3.5)
    amplitude = 0.8
    phases = jax.random.uniform(phase_key, (VARS, 2), jnp.float32, -math.pi, math.pi)
    cells_y = jnp.arange(NY, dtype=jnp.float32)
    cells_z = jnp.arange(NZ, dtype=jnp.float32)
    wave_y = jnp.cos(0.5 * math.pi * cells_y[None, :] + phases[:, 0:1])
    wave_z = jnp.cos(0.5 * math.pi * cells_z[None, :] + phases[:, 1:2])
    wave = wave_y[:, None, :, None] * wave_z[:, None, None, :]
    return jnp.clip(rough + amplitude * wave, -6.0, 6.0)


def draw_velocity(key, part):
    base = jax.random.fold_in(key, 67)
    sign_key = jax.random.fold_in(base, 1)
    size_key = jax.random.fold_in(base, 2)
    heading = jnp.where(jax.random.bernoulli(sign_key, 0.5, (3, 1, 1, 1)), 1.0, -1.0).astype(jnp.float32)
    lowest = 1.5
    magnitude = jax.random.uniform(size_key, (3, NX, NY, NZ), jnp.float32, lowest, 3.0)
    return heading * magnitude


def normal_values(rng, extent, deviation, bound, kind=jnp.bfloat16):
    drawn = deviation * jax.random.normal(rng, extent, jnp.float32)
    return jnp.clip(drawn, min=-bound, max=bound).astype(kind)


def setup_inputs(seed: int = 0) -> dict:
    seeds = jax.random.split(jax.random.key(seed), 8)
    fields = draw_fields(jax.random.fold_in(seeds[7], 71), 0)
    velocity = draw_velocity(jax.random.fold_in(seeds[7], 71), 0)
    diffusivity = jnp.clip(jnp.exp(jax.random.uniform(seeds[2], (VARS,), jnp.float32, math.log(0.05), math.log(0.5))), 0.05, 0.5)
    coupling = normal_values(seeds[3], (VARS, VARS), 0.2, 1.0, jnp.float32)
    factor_x = draw_factor_x(jax.random.fold_in(seeds[7], 71), 0)
    factor_y = draw_factor_y(jax.random.fold_in(seeds[7], 71), 0)
    factor_z = draw_factor_z(jax.random.fold_in(seeds[7], 71), 0)
    return dict(fields=fields, velocity=velocity, diffusivity=diffusivity, coupling=coupling, factor_x=factor_x, factor_y=factor_y, factor_z=factor_z)


time_step = 0.2

def offset_view(padded, dimension, offset):
    indices = [slice(None)]
    for other in (1, 2, 3):
        if other == dimension:
            first_cell = 2 + offset
            indices.append(slice(first_cell, first_cell + padded.shape[other] - 4))
        else:
            indices.append(slice(2, padded.shape[other] - 2))
    return padded[tuple(indices)]

def tendency(padded, velocity, diffusivity, coupling):
    center = offset_view(padded, 1, 0)
    transport = jnp.zeros_like(center)
    laplace = jnp.zeros_like(center)
    for dimension in (1, 2, 3):
        gradient = (8.0 * (offset_view(padded, dimension, 1) - offset_view(padded, dimension, -1)) - (offset_view(padded, dimension, 2) - offset_view(padded, dimension, -2))) / 12.0
        transport = transport + velocity[dimension - 1][None] * gradient
        laplace = laplace + offset_view(padded, dimension, 1) + offset_view(padded, dimension, -1) - 2.0 * center
    mixing = jnp.einsum('vw,wxyz->vxyz', coupling, center, precision=lax.Precision.HIGHEST)
    return -transport + diffusivity[:, None, None, None] * laplace + center * mixing

def pad_zeros(values):
    return jnp.pad(values, ((0, 0), (2, 2), (2, 2), (2, 2)))

def reference(fields, velocity, diffusivity, coupling, factor_x, factor_y, factor_z):
    state = fields
    for repeat in range(STEPS):
        section = state + time_step * tendency(pad_zeros(state), velocity, diffusivity, coupling)
        state = 0.5 * (state + section + time_step * tendency(pad_zeros(section), velocity, diffusivity, coupling))
    highest = lax.Precision.HIGHEST
    partial_value = jnp.einsum('vxyz,zc->vxyc', state, factor_z, precision=highest)
    partial_value = jnp.einsum('vxyc,yb->vxbc', partial_value, factor_y, precision=highest)
    return jnp.einsum('vxbc,xa->vabc', partial_value, factor_x, precision=highest)
```

```python
import jax
import jax.numpy as jnp
from jax import lax
from jax.experimental import pallas as pl
from jax.experimental.pallas import tpu as pltpu
from jax.sharding import PartitionSpec as P

TIME_STEP = 0.2
F32 = jnp.float32
HIGHEST = lax.Precision.HIGHEST
PLANES, ROWS = 24, 64
LOW, HIGH = 8, 16


def vmem():
    return pl.BlockSpec(memory_space=pltpu.VMEM)


def smem():
    return pl.BlockSpec(memory_space=pltpu.SMEM)


def f32(*shape):
    return jax.ShapeDtypeStruct(shape, F32)


def call(kernel, out_shape, in_specs, name, scratch=(), work=1000000):
    many = isinstance(out_shape, (list, tuple))
    return pl.pallas_call(
        kernel,
        out_shape=out_shape,
        in_specs=in_specs,
        out_specs=[vmem() for _ in out_shape] if many else vmem(),
        scratch_shapes=list(scratch),
        cost_estimate=pl.CostEstimate(flops=work, bytes_accessed=work, transcendentals=0),
        name=name,
    )


def lanes_of(rows):
    return lax.broadcasted_iota(jnp.int32, (rows, 128), 1)


def within(lane, first, size):
    return (lane >= first) & (lane < first + size)


def pack_xz(f, v, x_up, x_down, z_up, z_down):
    lane = lanes_of(32)
    for i in range(4):
        for x in range(8):
            plane = f[i, x]
            x_up[i * 8 + x] = plane
            x_down[i * 8 + x] = plane
    for a in range(3):
        for j in range(6):
            x_up[32 + a * 6 + j] = v[a, 2 + j]
            x_down[32 + a * 6 + j] = v[a, j]

    def plane_edges(x, carry):
        up = jnp.zeros((32, 128), F32)
        down = jnp.zeros((32, 128), F32)
        for i in range(4):
            plane = f[i, x]
            up = jnp.where(within(lane, 32 * i, 8), pltpu.roll(plane, (32 * i + 8) % 128, 1), up)
            down = jnp.where(within(lane, 32 * i + 24, 8), pltpu.roll(plane, 32 * i + 24, 1), down)
        for a in range(3):
            plane = v[a, x]
            up = jnp.where(within(lane, 32 * a + 8, 8), pltpu.roll(plane, 32 * a + 16, 1), up)
            down = jnp.where(within(lane, 32 * a + 16, 8), pltpu.roll(plane, 32 * a + 16, 1), down)
        z_up[x] = up
        z_down[x] = down
        return carry

    lax.fori_loop(0, 8, plane_edges, 0)


def pack_y(f, v, z_left, z_right, y_up, y_down):
    for out, row in ((y_up, 24), (y_down, 0)):
        for x in range(8):
            for i in range(4):
                out[i * 8 + x] = f[i, x, row : row + 8]
            for a in range(3):
                out[32 + a * 8 + x] = v[a, x, row : row + 8]
            out[56 + x] = z_left[x, row : row + 8] + z_right[x, row : row + 8]


def pack_x2(z_left, z_right, y_low, y_high, up, down):
    for out, first, first4 in ((up, 2, 4), (down, 0, 0)):
        for side, rows in ((0, y_low), (1, y_high)):
            for i in range(4):
                for j in range(6):
                    out[(i * 6 + j) * 2 + side] = rows[i * 8 + first + j]
            for a in range(3):
                for j in range(4):
                    out[48 + (a * 4 + j) * 2 + side] = rows[32 + a * 8 + first4 + j]
            for j in range(4):
                out[96 + j * 2 + side] = rows[56 + first4 + j]
        for j in range(6):
            halo = z_left[first + j] + z_right[first + j]
            for t in range(4):
                out[72 + j * 4 + t] = halo[8 * t : 8 * t + 8]


def spread_factor(fz, out):
    lane = lanes_of(128)
    wide = jnp.concatenate([fz[...], jnp.zeros((128, 96), F32)], axis=1)
    for v in range(4):
        placed = jnp.zeros((128, 128), F32)
        for k in range(4):
            rolled = pltpu.roll(wide, (24 * k + 8 * v) % 128, 1)
            placed = jnp.where(within(lane, 32 * k + 8 * v, 8), rolled, placed)
        out[v] = placed


def advance(
    d, c, f, v, z_left, z_right, x_low, x_high, y_low, y_high, e_low, e_high, rhs, fy,
    out, state, section, edge, edge2, wind, edge_wind, zm, final, mixed,
):
    gx, gy, gz = (lax.axis_index(n) for n in ("gx", "gy", "gz"))
    last_x, last_y, last_z = (lax.axis_size(n) - 1 for n in ("gx", "gy", "gz"))
    x_first, x_end = jnp.where(gx == 0, LOW, 0), jnp.where(gx == last_x, HIGH, PLANES)
    y_first, y_end = jnp.where(gy == 0, 16, 0), jnp.where(gy == last_y, 48, ROWS)
    scale = TIME_STEP / 12.0

    for i in range(4):
        for x in range(8):
            state[i, 8 + x, 16:48] = f[i, x]
            state[i, x, 16:48] = x_low[i * 8 + x]
            state[i, 16 + x, 16:48] = x_high[i * 8 + x]
            state[i, 8 + x, 8:16] = y_low[i * 8 + x]
            state[i, 8 + x, 48:56] = y_high[i * 8 + x]
        for j in range(6):
            for first, e in ((2, e_low), (16, e_high)):
                state[i, first + j, 8:16] = e[(i * 6 + j) * 2]
                state[i, first + j, 48:56] = e[(i * 6 + j) * 2 + 1]
    for a in range(3):
        for x in range(8):
            wind[a, 8 + x, 16:48] = v[a, x] * scale
            wind[a, 8 + x, 8:16] = y_low[32 + a * 8 + x] * scale
            wind[a, 8 + x, 48:56] = y_high[32 + a * 8 + x] * scale
        for j in range(6):
            wind[a, 2 + j, 16:48] = x_low[32 + a * 6 + j] * scale
            wind[a, 16 + j, 16:48] = x_high[32 + a * 6 + j] * scale
        for j in range(4):
            for first, e in ((4, e_low), (16, e_high)):
                wind[a, first + j, 8:16] = e[48 + (a * 4 + j) * 2] * scale
                wind[a, first + j, 48:56] = e[48 + (a * 4 + j) * 2 + 1] * scale
    for x in range(8):
        zm[8 + x, 16:48] = z_left[x] + z_right[x]
        zm[8 + x, 8:16] = y_low[56 + x]
        zm[8 + x, 48:56] = y_high[56 + x]
    for j in range(6):
        for first, e in ((2, e_low), (16, e_high)):
            for t in range(4):
                zm[first + j, 16 + 8 * t : 24 + 8 * t] = e[72 + j * 4 + t]
    for j in range(4):
        for first, e in ((4, e_low), (16, e_high)):
            zm[first + j, 8:16] = e[96 + j * 2]
            zm[first + j, 48:56] = e[96 + j * 2 + 1]

    def chunk(rows):
        lane = lanes_of(rows)
        return lane, lane % 32, lax.broadcasted_iota(jnp.int32, (rows, 128), 0)

    def roll(value, by):
        return pltpu.roll(value, by % 128, 1)

    def slabs(x, r, rows, winds):
        lane, in_group, _ = chunk(rows)
        halo = zm[x, r : r + rows]
        tile = halo
        for i in range(4):
            q = state[i, x, r : r + rows]
            tile = jnp.where(within(lane, 32 * i + 8, 8), roll(q, 32 * i + 8), tile)
            tile = jnp.where(within(lane, 32 * i + 16, 8), roll(q, 32 * i + 24), tile)
        edge[x, r : r + rows] = tile
        if winds:
            halo = halo * scale
            packed = jnp.where(in_group < 8, roll(halo, -8), roll(halo, 8))
            for a in range(3):
                q = wind[a, x, r : r + rows]
                packed = jnp.where(within(lane, 32 * a + 8, 8), roll(q, 32 * a + 8), packed)
                packed = jnp.where(within(lane, 32 * a + 16, 8), roll(q, 32 * a + 24), packed)
            for a in range(3):
                one = jnp.where(within(lane, 32 * a, 32), packed, 0.0)
                one = one + roll(one, 32)
                edge_wind[a, x, r : r + rows] = one + roll(one, 64)

    @pl.loop(4, 20)
    def _(x):
        for r in (8, 24, 40):
            slabs(x, r, 16, True)

    @pl.loop(0, 4)
    def _(j):
        x = jnp.where(j < 2, 2 + j, 18 + j)
        for r in (16, 32):
            slabs(x, r, 16, False)

    dd = [d[i] * TIME_STEP for i in range(4)]
    cc = [[c[i, w] * TIME_STEP for w in range(4)] for i in range(4)]

    def terms(plus, minus, plus2, minus2):
        return 8.0 * (plus - minus) - (plus2 - minus2), plus + minus

    def tendencies(src, slab, x, r, rows):
        lane, in_group, _ = chunk(rows)
        at = slice(r, r + rows)
        u = [wind[a, x, at] for a in range(3)]
        q = [src[i, x, at] for i in range(4)]
        s = slab[x, at]
        s = jnp.where(in_group >= 24, s, roll(s, 16))
        results = []
        for i in range(4):
            ends = roll(s, -24 - 32 * i)
            gz_, lz = terms(
                roll(jnp.where(lane == 0, ends, q[i]), -1),
                roll(jnp.where(lane == 127, ends, q[i]), 1),
                roll(jnp.where(lane < 2, ends, q[i]), -2),
                roll(jnp.where(lane >= 126, ends, q[i]), 2),
            )
            gx_, lx = terms(src[i, x + 1, at], src[i, x - 1, at], src[i, x + 2, at], src[i, x - 2, at])
            gy_, ly = terms(*(src[i, x, r + o : r + o + rows] for o in (1, -1, 2, -2)))
            mix = cc[i][0] * q[0] + cc[i][1] * q[1] + (cc[i][2] * q[2] + cc[i][3] * q[3])
            moved = u[0] * gx_ + u[1] * gy_ + u[2] * gz_
            results.append(dd[i] * (lx + ly + lz) - moved + q[i] * (mix - 6.0 * dd[i]))
        return q, results

    def slab_tendency(slab, x, r, rows):
        lane, _, _ = chunk(rows)
        group = lane // 32
        at = slice(r, r + rows)

        def by_group(values):
            return jnp.where(group < 2, jnp.where(group == 0, values[0], values[1]),
                             jnp.where(group == 2, values[2], values[3]))

        q = slab[x, at]
        gz_, lz = terms(roll(q, -1), roll(q, 1), roll(q, -2), roll(q, 2))
        gx_, lx = terms(slab[x + 1, at], slab[x - 1, at], slab[x + 2, at], slab[x - 2, at])
        gy_, ly = terms(*(slab[x, r + o : r + o + rows] for o in (1, -1, 2, -2)))
        mix = -6.0 * by_group(dd)
        for k in range(4):
            mix = mix + by_group([cc[i][(i - k) % 4] for i in range(4)]) * roll(q, 32 * k)
        moved = edge_wind[0, x, at] * gx_ + edge_wind[1, x, at] * gy_ + edge_wind[2, x, at] * gz_
        return q, by_group(dd) * (lx + ly + lz) - moved + q * mix

    def inside(x, r, rows):
        _, in_group, row = chunk(rows)
        first = jnp.where((x >= x_first) & (x < x_end), y_first, ROWS)
        ok = (row + r >= first) & (row + r < y_end)
        z_ok = ((in_group >= 8) | (gz != 0)) & ((in_group < 24) | (gz != last_z))
        return ok, z_ok

    def half(base, q, t):
        return 0.5 * (base + q + t)

    def stage(x, rows_at, slab_rows, src, slab, dst, slab_dst, mean):
        for r in rows_at:
            at = slice(r, r + 16)
            ok, _ = inside(x, r, 16)
            q, t = tendencies(src, slab, x, r, 16)
            for i in range(4):
                new = half(dst[i, x, at], q[i], t[i]) if mean else q[i] + t[i]
                dst[i, x, at] = jnp.where(ok, new, 0.0)
        for r in slab_rows:
            at = slice(r, r + 16)
            ok, z_ok = inside(x, r, 16)
            q, t = slab_tendency(slab, x, r, 16)
            new = half(slab_dst[x, at], q, t) if mean else q + t
            slab_dst[x, at] = jnp.where(ok & z_ok, new, 0.0)

    full, own = (8, 24, 40), (16, 32)

    @pl.loop(4, 20)
    def _(x):
        stage(x, full, full, state, edge, section, edge2, False)

    @pl.loop(0, 4)
    def _(j):
        stage(jnp.where(j < 2, 2 + j, 18 + j), own, (), state, edge, section, edge2, False)

    @pl.loop(6, 18)
    def _(x):
        stage(x, full, full, section, edge2, state, edge, True)

    @pl.loop(0, 4)
    def _(j):
        stage(jnp.where(j < 2, 4 + j, 16 + j), own, (), section, edge2, state, edge, True)

    @pl.loop(8, 16)
    def _(x):
        stage(x, full, own, state, edge, section, edge2, False)

    @pl.loop(0, 4)
    def _(j):
        stage(jnp.where(j < 2, 6 + j, 14 + j), own, (), state, edge, section, edge2, False)

    @pl.loop(0, 8)
    def _(x):
        for r in own:
            q, t = tendencies(section, edge2, 8 + x, r, 16)
            for i in range(4):
                row = pl.multiple_of(x * 32 + (r - 16), 16)
                final[i, pl.ds(row, 16)] = half(state[i, 8 + x, r : r + 16], q[i], t[i])

    total = jnp.dot(final[0], rhs[0], precision=HIGHEST, preferred_element_type=F32)
    for i in range(1, 4):
        total = total + jnp.dot(final[i], rhs[i], precision=HIGHEST, preferred_element_type=F32)
    for x in range(8):
        mixed[x * 32 : x * 32 + 32] = jnp.dot(
            fy[...], total[x * 32 : x * 32 + 32], precision=HIGHEST, preferred_element_type=F32
        )
    lane = lanes_of(8)
    for j in range(8):
        tiles = [mixed[pl.ds(4 * j + b, 8, stride=32), :] for b in range(4)]
        for k in range(4):
            tile = jnp.zeros((8, 128), F32)
            for b in range(4):
                tile = jnp.where(within(lane, 32 * b, 32), roll(tiles[b], 32 * (b - k)), tile)
            out[j * 4 + k] = tile


def contract_x(parts, fx, out):
    total = parts[0]
    for p in range(1, parts.shape[0]):
        total = total + parts[p]
    out[...] = jnp.dot(fx[...], total, precision=HIGHEST, preferred_element_type=F32)


def local(fields, velocity, diffusivity, coupling, factor_x, factor_y, factor_z):
    def both_ways(axis, up, down):
        pairs = [(i, i + 1) for i in range(lax.axis_size(axis) - 1)]
        return (
            lax.ppermute(up, axis, pairs),
            lax.ppermute(down, axis, [(b, a) for a, b in pairs]),
        )

    x_up, x_down, z_up, z_down = call(
        pack_xz, [f32(50, 32, 128)] * 2 + [f32(8, 32, 128)] * 2, [vmem()] * 2, "pack_xz"
    )(fields, velocity)
    x_low, x_high = both_ways("gx", x_up, x_down)
    z_left, z_right = both_ways("gz", z_up, z_down)
    y_up, y_down = call(pack_y, [f32(64, 8, 128)] * 2, [vmem()] * 4, "pack_y")(
        fields, velocity, z_left, z_right
    )
    y_low, y_high = both_ways("gy", y_up, y_down)
    e_up, e_down = call(pack_x2, [f32(104, 8, 128)] * 2, [vmem()] * 4, "pack_x2")(
        z_left, z_right, y_low, y_high
    )
    e_low, e_high = both_ways("gx", e_up, e_down)
    rhs = call(spread_factor, f32(4, 128, 128), [vmem()], "spread_factor")(factor_z)

    def tiles(*lead):
        return pltpu.VMEM((*lead, ROWS, 128), F32)

    gy, gz, gx = (lax.axis_size(n) for n in ("gy", "gz", "gx"))
    parts = call(
        advance,
        f32(32, 8, 128),
        [smem()] * 2 + [vmem()] * 12,
        "advance",
        scratch=[
            tiles(4, PLANES), tiles(4, PLANES), tiles(PLANES), tiles(PLANES),
            tiles(3, PLANES), tiles(3, PLANES), tiles(PLANES),
            pltpu.VMEM((4, 256, 128), F32), pltpu.VMEM((256, 128), F32),
        ],
        work=10000000,
    )(
        diffusivity, coupling, fields, velocity, z_left, z_right, x_low, x_high, y_low, y_high,
        e_low, e_high, rhs, factor_y.T,
    )
    parts = lax.all_to_all(parts, ("gy", "gz"), 0, 0, tiled=True)
    slices = call(contract_x, f32(32, 128), [vmem()] * 2, "contract_x")(parts, factor_x.T)
    slices = lax.all_to_all(slices, "gx", 0, 0, tiled=True)
    core = jnp.sum(slices.reshape(gx, 32 // gx, 4, 4, 8), axis=0)
    return core.transpose(2, 0, 1, 3)


def solution(mesh):
    return jax.shard_map(
        local,
        mesh=mesh,
        in_specs=(
            P(None, "gx", "gy", "gz"),
            P(None, "gx", "gy", "gz"),
            P(),
            P(),
            P("gx", None),
            P("gy", None),
            P("gz", None),
        ),
        out_specs=P(None, "gx", "gy", "gz"),
        check_vma=False,
    )
```

```python
import jax
import jax.numpy as jnp
from jax import lax
from jax.experimental import pallas as pl
from jax.experimental.pallas import tpu as pltpu
from jax.sharding import PartitionSpec as P

TIME_STEP = 0.2
F32 = jnp.float32
HIGHEST = lax.Precision.HIGHEST
PLANES, ROWS = 24, 64
LOW, HIGH = 8, 16


def vmem():
    return pl.BlockSpec(memory_space=pltpu.VMEM)


def smem():
    return pl.BlockSpec(memory_space=pltpu.SMEM)


def f32(*shape):
    return jax.ShapeDtypeStruct(shape, F32)


def call(kernel, out_shape, in_specs, name, scratch=(), work=1000000, mib=8):
    many = isinstance(out_shape, (list, tuple))
    return pl.pallas_call(
        kernel,
        out_shape=out_shape,
        in_specs=in_specs,
        out_specs=[vmem() for _ in out_shape] if many else vmem(),
        scratch_shapes=list(scratch),
        compiler_params=pltpu.CompilerParams(vmem_limit_bytes=mib << 20),
        cost_estimate=pl.CostEstimate(flops=work, bytes_accessed=work, transcendentals=0),
        name=name,
    )


def lanes_of(rows):
    return lax.broadcasted_iota(jnp.int32, (rows, 128), 1)


def within(lane, first, size):
    return (lane >= first) & (lane < first + size)


def dot(a, b, a_dim, b_dim):
    return lax.dot_general(
        a, b, (((a_dim,), (b_dim,)), ((), ())), precision=HIGHEST, preferred_element_type=F32
    )


def pack_xz(f, v, x_up, x_down, z_up, z_down):
    lane = lanes_of(32)
    for i in range(4):
        for x in range(8):
            plane = f[i, x]
            x_up[i * 8 + x] = plane
            x_down[i * 8 + x] = plane
    for a in range(3):
        for j in range(6):
            x_up[32 + a * 6 + j] = v[a, 2 + j]
            x_down[32 + a * 6 + j] = v[a, j]

    def plane_edges(x, carry):
        up = jnp.zeros((32, 128), F32)
        down = jnp.zeros((32, 128), F32)
        for i in range(4):
            plane = f[i, x]
            up = jnp.where(within(lane, 32 * i, 8), pltpu.roll(plane, (32 * i + 8) % 128, 1), up)
            down = jnp.where(within(lane, 32 * i + 24, 8), pltpu.roll(plane, 32 * i + 24, 1), down)
        for a in range(3):
            plane = v[a, x]
            up = jnp.where(within(lane, 32 * a + 8, 8), pltpu.roll(plane, 32 * a + 16, 1), up)
            down = jnp.where(within(lane, 32 * a + 16, 8), pltpu.roll(plane, 32 * a + 16, 1), down)
        z_up[x] = up
        z_down[x] = down
        return carry

    lax.fori_loop(0, 8, plane_edges, 0)


def pack_y(f, v, z_left, z_right, y_up, y_down):
    for out, row in ((y_up, 24), (y_down, 0)):
        for x in range(8):
            for i in range(4):
                out[i * 8 + x] = f[i, x, row : row + 8]
            for a in range(3):
                out[32 + a * 8 + x] = v[a, x, row : row + 8]
            out[56 + x] = z_left[x, row : row + 8] + z_right[x, row : row + 8]


def pack_x2(z_left, z_right, y_low, y_high, up, down):
    for out, first, first4 in ((up, 2, 4), (down, 0, 0)):
        for side, rows in ((0, y_low), (1, y_high)):
            for i in range(4):
                for j in range(6):
                    out[(i * 6 + j) * 2 + side] = rows[i * 8 + first + j]
            for a in range(3):
                for j in range(4):
                    out[48 + (a * 4 + j) * 2 + side] = rows[32 + a * 8 + first4 + j]
            for j in range(4):
                out[96 + j * 2 + side] = rows[56 + first4 + j]
        for j in range(6):
            halo = z_left[first + j] + z_right[first + j]
            for t in range(4):
                out[72 + j * 4 + t] = halo[8 * t : 8 * t + 8]


def advance(
    d, c, f, v, z_left, z_right, x_low, x_high, y_low, y_high, e_low, e_high, fz, fy,
    out, state, section, edge, edge2, wind, edge_wind, zm, final, mixed, rhs,
):
    gx, gy, gz = (lax.axis_index(n) for n in ("gx", "gy", "gz"))
    last_x, last_y, last_z = (lax.axis_size(n) - 1 for n in ("gx", "gy", "gz"))
    x_first, x_end = jnp.where(gx == 0, LOW, 0), jnp.where(gx == last_x, HIGH, PLANES)
    y_first, y_end = jnp.where(gy == 0, 16, 0), jnp.where(gy == last_y, 48, ROWS)
    scale = TIME_STEP / 12.0

    for i in range(4):
        for x in range(8):
            state[i, 8 + x, 16:48] = f[i, x]
            state[i, x, 16:48] = x_low[i * 8 + x]
            state[i, 16 + x, 16:48] = x_high[i * 8 + x]
            state[i, 8 + x, 8:16] = y_low[i * 8 + x]
            state[i, 8 + x, 48:56] = y_high[i * 8 + x]
        for j in range(6):
            for first, e in ((2, e_low), (16, e_high)):
                state[i, first + j, 8:16] = e[(i * 6 + j) * 2]
                state[i, first + j, 48:56] = e[(i * 6 + j) * 2 + 1]
    for a in range(3):
        for x in range(8):
            wind[a, 8 + x, 16:48] = v[a, x] * scale
            wind[a, 8 + x, 8:16] = y_low[32 + a * 8 + x] * scale
            wind[a, 8 + x, 48:56] = y_high[32 + a * 8 + x] * scale
        for j in range(6):
            wind[a, 2 + j, 16:48] = x_low[32 + a * 6 + j] * scale
            wind[a, 16 + j, 16:48] = x_high[32 + a * 6 + j] * scale
        for j in range(4):
            for first, e in ((4, e_low), (16, e_high)):
                wind[a, first + j, 8:16] = e[48 + (a * 4 + j) * 2] * scale
                wind[a, first + j, 48:56] = e[48 + (a * 4 + j) * 2 + 1] * scale
    for x in range(8):
        zm[8 + x, 16:48] = z_left[x] + z_right[x]
        zm[8 + x, 8:16] = y_low[56 + x]
        zm[8 + x, 48:56] = y_high[56 + x]
    for j in range(6):
        for first, e in ((2, e_low), (16, e_high)):
            for t in range(4):
                zm[first + j, 16 + 8 * t : 24 + 8 * t] = e[72 + j * 4 + t]
    for j in range(4):
        for first, e in ((4, e_low), (16, e_high)):
            zm[first + j, 8:16] = e[96 + j * 2]
            zm[first + j, 48:56] = e[96 + j * 2 + 1]

    def chunk(rows):
        lane = lanes_of(rows)
        return lane, lane % 32, lax.broadcasted_iota(jnp.int32, (rows, 128), 0)

    def roll(value, by):
        return pltpu.roll(value, by % 128, 1)

    def slabs(x, r, rows, winds):
        lane, in_group, _ = chunk(rows)
        halo = zm[x, r : r + rows]
        tile = halo
        for i in range(4):
            q = state[i, x, r : r + rows]
            tile = jnp.where(within(lane, 32 * i + 8, 8), roll(q, 32 * i + 8), tile)
            tile = jnp.where(within(lane, 32 * i + 16, 8), roll(q, 32 * i + 24), tile)
        edge[x, r : r + rows] = tile
        if winds:
            halo = halo * scale
            packed = jnp.where(in_group < 8, roll(halo, -8), roll(halo, 8))
            for a in range(3):
                q = wind[a, x, r : r + rows]
                packed = jnp.where(within(lane, 32 * a + 8, 8), roll(q, 32 * a + 8), packed)
                packed = jnp.where(within(lane, 32 * a + 16, 8), roll(q, 32 * a + 24), packed)
            for a in range(3):
                one = jnp.where(within(lane, 32 * a, 32), packed, 0.0)
                one = one + roll(one, 32)
                edge_wind[a, x, r : r + rows] = one + roll(one, 64)

    @pl.loop(4, 20)
    def _(x):
        for r in (8, 24, 40):
            slabs(x, r, 16, True)

    @pl.loop(0, 4)
    def _(j):
        x = jnp.where(j < 2, 2 + j, 18 + j)
        for r in (16, 32):
            slabs(x, r, 16, False)

    dd = [d[i] * TIME_STEP for i in range(4)]
    cc = [[c[i, w] * TIME_STEP for w in range(4)] for i in range(4)]

    def terms(plus, minus, plus2, minus2):
        return 8.0 * (plus - minus) - (plus2 - minus2), plus + minus

    def tendencies(src, slab, x, r, rows):
        lane, in_group, _ = chunk(rows)
        at = slice(r, r + rows)
        u = [wind[a, x, at] for a in range(3)]
        q = [src[i, x, at] for i in range(4)]
        s = slab[x, at]
        s = jnp.where(in_group >= 24, s, roll(s, 16))
        results = []
        for i in range(4):
            ends = roll(s, -24 - 32 * i)
            gz_, lz = terms(
                roll(jnp.where(lane == 0, ends, q[i]), -1),
                roll(jnp.where(lane == 127, ends, q[i]), 1),
                roll(jnp.where(lane < 2, ends, q[i]), -2),
                roll(jnp.where(lane >= 126, ends, q[i]), 2),
            )
            gx_, lx = terms(src[i, x + 1, at], src[i, x - 1, at], src[i, x + 2, at], src[i, x - 2, at])
            gy_, ly = terms(*(src[i, x, r + o : r + o + rows] for o in (1, -1, 2, -2)))
            mix = cc[i][0] * q[0] + cc[i][1] * q[1] + (cc[i][2] * q[2] + cc[i][3] * q[3])
            moved = u[0] * gx_ + u[1] * gy_ + u[2] * gz_
            results.append(dd[i] * (lx + ly + lz) - moved + q[i] * (mix - 6.0 * dd[i]))
        return q, results

    def slab_tendency(slab, x, r, rows):
        lane, _, _ = chunk(rows)
        group = lane // 32
        at = slice(r, r + rows)

        def by_group(values):
            return jnp.where(group < 2, jnp.where(group == 0, values[0], values[1]),
                             jnp.where(group == 2, values[2], values[3]))

        q = slab[x, at]
        gz_, lz = terms(roll(q, -1), roll(q, 1), roll(q, -2), roll(q, 2))
        gx_, lx = terms(slab[x + 1, at], slab[x - 1, at], slab[x + 2, at], slab[x - 2, at])
        gy_, ly = terms(*(slab[x, r + o : r + o + rows] for o in (1, -1, 2, -2)))
        mix = -6.0 * by_group(dd)
        for k in range(4):
            mix = mix + by_group([cc[i][(i - k) % 4] for i in range(4)]) * roll(q, 32 * k)
        moved = edge_wind[0, x, at] * gx_ + edge_wind[1, x, at] * gy_ + edge_wind[2, x, at] * gz_
        return q, by_group(dd) * (lx + ly + lz) - moved + q * mix

    def inside(x, r, rows):
        _, in_group, row = chunk(rows)
        first = jnp.where((x >= x_first) & (x < x_end), y_first, ROWS)
        ok = (row + r >= first) & (row + r < y_end)
        z_ok = ((in_group >= 8) | (gz != 0)) & ((in_group < 24) | (gz != last_z))
        return ok, z_ok

    def half(base, q, t):
        return 0.5 * (base + q + t)

    def stage(x, rows_at, slab_rows, src, slab, dst, slab_dst, mean):
        for r in rows_at:
            at = slice(r, r + 16)
            ok, _ = inside(x, r, 16)
            q, t = tendencies(src, slab, x, r, 16)
            for i in range(4):
                new = half(dst[i, x, at], q[i], t[i]) if mean else q[i] + t[i]
                dst[i, x, at] = jnp.where(ok, new, 0.0)
        for r in slab_rows:
            at = slice(r, r + 16)
            ok, z_ok = inside(x, r, 16)
            q, t = slab_tendency(slab, x, r, 16)
            new = half(slab_dst[x, at], q, t) if mean else q + t
            slab_dst[x, at] = jnp.where(ok & z_ok, new, 0.0)

    full, own = (8, 24, 40), (16, 32)

    @pl.loop(4, 20)
    def _(x):
        stage(x, full, full, state, edge, section, edge2, False)

    @pl.loop(0, 4)
    def _(j):
        stage(jnp.where(j < 2, 2 + j, 18 + j), own, (), state, edge, section, edge2, False)

    @pl.loop(6, 18)
    def _(x):
        stage(x, full, full, section, edge2, state, edge, True)

    @pl.loop(0, 4)
    def _(j):
        stage(jnp.where(j < 2, 4 + j, 16 + j), own, (), section, edge2, state, edge, True)

    @pl.loop(8, 16)
    def _(x):
        stage(x, full, own, state, edge, section, edge2, False)

    @pl.loop(0, 4)
    def _(j):
        stage(jnp.where(j < 2, 6 + j, 14 + j), own, (), state, edge, section, edge2, False)

    @pl.loop(0, 8)
    def _(x):
        for r in own:
            q, t = tendencies(section, edge2, 8 + x, r, 16)
            for i in range(4):
                row = pl.multiple_of(x * 32 + (r - 16), 16)
                final[i, pl.ds(row, 16)] = half(state[i, 8 + x, r : r + 16], q[i], t[i])

    rhs[...] = jnp.zeros((4, 128, 128), F32)
    for i in range(4):
        for k in range(4):
            rhs[i, 32 * k + 8 * i : 32 * k + 8 * i + 8] = fz[8 * k : 8 * k + 8]
    total = dot(final[0], rhs[0], 1, 1)
    for i in range(1, 4):
        total = total + dot(final[i], rhs[i], 1, 1)
    for x in range(8):
        mixed[x * 32 : x * 32 + 32] = dot(fy[...], total[x * 32 : x * 32 + 32], 0, 0)
    lane = lanes_of(8)
    for j in range(8):
        tiles = [mixed[pl.ds(4 * j + b, 8, stride=32), :] for b in range(4)]
        for k in range(4):
            tile = jnp.zeros((8, 128), F32)
            for b in range(4):
                tile = jnp.where(within(lane, 32 * b, 32), roll(tiles[b], 32 * (b - k)), tile)
            out[j * 4 + k] = tile


def contract_x(parts, fx, out):
    total = parts[0]
    for p in range(1, parts.shape[0]):
        total = total + parts[p]
    out[...] = dot(fx[...], total, 0, 0)


def local(fields, velocity, diffusivity, coupling, factor_x, factor_y, factor_z):
    def both_ways(axis, up, down):
        pairs = [(i, i + 1) for i in range(lax.axis_size(axis) - 1)]
        return (
            lax.ppermute(up, axis, pairs),
            lax.ppermute(down, axis, [(b, a) for a, b in pairs]),
        )

    x_up, x_down, z_up, z_down = call(
        pack_xz, [f32(50, 32, 128)] * 2 + [f32(8, 32, 128)] * 2, [vmem()] * 2, "pack_xz"
    )(fields, velocity)
    x_low, x_high = both_ways("gx", x_up, x_down)
    z_left, z_right = both_ways("gz", z_up, z_down)
    y_up, y_down = call(pack_y, [f32(64, 8, 128)] * 2, [vmem()] * 4, "pack_y")(
        fields, velocity, z_left, z_right
    )
    y_low, y_high = both_ways("gy", y_up, y_down)
    e_up, e_down = call(pack_x2, [f32(104, 8, 128)] * 2, [vmem()] * 4, "pack_x2")(
        z_left, z_right, y_low, y_high
    )
    e_low, e_high = both_ways("gx", e_up, e_down)

    def tiles(*lead):
        return pltpu.VMEM((*lead, ROWS, 128), F32)

    gy, gz, gx = (lax.axis_size(n) for n in ("gy", "gz", "gx"))
    parts = call(
        advance,
        f32(32, 8, 128),
        [smem()] * 2 + [vmem()] * 12,
        "advance",
        scratch=[
            tiles(4, PLANES), tiles(4, PLANES), tiles(PLANES), tiles(PLANES),
            tiles(3, PLANES), tiles(3, PLANES), tiles(PLANES),
            pltpu.VMEM((4, 256, 128), F32), pltpu.VMEM((256, 128), F32),
            pltpu.VMEM((4, 128, 128), F32),
        ],
        work=10000000,
        mib=24,
    )(
        diffusivity, coupling, fields, velocity, z_left, z_right, x_low, x_high, y_low, y_high,
        e_low, e_high, factor_z.T, factor_y,
    )
    parts = lax.all_to_all(parts, ("gy", "gz"), 0, 0, tiled=True)
    slices = call(contract_x, f32(32, 128), [vmem()] * 2, "contract_x")(parts, factor_x)
    slices = lax.all_to_all(slices, "gx", 0, 0, tiled=True)
    core = jnp.sum(slices.reshape(gx, 32 // gx, 4, 4, 8), axis=0)
    return core.transpose(2, 0, 1, 3)


def solution(mesh):
    return jax.shard_map(
        local,
        mesh=mesh,
        in_specs=(
            P(None, "gx", "gy", "gz"),
            P(None, "gx", "gy", "gz"),
            P(),
            P(),
            P("gx", None),
            P("gy", None),
            P("gz", None),
        ),
        out_specs=P(None, "gx", "gy", "gz"),
        check_vma=False,
    )
```

```python
import jax
import jax.numpy as jnp
from jax import lax
from jax.experimental import pallas as pl
from jax.experimental.pallas import tpu as pltpu
from jax.sharding import PartitionSpec as P

TIME_STEP = 0.2
F32 = jnp.float32
HIGHEST = lax.Precision.HIGHEST
PLANES, ROWS = 24, 64
LOW, HIGH = 8, 16


def vmem():
    return pl.BlockSpec(memory_space=pltpu.VMEM)


def smem():
    return pl.BlockSpec(memory_space=pltpu.SMEM)


def f32(*shape):
    return jax.ShapeDtypeStruct(shape, F32)


def call(kernel, out_shape, in_specs, name, scratch=(), work=1000000, mib=8):
    many = isinstance(out_shape, (list, tuple))
    return pl.pallas_call(
        kernel,
        out_shape=out_shape,
        in_specs=in_specs,
        out_specs=[vmem() for _ in out_shape] if many else vmem(),
        scratch_shapes=list(scratch),
        compiler_params=pltpu.CompilerParams(vmem_limit_bytes=mib << 20),
        cost_estimate=pl.CostEstimate(flops=work, bytes_accessed=work, transcendentals=0),
        name=name,
    )


def lanes_of(rows):
    return lax.broadcasted_iota(jnp.int32, (rows, 128), 1)


def within(lane, first, size):
    return (lane >= first) & (lane < first + size)


def dot(a, b, a_dim, b_dim):
    return lax.dot_general(
        a, b, (((a_dim,), (b_dim,)), ((), ())), precision=HIGHEST, preferred_element_type=F32
    )


def padded(rows):
    return jnp.concatenate([rows, jnp.zeros((rows.shape[0], 128 - rows.shape[1]), F32)], axis=1)


def pack_xz(f, v, fz, x_up, x_down, z_up, z_down):
    lane = lanes_of(32)
    for j in range(6):
        for i in range(4):
            x_up[i * 6 + j] = f[i, 2 + j]
            x_down[i * 6 + j] = f[i, j]
    for j in range(4):
        for a in range(3):
            x_up[24 + a * 4 + j] = v[a, 4 + j]
            x_down[24 + a * 4 + j] = v[a, j]

    def plane_edges(x, carry):
        up = jnp.zeros((32, 128), F32)
        down = jnp.zeros((32, 128), F32)
        for i in range(4):
            plane = f[i, x]
            up = jnp.where(within(lane, 32 * i, 8), pltpu.roll(plane, (32 * i + 8) % 128, 1), up)
            down = jnp.where(within(lane, 32 * i + 24, 8), pltpu.roll(plane, 32 * i + 24, 1), down)
        for a in range(4):
            plane = pltpu.roll(v[a, x] if a < 3 else fz[...], 32 * a + 16, 1)
            up = jnp.where(within(lane, 32 * a + 8, 8), plane, up)
            down = jnp.where(within(lane, 32 * a + 16, 8), plane, down)
        z_up[x] = up
        z_down[x] = down
        return carry

    lax.fori_loop(0, 8, plane_edges, 0)


def pack_y(f, v, fy, z_left, z_right, y_up, y_down):
    for out, row, row4 in ((y_up, 24, 28), (y_down, 0, 0)):
        for x in range(8):
            half = slice(4 * (x % 2), 4 * (x % 2) + 4)
            for i in range(4):
                out[i * 8 + x] = f[i, x, row : row + 8]
            for a in range(3):
                out[32 + a * 4 + x // 2, half] = v[a, x, row4 : row4 + 4]
            out[44 + x // 2, half] = z_left[x, row4 : row4 + 4] + z_right[x, row4 : row4 + 4]
        out[48] = padded(fy[row : row + 8])


def pack_x2(z_left, z_right, y_low, y_high, fx, up, down):
    for out, near, far, first in ((up, 6, 4, 4), (down, 0, 2, 0)):
        for side, rows in ((0, y_low), (1, y_high)):
            four = slice(4, 8) if side == 0 else slice(0, 4)
            two = slice(6, 8) if side == 0 else slice(0, 2)
            for j in range(2):
                for i in range(4):
                    out[i * 2 + side, 4 * j : 4 * j + 4] = rows[i * 8 + near + j, four]
                    at = 4 * (i % 2) + 2 * j
                    out[8 + i // 2 * 2 + side, at : at + 2] = rows[i * 8 + far + j, two]
                x = near + j
                at = 4 * (x % 2) + (2 if side == 0 else 0)
                for a in range(3):
                    to = 4 * (a % 2) + 2 * j
                    out[12 + a // 2 * 2 + side, to : to + 2] = rows[32 + a * 4 + x // 2, at : at + 2]
                to = 4 * side + 2 * j
                out[32, to : to + 2] = rows[44 + x // 2, at : at + 2]
        for j in range(4):
            halo = z_left[first + j] + z_right[first + j]
            for t in range(4):
                out[16 + j * 4 + t] = halo[8 * t : 8 * t + 8]
        out[33] = padded(fx[...])


def advance(
    d, c, f, v, z_left, z_right, x_low, x_high, y_low, y_high, e_low, e_high, fz, fy,
    out, state, section, edge, edge2, wind, edge_wind, zm, final, faces, mixed, rhs, fye,
):
    gx, gy, gz = (lax.axis_index(n) for n in ("gx", "gy", "gz"))
    last_x, last_y, last_z = (lax.axis_size(n) - 1 for n in ("gx", "gy", "gz"))
    x_first, x_end = jnp.where(gx == 0, LOW, 0), jnp.where(gx == last_x, HIGH, PLANES)
    y_first, y_end = jnp.where(gy == 0, 16, 0), jnp.where(gy == last_y, 48, ROWS)
    scale = TIME_STEP / 12.0

    for i in range(4):
        for x in range(8):
            state[i, 8 + x, 16:48] = f[i, x]
            state[i, 8 + x, 8:16] = y_low[i * 8 + x]
            state[i, 8 + x, 48:56] = y_high[i * 8 + x]
        for j in range(6):
            state[i, 2 + j, 16:48] = x_low[i * 6 + j]
            state[i, 16 + j, 16:48] = x_high[i * 6 + j]
        for e, near, far in ((e_low, 6, 4), (e_high, 16, 18)):
            for j in range(2):
                state[i, near + j, 12:16] = e[i * 2, 4 * j : 4 * j + 4]
                state[i, near + j, 48:52] = e[i * 2 + 1, 4 * j : 4 * j + 4]
                at = 4 * (i % 2) + 2 * j
                state[i, far + j, 14:16] = e[8 + i // 2 * 2, at : at + 2]
                state[i, far + j, 48:50] = e[9 + i // 2 * 2, at : at + 2]
    for a in range(3):
        for x in range(8):
            half_tile = slice(4 * (x % 2), 4 * (x % 2) + 4)
            wind[a, 8 + x, 16:48] = v[a, x] * scale
            wind[a, 8 + x, 12:16] = y_low[32 + a * 4 + x // 2, half_tile] * scale
            wind[a, 8 + x, 48:52] = y_high[32 + a * 4 + x // 2, half_tile] * scale
        for j in range(4):
            wind[a, 4 + j, 16:48] = x_low[24 + a * 4 + j] * scale
            wind[a, 16 + j, 16:48] = x_high[24 + a * 4 + j] * scale
        for e, near in ((e_low, 6), (e_high, 16)):
            for j in range(2):
                at = 4 * (a % 2) + 2 * j
                wind[a, near + j, 14:16] = e[12 + a // 2 * 2, at : at + 2] * scale
                wind[a, near + j, 48:50] = e[13 + a // 2 * 2, at : at + 2] * scale
    for x in range(8):
        half_tile = slice(4 * (x % 2), 4 * (x % 2) + 4)
        zm[8 + x, 16:48] = z_left[x] + z_right[x]
        zm[8 + x, 12:16] = y_low[44 + x // 2, half_tile]
        zm[8 + x, 48:52] = y_high[44 + x // 2, half_tile]
    for e, near, first in ((e_low, 6, 4), (e_high, 16, 16)):
        for j in range(4):
            for t in range(4):
                zm[first + j, 16 + 8 * t : 24 + 8 * t] = e[16 + j * 4 + t]
        for j in range(2):
            zm[near + j, 14:16] = e[32, 2 * j : 2 * j + 2]
            zm[near + j, 48:50] = e[32, 4 + 2 * j : 6 + 2 * j]

    def chunk(rows):
        lane = lanes_of(rows)
        return lane, lane % 32, lax.broadcasted_iota(jnp.int32, (rows, 128), 0)

    def roll(value, by):
        return pltpu.roll(value, by % 128, 1)

    def slabs(x, r, rows, winds):
        lane, in_group, _ = chunk(rows)
        halo = zm[x, r : r + rows]
        tile = halo
        for i in range(4):
            q = state[i, x, r : r + rows]
            tile = jnp.where(within(lane, 32 * i + 8, 8), roll(q, 32 * i + 8), tile)
            tile = jnp.where(within(lane, 32 * i + 16, 8), roll(q, 32 * i + 24), tile)
        edge[x, r : r + rows] = tile
        if winds:
            halo = halo * scale
            packed = jnp.where(in_group < 8, roll(halo, -8), roll(halo, 8))
            for a in range(3):
                q = wind[a, x, r : r + rows]
                packed = jnp.where(within(lane, 32 * a + 8, 8), roll(q, 32 * a + 8), packed)
                packed = jnp.where(within(lane, 32 * a + 16, 8), roll(q, 32 * a + 24), packed)
            for a in range(3):
                one = jnp.where(within(lane, 32 * a, 32), packed, 0.0)
                one = one + roll(one, 32)
                edge_wind[a, x, r : r + rows] = one + roll(one, 64)

    full, own = (8, 24, 40), (16, 32)

    @pl.loop(6, 18)
    def _(x):
        for r in full:
            slabs(x, r, 16, True)

    @pl.loop(0, 4)
    def _(j):
        for r in own:
            slabs(jnp.where(j < 2, 4 + j, 16 + j), r, 16, False)

    dd = [d[i] * TIME_STEP for i in range(4)]
    cc = [[c[i, w] * TIME_STEP for w in range(4)] for i in range(4)]

    def terms(plus, minus, plus2, minus2):
        return 8.0 * (plus - minus) - (plus2 - minus2), plus + minus

    def tendencies(src, slab, x, r, rows):
        lane, in_group, _ = chunk(rows)
        at = slice(r, r + rows)
        u = [wind[a, x, at] for a in range(3)]
        q = [src[i, x, at] for i in range(4)]
        s = slab[x, at]
        s = jnp.where(in_group >= 24, s, roll(s, 16))
        results = []
        for i in range(4):
            ends = roll(s, -24 - 32 * i)
            gz_, lz = terms(
                roll(jnp.where(lane == 0, ends, q[i]), -1),
                roll(jnp.where(lane == 127, ends, q[i]), 1),
                roll(jnp.where(lane < 2, ends, q[i]), -2),
                roll(jnp.where(lane >= 126, ends, q[i]), 2),
            )
            gx_, lx = terms(src[i, x + 1, at], src[i, x - 1, at], src[i, x + 2, at], src[i, x - 2, at])
            gy_, ly = terms(*(src[i, x, r + o : r + o + rows] for o in (1, -1, 2, -2)))
            mix = cc[i][0] * q[0] + cc[i][1] * q[1] + (cc[i][2] * q[2] + cc[i][3] * q[3])
            moved = u[0] * gx_ + u[1] * gy_ + u[2] * gz_
            results.append(dd[i] * (lx + ly + lz) - moved + q[i] * (mix - 6.0 * dd[i]))
        return q, results

    def slab_tendency(slab, x, r, rows):
        lane, _, _ = chunk(rows)
        group = lane // 32
        at = slice(r, r + rows)

        def by_group(values):
            return jnp.where(group < 2, jnp.where(group == 0, values[0], values[1]),
                             jnp.where(group == 2, values[2], values[3]))

        q = slab[x, at]
        gz_, lz = terms(roll(q, -1), roll(q, 1), roll(q, -2), roll(q, 2))
        gx_, lx = terms(slab[x + 1, at], slab[x - 1, at], slab[x + 2, at], slab[x - 2, at])
        gy_, ly = terms(*(slab[x, r + o : r + o + rows] for o in (1, -1, 2, -2)))
        mix = -6.0 * by_group(dd)
        for k in range(4):
            mix = mix + by_group([cc[i][(i - k) % 4] for i in range(4)]) * roll(q, 32 * k)
        moved = edge_wind[0, x, at] * gx_ + edge_wind[1, x, at] * gy_ + edge_wind[2, x, at] * gz_
        return q, by_group(dd) * (lx + ly + lz) - moved + q * mix

    def inside(x, r, rows):
        _, in_group, row = chunk(rows)
        first = jnp.where((x >= x_first) & (x < x_end), y_first, ROWS)
        ok = (row + r >= first) & (row + r < y_end)
        z_ok = ((in_group >= 8) | (gz != 0)) & ((in_group < 24) | (gz != last_z))
        return ok, z_ok

    def half(base, q, t):
        return 0.5 * (base + q + t)

    def stage(x, rows_at, slab_rows, src, slab, dst, slab_dst, mean):
        for r in rows_at:
            at = slice(r, r + 16)
            ok, _ = inside(x, r, 16)
            q, t = tendencies(src, slab, x, r, 16)
            for i in range(4):
                new = half(dst[i, x, at], q[i], t[i]) if mean else q[i] + t[i]
                dst[i, x, at] = jnp.where(ok, new, 0.0)
        for r in slab_rows:
            at = slice(r, r + 16)
            ok, z_ok = inside(x, r, 16)
            q, t = slab_tendency(slab, x, r, 16)
            new = half(slab_dst[x, at], q, t) if mean else q + t
            slab_dst[x, at] = jnp.where(ok & z_ok, new, 0.0)

    @pl.loop(6, 18)
    def _(x):
        stage(x, full, full, state, edge, section, edge2, False)

    @pl.loop(0, 4)
    def _(j):
        stage(jnp.where(j < 2, 4 + j, 16 + j), own, (), state, edge, section, edge2, False)

    @pl.loop(8, 16)
    def _(x):
        stage(x, full, own, section, edge2, state, edge, True)

    @pl.loop(0, 4)
    def _(j):
        stage(jnp.where(j < 2, 6 + j, 14 + j), own, (), section, edge2, state, edge, True)

    @pl.loop(8, 16)
    def _(x):
        stage(x, own, (), state, edge, section, edge2, False)

    for i in range(4):
        for x in (6, 7, 16, 17):
            section[i, x, 16:48] = jnp.zeros((32, 128), F32)
        for x in range(8):
            section[i, 8 + x, 0:16] = jnp.zeros((16, 128), F32)
            section[i, 8 + x, 48:64] = jnp.zeros((16, 128), F32)

    @pl.loop(0, 8)
    def _(x):
        base = pl.multiple_of(x * 48, 16)
        for r in own:
            lane, _, _ = chunk(16)
            at = slice(r, r + 16)
            u = [wind[a, 8 + x, at] for a in range(3)]
            u_out = roll(zm[8 + x, at], 48) * (0.5 * scale)
            q = [section[i, 8 + x, at] for i in range(4)]
            for i in range(4):
                plus, minus, plus2, minus2 = (roll(q[i], o) for o in (-1, 1, -2, 2))
                src = section
                gz_, lz = terms(
                    jnp.where(lane == 127, 0.0, plus),
                    jnp.where(lane == 0, 0.0, minus),
                    jnp.where(lane >= 126, 0.0, plus2),
                    jnp.where(lane < 2, 0.0, minus2),
                )
                gx_, lx = terms(*(src[i, 8 + x + o, at] for o in (1, -1, 2, -2)))
                gy_, ly = terms(*(src[i, 8 + x, r + o : r + o + 16] for o in (1, -1, 2, -2)))
                mix = cc[i][0] * q[0] + cc[i][1] * q[1] + (cc[i][2] * q[2] + cc[i][3] * q[3])
                moved = u[0] * gx_ + u[1] * gy_ + u[2] * gz_
                t = dd[i] * (lx + ly + lz) - moved + q[i] * (mix - 6.0 * dd[i])
                row = pl.multiple_of(base + (r - 8), 8)
                final[i, pl.ds(row, 16), 0:128] = half(state[i, 8 + x, at], q[i], t)
                one = jnp.where(lane == 127, plus, jnp.where(lane == 0, -minus, 0.0))
                two = jnp.where(lane >= 126, plus2, jnp.where(lane < 2, -minus2, 0.0))
                spread = jnp.where(lane == 127, plus, jnp.where(lane == 0, minus, 0.0))
                beyond = (0.5 * dd[i]) * spread - u_out * (8.0 * one - two)
                final[i, pl.ds(row, 16), 128:256] = jnp.where((lane >= 126) | (lane < 2), beyond, 0.0)
        row8 = lax.broadcasted_iota(jnp.int32, (8, 128), 0)
        for r, to, kept in ((8, 0, row8 >= 6), (48, 40, row8 < 2)):
            u_y = wind[1, 8 + x, r : r + 8]
            for i in range(4):
                gy_, ly = terms(*(section[i, 8 + x, r + o : r + o + 8] for o in (1, -1, 2, -2)))
                row = pl.multiple_of(base + to, 8)
                face = jnp.where(kept, 0.5 * (dd[i] * ly - u_y * gy_), 0.0)
                final[i, pl.ds(row, 8), 0:128] = face
                final[i, pl.ds(row, 8), 128:256] = jnp.zeros((8, 128), F32)
    for i in range(4):
        first, second = section[i, 8, 16:48], section[i, 9, 16:48]
        last, before = section[i, 15, 16:48], section[i, 14, 16:48]
        u = [wind[0, x, 16:48] for x in (6, 7, 16, 17)]
        faces[i, 0:32] = 0.5 * (u[0] * first)
        faces[i, 32:64] = 0.5 * (dd[i] * first - u[1] * (8.0 * first - second))
        faces[i, 64:96] = 0.5 * (dd[i] * last + u[2] * (8.0 * last - before))
        faces[i, 96:128] = -0.5 * (u[3] * last)

    lane32 = lanes_of(32)
    outer = jnp.where((lane32 >= 126) | (lane32 < 2), roll(zm[8, 16:48], 16), 0.0)
    rhs[...] = jnp.zeros((4, 128, 256), F32)
    for i in range(4):
        for k in range(4):
            at = slice(32 * k + 8 * i, 32 * k + 8 * i + 8)
            rhs[i, at, 0:128] = fz[8 * k : 8 * k + 8]
            rhs[i, at, 128:256] = outer[8 * k : 8 * k + 8]
    fye[0:8] = y_low[48, :, 0:32]
    fye[8:40] = fy[...]
    fye[40:48] = y_high[48, :, 0:32]
    total = dot(final[0], rhs[0], 1, 1)
    total_faces = dot(faces[0], rhs[0, :, 0:128], 1, 1)
    for i in range(1, 4):
        total = total + dot(final[i], rhs[i], 1, 1)
        total_faces = total_faces + dot(faces[i], rhs[i, :, 0:128], 1, 1)
    for x in range(8):
        mixed[x * 32 : x * 32 + 32] = dot(fye[...], total[x * 48 : x * 48 + 48], 0, 0)
    for x in range(4):
        mixed[256 + x * 32 : 288 + x * 32] = dot(fy[...], total_faces[x * 32 : x * 32 + 32], 0, 0)
    lane = lanes_of(4)
    for j in range(8):
        for t in range(3):
            tiles = [mixed[pl.ds(128 * t + 4 * j + b, 4, stride=32), :] for b in range(4)]
            for k in range(4):
                tile = jnp.zeros((4, 128), F32)
                for b in range(4):
                    tile = jnp.where(within(lane, 32 * b, 32), roll(tiles[b], 32 * (b - k)), tile)
                out[j * 4 + k, :, 128 * t : 128 * t + 128] = tile


def contract_x(parts, fx, e_low, e_high, out):
    total = parts[0]
    for p in range(1, parts.shape[0]):
        total = total + parts[p]
    outer = jnp.concatenate([e_low[33, 6:8, 0:32], e_high[33, 0:2, 0:32]], axis=0)
    result = dot(fx[0:4], total[:, 0:128], 0, 0) + dot(fx[4:8], total[:, 128:256], 0, 0)
    out[...] = result + dot(outer, total[:, 256:384], 0, 0)


def local(fields, velocity, diffusivity, coupling, factor_x, factor_y, factor_z):
    def both_ways(axis, up, down):
        pairs = [(i, i + 1) for i in range(lax.axis_size(axis) - 1)]
        return (
            lax.ppermute(up, axis, pairs),
            lax.ppermute(down, axis, [(b, a) for a, b in pairs]),
        )

    x_up, x_down, z_up, z_down = call(
        pack_xz, [f32(36, 32, 128)] * 2 + [f32(8, 32, 128)] * 2, [vmem()] * 3, "pack_xz"
    )(fields, velocity, factor_z.T)
    x_low, x_high = both_ways("gx", x_up, x_down)
    z_left, z_right = both_ways("gz", z_up, z_down)
    y_up, y_down = call(pack_y, [f32(49, 8, 128)] * 2, [vmem()] * 5, "pack_y")(
        fields, velocity, factor_y, z_left, z_right
    )
    y_low, y_high = both_ways("gy", y_up, y_down)
    e_up, e_down = call(pack_x2, [f32(34, 8, 128)] * 2, [vmem()] * 5, "pack_x2")(
        z_left, z_right, y_low, y_high, factor_x
    )
    e_low, e_high = both_ways("gx", e_up, e_down)

    def tiles(*lead):
        return pltpu.VMEM((*lead, ROWS, 128), F32)

    gy, gz, gx = (lax.axis_size(n) for n in ("gy", "gz", "gx"))
    parts = call(
        advance,
        f32(32, 4, 384),
        [smem()] * 2 + [vmem()] * 12,
        "advance",
        scratch=[
            tiles(4, PLANES), tiles(4, PLANES), tiles(PLANES), tiles(PLANES),
            tiles(3, PLANES), tiles(3, PLANES), tiles(PLANES),
            pltpu.VMEM((4, 384, 256), F32), pltpu.VMEM((4, 128, 128), F32), pltpu.VMEM((384, 128), F32),
            pltpu.VMEM((4, 128, 256), F32), pltpu.VMEM((48, 32), F32),
        ],
        work=10000000,
        mib=24,
    )(
        diffusivity, coupling, fields, velocity, z_left, z_right, x_low, x_high, y_low, y_high,
        e_low, e_high, factor_z.T, factor_y,
    )
    parts = lax.all_to_all(parts, ("gy", "gz"), 0, 0, tiled=True)
    slices = call(contract_x, f32(32, 128), [vmem()] * 4, "contract_x")(
        parts, factor_x, e_low, e_high
    )
    slices = lax.all_to_all(slices, "gx", 0, 0, tiled=True)
    core = jnp.sum(slices.reshape(gx, 32 // gx, 4, 4, 8), axis=0)
    return core.transpose(2, 0, 1, 3)


def solution(mesh):
    return jax.shard_map(
        local,
        mesh=mesh,
        in_specs=(
            P(None, "gx", "gy", "gz"),
            P(None, "gx", "gy", "gz"),
            P(),
            P(),
            P("gx", None),
            P("gy", None),
            P("gz", None),
        ),
        out_specs=P(None, "gx", "gy", "gz"),
        check_vma=False,
    )
```

```python
import jax
import jax.numpy as jnp
from jax import lax
from jax.experimental import pallas as pl
from jax.experimental.pallas import tpu as pltpu
from jax.sharding import PartitionSpec as P

TIME_STEP = 0.2
F32 = jnp.float32
PLANES, ROWS = 24, 64
LOW, HIGH = 8, 16


def vmem():
    return pl.BlockSpec(memory_space=pltpu.VMEM)


def smem():
    return pl.BlockSpec(memory_space=pltpu.SMEM)


def f32(*shape):
    return jax.ShapeDtypeStruct(shape, F32)


def call(kernel, out_shape, in_specs, name, scratch=(), work=1000000, mib=8):
    many = isinstance(out_shape, (list, tuple))
    return pl.pallas_call(
        kernel,
        out_shape=out_shape,
        in_specs=in_specs,
        out_specs=[vmem() for _ in out_shape] if many else vmem(),
        scratch_shapes=list(scratch),
        compiler_params=pltpu.CompilerParams(vmem_limit_bytes=mib << 20),
        cost_estimate=pl.CostEstimate(flops=work, bytes_accessed=work, transcendentals=0),
        name=name,
    )


def lanes_of(rows):
    return lax.broadcasted_iota(jnp.int32, (rows, 128), 1)


def within(lane, first, size):
    return (lane >= first) & (lane < first + size)


def halves(a):
    high = a.astype(jnp.bfloat16)
    return high, (a - high.astype(F32)).astype(jnp.bfloat16)


def dot(a, b, a_dim, b_dim):
    def product(p, q):
        return lax.dot_general(p, q, (((a_dim,), (b_dim,)), ((), ())), preferred_element_type=F32)

    (a_high, a_low), (b_high, b_low) = halves(a), halves(b)
    return product(a_high, b_high) + (product(a_high, b_low) + product(a_low, b_high))


def padded(rows):
    return jnp.concatenate([rows, jnp.zeros((rows.shape[0], 128 - rows.shape[1]), F32)], axis=1)


def ways(axis):
    odd = lax.rem(lax.axis_index(axis), 2)
    return 1 - odd, odd


def pack_xz(f, v, fz, x_even, x_odd, z_even, z_odd):
    lane = lanes_of(32)
    for out, up in zip((x_even, x_odd), ways("gx")):
        for j in range(6):
            for i in range(4):
                out[i * 6 + j] = f[i, 2 * up + j]
        for j in range(4):
            for a in range(3):
                out[24 + a * 4 + j] = v[a, 4 * up + j]
    even_up, _ = ways("gz")

    def plane_edges(x, carry):
        up = jnp.zeros((32, 128), F32)
        down = jnp.zeros((32, 128), F32)
        for i in range(4):
            plane = f[i, x]
            up = jnp.where(within(lane, 32 * i, 8), pltpu.roll(plane, (32 * i + 8) % 128, 1), up)
            down = jnp.where(within(lane, 32 * i + 24, 8), pltpu.roll(plane, 32 * i + 24, 1), down)
        for a in range(4):
            plane = pltpu.roll(v[a, x] if a < 3 else fz[...], 32 * a + 16, 1)
            up = jnp.where(within(lane, 32 * a + 8, 8), plane, up)
            down = jnp.where(within(lane, 32 * a + 16, 8), plane, down)
        z_even[x] = jnp.where(even_up == 1, up, down)
        z_odd[x] = jnp.where(even_up == 1, down, up)
        return carry

    lax.fori_loop(0, 8, plane_edges, 0)


def pack_y(f, v, fy, z_even, z_odd, y_even, y_odd):
    for out, up in zip((y_even, y_odd), ways("gy")):

        def edge_rows(high, low):
            return jnp.where(up == 1, high, low)

        for x in range(8):
            half = slice(4 * (x % 2), 4 * (x % 2) + 4)
            for i in range(4):
                out[i * 8 + x] = edge_rows(f[i, x, 24:32], f[i, x, 0:8])
            for a in range(3):
                out[32 + a * 4 + x // 2, half] = edge_rows(v[a, x, 28:32], v[a, x, 0:4])
            out[44 + x // 2, half] = edge_rows(
                z_even[x, 28:32] + z_odd[x, 28:32], z_even[x, 0:4] + z_odd[x, 0:4]
            )
        out[48] = padded(edge_rows(fy[24:32], fy[0:8]))


def sides(axis, even, odd):
    low_is_odd = ways(axis)[0] == 1

    def low(*at):
        return jnp.where(low_is_odd, odd[at], even[at])

    def high(*at):
        return jnp.where(low_is_odd, even[at], odd[at])

    return low, high


def pack_x2(z_even, z_odd, y_even, y_odd, fx, even, odd):
    y_low, y_high = sides("gy", y_even, y_odd)
    for out, up in zip((even, odd), ways("gx")):
        near, far, first = 6 * up, 2 + 2 * up, 4 * up
        for side, rows in ((0, y_low), (1, y_high)):
            four = slice(4, 8) if side == 0 else slice(0, 4)
            two = slice(6, 8) if side == 0 else slice(0, 2)
            for j in range(2):
                for i in range(4):
                    out[i * 2 + side, 4 * j : 4 * j + 4] = rows(i * 8 + near + j, four)
                    at = 4 * (i % 2) + 2 * j
                    out[8 + i // 2 * 2 + side, at : at + 2] = rows(i * 8 + far + j, two)
                at = 4 * j + (2 if side == 0 else 0)
                for a in range(3):
                    to = 4 * (a % 2) + 2 * j
                    out[12 + a // 2 * 2 + side, to : to + 2] = rows(32 + a * 4 + 3 * up, slice(at, at + 2))
                to = 4 * side + 2 * j
                out[32, to : to + 2] = rows(44 + 3 * up, slice(at, at + 2))
        for j in range(4):
            halo = z_even[first + j] + z_odd[first + j]
            for t in range(4):
                out[16 + j * 4 + t] = halo[8 * t : 8 * t + 8]
        out[33] = padded(fx[...])


def advance(
    d, c, f, v, z_even, z_odd, x_even, x_odd, y_even, y_odd, e_even, e_odd, fz, fy,
    out, state, section, edge, edge2, wind, edge_wind, zm, final, faces, mixed, rhs, fye,
):
    gx, gy, gz = (lax.axis_index(n) for n in ("gx", "gy", "gz"))
    last_x, last_y, last_z = (lax.axis_size(n) - 1 for n in ("gx", "gy", "gz"))
    x_first, x_end = jnp.where(gx == 0, LOW, 0), jnp.where(gx == last_x, HIGH, PLANES)
    y_first, y_end = jnp.where(gy == 0, 16, 0), jnp.where(gy == last_y, 48, ROWS)
    scale = TIME_STEP / 12.0

    y_low, y_high = sides("gy", y_even, y_odd)
    even_up, odd_up = ways("gx")
    for i in range(4):
        for x in range(8):
            state[i, 8 + x, 16:48] = f[i, x]
            state[i, 8 + x, 8:16] = y_low(i * 8 + x)
            state[i, 8 + x, 48:56] = y_high(i * 8 + x)
        for halo, above in ((x_even, even_up), (x_odd, odd_up)):
            for j in range(6):
                state[i, 2 + 14 * above + j, 16:48] = halo[i * 6 + j]
        for e, above in ((e_even, even_up), (e_odd, odd_up)):
            near, far = 6 + 10 * above, 4 + 14 * above
            for j in range(2):
                state[i, near + j, 12:16] = e[i * 2, 4 * j : 4 * j + 4]
                state[i, near + j, 48:52] = e[i * 2 + 1, 4 * j : 4 * j + 4]
                at = 4 * (i % 2) + 2 * j
                state[i, far + j, 14:16] = e[8 + i // 2 * 2, at : at + 2]
                state[i, far + j, 48:50] = e[9 + i // 2 * 2, at : at + 2]
    for a in range(3):
        for x in range(8):
            half_tile = slice(4 * (x % 2), 4 * (x % 2) + 4)
            wind[a, 8 + x, 16:48] = v[a, x] * scale
            wind[a, 8 + x, 12:16] = y_low(32 + a * 4 + x // 2, half_tile) * scale
            wind[a, 8 + x, 48:52] = y_high(32 + a * 4 + x // 2, half_tile) * scale
        for halo, above in ((x_even, even_up), (x_odd, odd_up)):
            for j in range(4):
                wind[a, 4 + 12 * above + j, 16:48] = halo[24 + a * 4 + j] * scale
        for e, above in ((e_even, even_up), (e_odd, odd_up)):
            near = 6 + 10 * above
            for j in range(2):
                at = 4 * (a % 2) + 2 * j
                wind[a, near + j, 14:16] = e[12 + a // 2 * 2, at : at + 2] * scale
                wind[a, near + j, 48:50] = e[13 + a // 2 * 2, at : at + 2] * scale
    for x in range(8):
        half_tile = slice(4 * (x % 2), 4 * (x % 2) + 4)
        zm[8 + x, 16:48] = z_even[x] + z_odd[x]
        zm[8 + x, 12:16] = y_low(44 + x // 2, half_tile)
        zm[8 + x, 48:52] = y_high(44 + x // 2, half_tile)
    for e, above in ((e_even, even_up), (e_odd, odd_up)):
        near, first = 6 + 10 * above, 4 + 12 * above
        for j in range(4):
            for t in range(4):
                zm[first + j, 16 + 8 * t : 24 + 8 * t] = e[16 + j * 4 + t]
        for j in range(2):
            zm[near + j, 14:16] = e[32, 2 * j : 2 * j + 2]
            zm[near + j, 48:50] = e[32, 4 + 2 * j : 6 + 2 * j]

    def chunk(rows):
        lane = lanes_of(rows)
        return lane, lane % 32, lax.broadcasted_iota(jnp.int32, (rows, 128), 0)

    def roll(value, by):
        return pltpu.roll(value, by % 128, 1)

    def slabs(x, r, rows, winds):
        lane, in_group, _ = chunk(rows)
        halo = zm[x, r : r + rows]
        tile = halo
        for i in range(4):
            q = state[i, x, r : r + rows]
            tile = jnp.where(within(lane, 32 * i + 8, 8), roll(q, 32 * i + 8), tile)
            tile = jnp.where(within(lane, 32 * i + 16, 8), roll(q, 32 * i + 24), tile)
        edge[x, r : r + rows] = tile
        if winds:
            halo = halo * scale
            packed = jnp.where(in_group < 8, roll(halo, -8), roll(halo, 8))
            for a in range(3):
                q = wind[a, x, r : r + rows]
                packed = jnp.where(within(lane, 32 * a + 8, 8), roll(q, 32 * a + 8), packed)
                packed = jnp.where(within(lane, 32 * a + 16, 8), roll(q, 32 * a + 24), packed)
            for a in range(3):
                one = jnp.where(within(lane, 32 * a, 32), packed, 0.0)
                one = one + roll(one, 32)
                edge_wind[a, x, r : r + rows] = one + roll(one, 64)

    full, own = (8, 24, 40), (16, 32)

    @pl.loop(6, 18)
    def _(x):
        for r in full:
            slabs(x, r, 16, True)

    @pl.loop(0, 4)
    def _(j):
        for r in own:
            slabs(jnp.where(j < 2, 4 + j, 16 + j), r, 16, False)

    dd = [d[i] * TIME_STEP for i in range(4)]
    cc = [[c[i, w] * TIME_STEP for w in range(4)] for i in range(4)]

    def terms(plus, minus, plus2, minus2):
        return 8.0 * (plus - minus) - (plus2 - minus2), plus + minus

    def tendencies(src, slab, x, r, rows):
        lane, in_group, _ = chunk(rows)
        at = slice(r, r + rows)
        u = [wind[a, x, at] for a in range(3)]
        q = [src[i, x, at] for i in range(4)]
        s = slab[x, at]
        s = jnp.where(in_group >= 24, s, roll(s, 16))
        results = []
        for i in range(4):
            ends = roll(s, -24 - 32 * i)
            gz_, lz = terms(
                roll(jnp.where(lane == 0, ends, q[i]), -1),
                roll(jnp.where(lane == 127, ends, q[i]), 1),
                roll(jnp.where(lane < 2, ends, q[i]), -2),
                roll(jnp.where(lane >= 126, ends, q[i]), 2),
            )
            gx_, lx = terms(src[i, x + 1, at], src[i, x - 1, at], src[i, x + 2, at], src[i, x - 2, at])
            gy_, ly = terms(*(src[i, x, r + o : r + o + rows] for o in (1, -1, 2, -2)))
            mix = cc[i][0] * q[0] + cc[i][1] * q[1] + (cc[i][2] * q[2] + cc[i][3] * q[3])
            moved = u[0] * gx_ + u[1] * gy_ + u[2] * gz_
            results.append(dd[i] * (lx + ly + lz) - moved + q[i] * (mix - 6.0 * dd[i]))
        return q, results

    def slab_tendency(slab, x, r, rows):
        lane, _, _ = chunk(rows)
        group = lane // 32
        at = slice(r, r + rows)

        def by_group(values):
            return jnp.where(group < 2, jnp.where(group == 0, values[0], values[1]),
                             jnp.where(group == 2, values[2], values[3]))

        q = slab[x, at]
        gz_, lz = terms(roll(q, -1), roll(q, 1), roll(q, -2), roll(q, 2))
        gx_, lx = terms(slab[x + 1, at], slab[x - 1, at], slab[x + 2, at], slab[x - 2, at])
        gy_, ly = terms(*(slab[x, r + o : r + o + rows] for o in (1, -1, 2, -2)))
        mix = -6.0 * by_group(dd)
        for k in range(4):
            mix = mix + by_group([cc[i][(i - k) % 4] for i in range(4)]) * roll(q, 32 * k)
        moved = edge_wind[0, x, at] * gx_ + edge_wind[1, x, at] * gy_ + edge_wind[2, x, at] * gz_
        return q, by_group(dd) * (lx + ly + lz) - moved + q * mix

    def inside(x, r, rows):
        _, in_group, row = chunk(rows)
        first = jnp.where((x >= x_first) & (x < x_end), y_first, ROWS)
        ok = (row + r >= first) & (row + r < y_end)
        z_ok = ((in_group >= 8) | (gz != 0)) & ((in_group < 24) | (gz != last_z))
        return ok, z_ok

    def half(base, q, t):
        return 0.5 * (base + q + t)

    def stage(x, rows_at, slab_rows, src, slab, dst, slab_dst, mean):
        for r in rows_at:
            at = slice(r, r + 16)
            ok, _ = inside(x, r, 16)
            q, t = tendencies(src, slab, x, r, 16)
            for i in range(4):
                new = half(dst[i, x, at], q[i], t[i]) if mean else q[i] + t[i]
                dst[i, x, at] = jnp.where(ok, new, 0.0)
        for r in slab_rows:
            at = slice(r, r + 16)
            ok, z_ok = inside(x, r, 16)
            q, t = slab_tendency(slab, x, r, 16)
            new = half(slab_dst[x, at], q, t) if mean else q + t
            slab_dst[x, at] = jnp.where(ok & z_ok, new, 0.0)

    @pl.loop(6, 18)
    def _(x):
        stage(x, full, full, state, edge, section, edge2, False)

    @pl.loop(0, 4)
    def _(j):
        stage(jnp.where(j < 2, 4 + j, 16 + j), own, (), state, edge, section, edge2, False)

    @pl.loop(8, 16)
    def _(x):
        stage(x, full, own, section, edge2, state, edge, True)

    @pl.loop(0, 4)
    def _(j):
        stage(jnp.where(j < 2, 6 + j, 14 + j), own, (), section, edge2, state, edge, True)

    @pl.loop(8, 16)
    def _(x):
        stage(x, own, (), state, edge, section, edge2, False)

    for i in range(4):
        for x in (6, 7, 16, 17):
            section[i, x, 16:48] = jnp.zeros((32, 128), F32)
        for x in range(8):
            section[i, 8 + x, 0:16] = jnp.zeros((16, 128), F32)
            section[i, 8 + x, 48:64] = jnp.zeros((16, 128), F32)

    @pl.loop(0, 8)
    def _(x):
        base = pl.multiple_of(x * 48, 16)
        for r in own:
            lane, _, _ = chunk(16)
            at = slice(r, r + 16)
            u = [wind[a, 8 + x, at] for a in range(3)]
            u_out = roll(zm[8 + x, at], 48) * (0.5 * scale)
            q = [section[i, 8 + x, at] for i in range(4)]
            for i in range(4):
                plus, minus, plus2, minus2 = (roll(q[i], o) for o in (-1, 1, -2, 2))
                src = section
                gz_, lz = terms(
                    jnp.where(lane == 127, 0.0, plus),
                    jnp.where(lane == 0, 0.0, minus),
                    jnp.where(lane >= 126, 0.0, plus2),
                    jnp.where(lane < 2, 0.0, minus2),
                )
                gx_, lx = terms(*(src[i, 8 + x + o, at] for o in (1, -1, 2, -2)))
                gy_, ly = terms(*(src[i, 8 + x, r + o : r + o + 16] for o in (1, -1, 2, -2)))
                mix = cc[i][0] * q[0] + cc[i][1] * q[1] + (cc[i][2] * q[2] + cc[i][3] * q[3])
                moved = u[0] * gx_ + u[1] * gy_ + u[2] * gz_
                t = dd[i] * (lx + ly + lz) - moved + q[i] * (mix - 6.0 * dd[i])
                row = pl.multiple_of(base + (r - 8), 8)
                final[i, pl.ds(row, 16), 0:128] = half(state[i, 8 + x, at], q[i], t)
                one = jnp.where(lane == 127, plus, jnp.where(lane == 0, -minus, 0.0))
                two = jnp.where(lane >= 126, plus2, jnp.where(lane < 2, -minus2, 0.0))
                spread = jnp.where(lane == 127, plus, jnp.where(lane == 0, minus, 0.0))
                beyond = (0.5 * dd[i]) * spread - u_out * (8.0 * one - two)
                final[i, pl.ds(row, 16), 128:256] = jnp.where((lane >= 126) | (lane < 2), beyond, 0.0)
        row8 = lax.broadcasted_iota(jnp.int32, (8, 128), 0)
        for r, to, kept in ((8, 0, row8 >= 6), (48, 40, row8 < 2)):
            u_y = wind[1, 8 + x, r : r + 8]
            for i in range(4):
                gy_, ly = terms(*(section[i, 8 + x, r + o : r + o + 8] for o in (1, -1, 2, -2)))
                row = pl.multiple_of(base + to, 8)
                face = jnp.where(kept, 0.5 * (dd[i] * ly - u_y * gy_), 0.0)
                final[i, pl.ds(row, 8), 0:128] = face
                final[i, pl.ds(row, 8), 128:256] = jnp.zeros((8, 128), F32)
    for i in range(4):
        first, second = section[i, 8, 16:48], section[i, 9, 16:48]
        last, before = section[i, 15, 16:48], section[i, 14, 16:48]
        u = [wind[0, x, 16:48] for x in (6, 7, 16, 17)]
        faces[i, 0:32] = 0.5 * (u[0] * first)
        faces[i, 32:64] = 0.5 * (dd[i] * first - u[1] * (8.0 * first - second))
        faces[i, 64:96] = 0.5 * (dd[i] * last + u[2] * (8.0 * last - before))
        faces[i, 96:128] = -0.5 * (u[3] * last)

    lane32 = lanes_of(32)
    outer = jnp.where((lane32 >= 126) | (lane32 < 2), roll(zm[8, 16:48], 16), 0.0)
    rhs[...] = jnp.zeros((4, 128, 256), F32)
    for i in range(4):
        for k in range(4):
            at = slice(32 * k + 8 * i, 32 * k + 8 * i + 8)
            rhs[i, at, 0:128] = fz[8 * k : 8 * k + 8]
            rhs[i, at, 128:256] = outer[8 * k : 8 * k + 8]
    fye[0:8] = y_low(48, slice(0, 8), slice(0, 32))
    fye[8:40] = fy[...]
    fye[40:48] = y_high(48, slice(0, 8), slice(0, 32))
    total = dot(final[0], rhs[0], 1, 1)
    total_faces = dot(faces[0], rhs[0, :, 0:128], 1, 1)
    for i in range(1, 4):
        total = total + dot(final[i], rhs[i], 1, 1)
        total_faces = total_faces + dot(faces[i], rhs[i, :, 0:128], 1, 1)
    for x in range(8):
        mixed[x * 32 : x * 32 + 32] = dot(fye[...], total[x * 48 : x * 48 + 48], 0, 0)
    for x in range(4):
        mixed[256 + x * 32 : 288 + x * 32] = dot(fy[...], total_faces[x * 32 : x * 32 + 32], 0, 0)
    lane = lanes_of(4)
    for j in range(8):
        for t in range(3):
            tiles = [mixed[pl.ds(128 * t + 4 * j + b, 4, stride=32), :] for b in range(4)]
            for k in range(4):
                tile = jnp.zeros((4, 128), F32)
                for b in range(4):
                    tile = jnp.where(within(lane, 32 * b, 32), roll(tiles[b], 32 * (b - k)), tile)
                out[j * 4 + k, :, 128 * t : 128 * t + 128] = tile


def contract_x(parts, fx, e_even, e_odd, out):
    total = parts[0]
    for p in range(1, parts.shape[0]):
        total = total + parts[p]
    e_low, e_high = sides("gx", e_even, e_odd)
    outer = [e_low(33, slice(6, 8), slice(0, 32)), e_high(33, slice(0, 2), slice(0, 32))]
    outer = jnp.concatenate(outer, axis=0)
    result = dot(fx[0:4], total[:, 0:128], 0, 0) + dot(fx[4:8], total[:, 128:256], 0, 0)
    out[...] = result + dot(outer, total[:, 256:384], 0, 0)


def local(fields, velocity, diffusivity, coupling, factor_x, factor_y, factor_z):
    def swapped(axis, even, odd):
        last = lax.axis_size(axis) - 1
        pairs = [[(i, i + 1) for i in range(first, last, 2)] for first in (0, 1)]
        even_pairs, odd_pairs = ([*p, *((b, a) for a, b in p)] for p in pairs)
        return lax.ppermute(even, axis, even_pairs), lax.ppermute(odd, axis, odd_pairs)

    x_even, x_odd, z_even, z_odd = call(
        pack_xz, [f32(36, 32, 128)] * 2 + [f32(8, 32, 128)] * 2, [vmem()] * 3, "pack_xz"
    )(fields, velocity, factor_z.T)
    x_even, x_odd = swapped("gx", x_even, x_odd)
    z_even, z_odd = swapped("gz", z_even, z_odd)
    y_even, y_odd = call(pack_y, [f32(49, 8, 128)] * 2, [vmem()] * 5, "pack_y")(
        fields, velocity, factor_y, z_even, z_odd
    )
    y_even, y_odd = swapped("gy", y_even, y_odd)
    e_even, e_odd = call(pack_x2, [f32(34, 8, 128)] * 2, [vmem()] * 5, "pack_x2")(
        z_even, z_odd, y_even, y_odd, factor_x
    )
    e_even, e_odd = swapped("gx", e_even, e_odd)

    def tiles(*lead):
        return pltpu.VMEM((*lead, ROWS, 128), F32)

    gy, gz, gx = (lax.axis_size(n) for n in ("gy", "gz", "gx"))
    parts = call(
        advance,
        f32(32, 4, 384),
        [smem()] * 2 + [vmem()] * 12,
        "advance",
        scratch=[
            tiles(4, PLANES), tiles(4, PLANES), tiles(PLANES), tiles(PLANES),
            tiles(3, PLANES), tiles(3, PLANES), tiles(PLANES),
            pltpu.VMEM((4, 384, 256), F32), pltpu.VMEM((4, 128, 128), F32), pltpu.VMEM((384, 128), F32),
            pltpu.VMEM((4, 128, 256), F32), pltpu.VMEM((48, 32), F32),
        ],
        work=10000000,
        mib=24,
    )(
        diffusivity, coupling, fields, velocity, z_even, z_odd, x_even, x_odd, y_even, y_odd,
        e_even, e_odd, factor_z.T, factor_y,
    )
    parts = lax.all_to_all(parts, ("gy", "gz"), 0, 0, tiled=True)
    slices = call(contract_x, f32(32, 128), [vmem()] * 4, "contract_x")(
        parts, factor_x, e_even, e_odd
    )
    slices = lax.all_to_all(slices, "gx", 0, 0, tiled=True)
    core = jnp.sum(slices.reshape(gx, 32 // gx, 4, 4, 8), axis=0)
    return core.transpose(2, 0, 1, 3)


def solution(mesh):
    return jax.shard_map(
        local,
        mesh=mesh,
        in_specs=(
            P(None, "gx", "gy", "gz"),
            P(None, "gx", "gy", "gz"),
            P(),
            P(),
            P("gx", None),
            P("gy", None),
            P("gz", None),
        ),
        out_specs=P(None, "gx", "gy", "gz"),
        check_vma=False,
    )
```

```python
import jax
import jax.numpy as jnp
from jax import lax
from jax.experimental import pallas as pl
from jax.experimental.pallas import tpu as pltpu
from jax.sharding import PartitionSpec as P


TIME_STEP = 0.2
F32 = jnp.float32
PLANES, ROWS = 24, 64
LOW, HIGH = 8, 16


def vmem():
    return pl.BlockSpec(memory_space=pltpu.VMEM)


def smem():
    return pl.BlockSpec(memory_space=pltpu.SMEM)


def f32(*shape):
    return jax.ShapeDtypeStruct(shape, F32)


def call(kernel, out_shape, in_specs, scratch=(), work=1000000, mib=8):
    many = isinstance(out_shape, (list, tuple))
    return pl.pallas_call(
        kernel,
        out_shape=out_shape,
        in_specs=in_specs,
        out_specs=[vmem() for _ in out_shape] if many else vmem(),
        scratch_shapes=list(scratch),
        compiler_params=pltpu.CompilerParams(vmem_limit_bytes=mib << 20),
        cost_estimate=pl.CostEstimate(flops=work, bytes_accessed=work, transcendentals=0),
    )


def lanes_of(rows):
    return lax.broadcasted_iota(jnp.int32, (rows, 128), 1)


def within(lane, first, size):
    return (lane >= first) & (lane < first + size)


def halves(a):
    high = a.astype(jnp.bfloat16)
    return high, (a - high.astype(F32)).astype(jnp.bfloat16)


def dot(a, b, a_dim, b_dim):
    def product(p, q):
        return lax.dot_general(p, q, (((a_dim,), (b_dim,)), ((), ())), preferred_element_type=F32)

    (a_high, a_low), (b_high, b_low) = halves(a), halves(b)
    return product(a_high, b_high) + (product(a_high, b_low) + product(a_low, b_high))


def padded(rows):
    return jnp.concatenate([rows, jnp.zeros((rows.shape[0], 128 - rows.shape[1]), F32)], axis=1)


def ways(axis):
    odd = lax.rem(lax.axis_index(axis), 2)
    return 1 - odd, odd


def pack_xz(f_in, v_in, fz_in, x_even, x_odd, z_even, z_odd, f, v, fz, arrived):
    pairs = ((f_in, f), (v_in, v), (fz_in, fz))
    copies = [pltpu.make_async_copy(a, b, arrived.at[n]) for n, (a, b) in enumerate(pairs)]
    for copy in copies:
        copy.start()
    for copy in copies:
        copy.wait()
    lane = lanes_of(32)
    for out, up in zip((x_even, x_odd), ways("gx")):
        for j in range(6):
            for i in range(4):
                out[i * 6 + j] = f[i, 2 * up + j]
        for j in range(4):
            for a in range(3):
                out[24 + a * 4 + j] = v[a, 4 * up + j]
    even_up, _ = ways("gz")

    def plane_edges(x, carry):
        up = jnp.zeros((32, 128), F32)
        down = jnp.zeros((32, 128), F32)
        for i in range(4):
            plane = f[i, x]
            up = jnp.where(within(lane, 32 * i, 8), pltpu.roll(plane, (32 * i + 8) % 128, 1), up)
            down = jnp.where(within(lane, 32 * i + 24, 8), pltpu.roll(plane, 32 * i + 24, 1), down)
        for a in range(4):
            plane = pltpu.roll(v[a, x] if a < 3 else fz[...], 32 * a + 16, 1)
            up = jnp.where(within(lane, 32 * a + 8, 8), plane, up)
            down = jnp.where(within(lane, 32 * a + 16, 8), plane, down)
        z_even[x] = jnp.where(even_up == 1, up, down)
        z_odd[x] = jnp.where(even_up == 1, down, up)
        return carry

    lax.fori_loop(0, 8, plane_edges, 0)


def pack_y(f, v, fy, z_even, z_odd, y_even, y_odd):
    for out, up in zip((y_even, y_odd), ways("gy")):

        def edge_rows(high, low):
            return jnp.where(up == 1, high, low)

        for x in range(8):
            half = slice(4 * (x % 2), 4 * (x % 2) + 4)
            for i in range(4):
                out[i * 8 + x] = edge_rows(f[i, x, 24:32], f[i, x, 0:8])
            for a in range(3):
                out[32 + a * 4 + x // 2, half] = edge_rows(v[a, x, 28:32], v[a, x, 0:4])
            out[44 + x // 2, half] = edge_rows(
                z_even[x, 28:32] + z_odd[x, 28:32], z_even[x, 0:4] + z_odd[x, 0:4]
            )
        out[48] = padded(edge_rows(fy[24:32], fy[0:8]))


def sides(axis, even, odd):
    low_is_odd = ways(axis)[0] == 1

    def low(*at):
        return jnp.where(low_is_odd, odd[at], even[at])

    def high(*at):
        return jnp.where(low_is_odd, even[at], odd[at])

    return low, high


def pack_x2(z_even, z_odd, y_even, y_odd, fx, even, odd):
    y_low, y_high = sides("gy", y_even, y_odd)
    for out, up in zip((even, odd), ways("gx")):
        near, far, first = 6 * up, 2 + 2 * up, 4 * up
        for side, rows in ((0, y_low), (1, y_high)):
            four = slice(4, 8) if side == 0 else slice(0, 4)
            two = slice(6, 8) if side == 0 else slice(0, 2)
            for j in range(2):
                for i in range(4):
                    out[i * 2 + side, 4 * j : 4 * j + 4] = rows(i * 8 + near + j, four)
                    at = 4 * (i % 2) + 2 * j
                    out[8 + i // 2 * 2 + side, at : at + 2] = rows(i * 8 + far + j, two)
                at = 4 * j + (2 if side == 0 else 0)
                for a in range(3):
                    to = 4 * (a % 2) + 2 * j
                    out[12 + a // 2 * 2 + side, to : to + 2] = rows(32 + a * 4 + 3 * up, slice(at, at + 2))
                to = 4 * side + 2 * j
                out[32, to : to + 2] = rows(44 + 3 * up, slice(at, at + 2))
        for j in range(4):
            halo = z_even[first + j] + z_odd[first + j]
            for t in range(4):
                out[16 + j * 4 + t] = halo[8 * t : 8 * t + 8]
        out[33] = padded(fx[...])


def advance(
    d, c, f, v, z_even, z_odd, x_even, x_odd, y_even, y_odd, e_even, e_odd, fz, fy,
    out, state, section, edge, edge2, wind, edge_wind, zm, final, faces, mixed, rhs, fye,
):
    gx, gy, gz = (lax.axis_index(n) for n in ("gx", "gy", "gz"))
    last_x, last_y, last_z = (lax.axis_size(n) - 1 for n in ("gx", "gy", "gz"))
    x_first, x_end = jnp.where(gx == 0, LOW, 0), jnp.where(gx == last_x, HIGH, PLANES)
    y_first, y_end = jnp.where(gy == 0, 16, 0), jnp.where(gy == last_y, 48, ROWS)
    scale = TIME_STEP / 12.0

    y_low, y_high = sides("gy", y_even, y_odd)
    even_up, odd_up = ways("gx")
    for i in range(4):
        for x in range(8):
            state[i, 8 + x, 16:48] = f[i, x]
            state[i, 8 + x, 8:16] = y_low(i * 8 + x)
            state[i, 8 + x, 48:56] = y_high(i * 8 + x)
        for halo, above in ((x_even, even_up), (x_odd, odd_up)):
            for j in range(6):
                state[i, 2 + 14 * above + j, 16:48] = halo[i * 6 + j]
        for e, above in ((e_even, even_up), (e_odd, odd_up)):
            near, far = 6 + 10 * above, 4 + 14 * above
            for j in range(2):
                state[i, near + j, 12:16] = e[i * 2, 4 * j : 4 * j + 4]
                state[i, near + j, 48:52] = e[i * 2 + 1, 4 * j : 4 * j + 4]
                at = 4 * (i % 2) + 2 * j
                state[i, far + j, 14:16] = e[8 + i // 2 * 2, at : at + 2]
                state[i, far + j, 48:50] = e[9 + i // 2 * 2, at : at + 2]
    for a in range(3):
        for x in range(8):
            half_tile = slice(4 * (x % 2), 4 * (x % 2) + 4)
            wind[a, 8 + x, 16:48] = v[a, x] * scale
            wind[a, 8 + x, 12:16] = y_low(32 + a * 4 + x // 2, half_tile) * scale
            wind[a, 8 + x, 48:52] = y_high(32 + a * 4 + x // 2, half_tile) * scale
        for halo, above in ((x_even, even_up), (x_odd, odd_up)):
            for j in range(4):
                wind[a, 4 + 12 * above + j, 16:48] = halo[24 + a * 4 + j] * scale
        for e, above in ((e_even, even_up), (e_odd, odd_up)):
            near = 6 + 10 * above
            for j in range(2):
                at = 4 * (a % 2) + 2 * j
                wind[a, near + j, 14:16] = e[12 + a // 2 * 2, at : at + 2] * scale
                wind[a, near + j, 48:50] = e[13 + a // 2 * 2, at : at + 2] * scale
    for x in range(8):
        half_tile = slice(4 * (x % 2), 4 * (x % 2) + 4)
        zm[8 + x, 16:48] = z_even[x] + z_odd[x]
        zm[8 + x, 12:16] = y_low(44 + x // 2, half_tile)
        zm[8 + x, 48:52] = y_high(44 + x // 2, half_tile)
    for e, above in ((e_even, even_up), (e_odd, odd_up)):
        near, first = 6 + 10 * above, 4 + 12 * above
        for j in range(4):
            for t in range(4):
                zm[first + j, 16 + 8 * t : 24 + 8 * t] = e[16 + j * 4 + t]
        for j in range(2):
            zm[near + j, 14:16] = e[32, 2 * j : 2 * j + 2]
            zm[near + j, 48:50] = e[32, 4 + 2 * j : 6 + 2 * j]

    def chunk(rows):
        lane = lanes_of(rows)
        return lane, lane % 32, lax.broadcasted_iota(jnp.int32, (rows, 128), 0)

    def roll(value, by):
        return pltpu.roll(value, by % 128, 1)

    def slabs(x, r, rows, winds):
        lane, in_group, _ = chunk(rows)
        halo = zm[x, r : r + rows]
        tile = halo
        for i in range(4):
            q = state[i, x, r : r + rows]
            tile = jnp.where(within(lane, 32 * i + 8, 8), roll(q, 32 * i + 8), tile)
            tile = jnp.where(within(lane, 32 * i + 16, 8), roll(q, 32 * i + 24), tile)
        edge[x, r : r + rows] = tile
        if winds:
            halo = halo * scale
            packed = jnp.where(in_group < 8, roll(halo, -8), roll(halo, 8))
            for a in range(3):
                q = wind[a, x, r : r + rows]
                packed = jnp.where(within(lane, 32 * a + 8, 8), roll(q, 32 * a + 8), packed)
                packed = jnp.where(within(lane, 32 * a + 16, 8), roll(q, 32 * a + 24), packed)
            for a in range(3):
                one = jnp.where(within(lane, 32 * a, 32), packed, 0.0)
                one = one + roll(one, 32)
                edge_wind[a, x, r : r + rows] = one + roll(one, 64)

    full, own = (8, 24, 40), (16, 32)

    @pl.loop(6, 18)
    def _(x):
        for r in full:
            slabs(x, r, 16, True)

    @pl.loop(0, 4)
    def _(j):
        for r in own:
            slabs(jnp.where(j < 2, 4 + j, 16 + j), r, 16, False)

    dd = [d[i] * TIME_STEP for i in range(4)]
    cc = [[c[i, w] * TIME_STEP for w in range(4)] for i in range(4)]

    def terms(plus, minus, plus2, minus2):
        return 8.0 * (plus - minus) - (plus2 - minus2), plus + minus

    def tendencies(src, slab, x, r, rows):
        lane, in_group, _ = chunk(rows)
        at = slice(r, r + rows)
        u = [wind[a, x, at] for a in range(3)]
        q = [src[i, x, at] for i in range(4)]
        s = slab[x, at]
        s = jnp.where(in_group >= 24, s, roll(s, 16))
        results = []
        for i in range(4):
            ends = roll(s, -24 - 32 * i)
            gz_, lz = terms(
                roll(jnp.where(lane == 0, ends, q[i]), -1),
                roll(jnp.where(lane == 127, ends, q[i]), 1),
                roll(jnp.where(lane < 2, ends, q[i]), -2),
                roll(jnp.where(lane >= 126, ends, q[i]), 2),
            )
            gx_, lx = terms(src[i, x + 1, at], src[i, x - 1, at], src[i, x + 2, at], src[i, x - 2, at])
            gy_, ly = terms(*(src[i, x, r + o : r + o + rows] for o in (1, -1, 2, -2)))
            mix = cc[i][0] * q[0] + cc[i][1] * q[1] + (cc[i][2] * q[2] + cc[i][3] * q[3])
            moved = u[0] * gx_ + u[1] * gy_ + u[2] * gz_
            results.append(dd[i] * (lx + ly + lz) - moved + q[i] * (mix - 6.0 * dd[i]))
        return q, results

    def slab_tendency(slab, x, r, rows):
        lane, _, _ = chunk(rows)
        group = lane // 32
        at = slice(r, r + rows)

        def by_group(values):
            return jnp.where(group < 2, jnp.where(group == 0, values[0], values[1]),
                             jnp.where(group == 2, values[2], values[3]))

        q = slab[x, at]
        gz_, lz = terms(roll(q, -1), roll(q, 1), roll(q, -2), roll(q, 2))
        gx_, lx = terms(slab[x + 1, at], slab[x - 1, at], slab[x + 2, at], slab[x - 2, at])
        gy_, ly = terms(*(slab[x, r + o : r + o + rows] for o in (1, -1, 2, -2)))
        mix = -6.0 * by_group(dd)
        for k in range(4):
            mix = mix + by_group([cc[i][(i - k) % 4] for i in range(4)]) * roll(q, 32 * k)
        moved = edge_wind[0, x, at] * gx_ + edge_wind[1, x, at] * gy_ + edge_wind[2, x, at] * gz_
        return q, by_group(dd) * (lx + ly + lz) - moved + q * mix

    def inside(x, r, rows):
        _, in_group, row = chunk(rows)
        first = jnp.where((x >= x_first) & (x < x_end), y_first, ROWS)
        ok = (row + r >= first) & (row + r < y_end)
        z_ok = ((in_group >= 8) | (gz != 0)) & ((in_group < 24) | (gz != last_z))
        return ok, z_ok

    def half(base, q, t):
        return 0.5 * (base + q + t)

    def stage(x, rows_at, slab_rows, src, slab, dst, slab_dst, mean):
        for r in rows_at:
            at = slice(r, r + 16)
            ok, _ = inside(x, r, 16)
            q, t = tendencies(src, slab, x, r, 16)
            for i in range(4):
                new = half(dst[i, x, at], q[i], t[i]) if mean else q[i] + t[i]
                dst[i, x, at] = jnp.where(ok, new, 0.0)
        for r in slab_rows:
            at = slice(r, r + 16)
            ok, z_ok = inside(x, r, 16)
            q, t = slab_tendency(slab, x, r, 16)
            new = half(slab_dst[x, at], q, t) if mean else q + t
            slab_dst[x, at] = jnp.where(ok & z_ok, new, 0.0)

    @pl.loop(6, 18)
    def _(x):
        stage(x, full, full, state, edge, section, edge2, False)

    @pl.loop(0, 4)
    def _(j):
        stage(jnp.where(j < 2, 4 + j, 16 + j), own, (), state, edge, section, edge2, False)

    @pl.loop(8, 16)
    def _(x):
        stage(x, full, own, section, edge2, state, edge, True)

    @pl.loop(0, 4)
    def _(j):
        stage(jnp.where(j < 2, 6 + j, 14 + j), own, (), section, edge2, state, edge, True)

    @pl.loop(8, 16)
    def _(x):
        stage(x, own, (), state, edge, section, edge2, False)

    for i in range(4):
        for x in (6, 7, 16, 17):
            section[i, x, 16:48] = jnp.zeros((32, 128), F32)
        for x in range(8):
            section[i, 8 + x, 0:16] = jnp.zeros((16, 128), F32)
            section[i, 8 + x, 48:64] = jnp.zeros((16, 128), F32)

    @pl.loop(0, 8)
    def _(x):
        base = pl.multiple_of(x * 48, 16)
        for r in own:
            lane, _, _ = chunk(16)
            at = slice(r, r + 16)
            u = [wind[a, 8 + x, at] for a in range(3)]
            u_out = roll(zm[8 + x, at], 48) * (0.5 * scale)
            q = [section[i, 8 + x, at] for i in range(4)]
            for i in range(4):
                plus, minus, plus2, minus2 = (roll(q[i], o) for o in (-1, 1, -2, 2))
                src = section
                gz_, lz = terms(
                    jnp.where(lane == 127, 0.0, plus),
                    jnp.where(lane == 0, 0.0, minus),
                    jnp.where(lane >= 126, 0.0, plus2),
                    jnp.where(lane < 2, 0.0, minus2),
                )
                gx_, lx = terms(*(src[i, 8 + x + o, at] for o in (1, -1, 2, -2)))
                gy_, ly = terms(*(src[i, 8 + x, r + o : r + o + 16] for o in (1, -1, 2, -2)))
                mix = cc[i][0] * q[0] + cc[i][1] * q[1] + (cc[i][2] * q[2] + cc[i][3] * q[3])
                moved = u[0] * gx_ + u[1] * gy_ + u[2] * gz_
                t = dd[i] * (lx + ly + lz) - moved + q[i] * (mix - 6.0 * dd[i])
                row = pl.multiple_of(base + (r - 8), 8)
                final[i, pl.ds(row, 16), 0:128] = half(state[i, 8 + x, at], q[i], t)
                one = jnp.where(lane == 127, plus, jnp.where(lane == 0, -minus, 0.0))
                two = jnp.where(lane >= 126, plus2, jnp.where(lane < 2, -minus2, 0.0))
                spread = jnp.where(lane == 127, plus, jnp.where(lane == 0, minus, 0.0))
                beyond = (0.5 * dd[i]) * spread - u_out * (8.0 * one - two)
                final[i, pl.ds(row, 16), 128:256] = jnp.where((lane >= 126) | (lane < 2), beyond, 0.0)
        row8 = lax.broadcasted_iota(jnp.int32, (8, 128), 0)
        for r, to, kept in ((8, 0, row8 >= 6), (48, 40, row8 < 2)):
            u_y = wind[1, 8 + x, r : r + 8]
            for i in range(4):
                gy_, ly = terms(*(section[i, 8 + x, r + o : r + o + 8] for o in (1, -1, 2, -2)))
                row = pl.multiple_of(base + to, 8)
                face = jnp.where(kept, 0.5 * (dd[i] * ly - u_y * gy_), 0.0)
                final[i, pl.ds(row, 8), 0:128] = face
                final[i, pl.ds(row, 8), 128:256] = jnp.zeros((8, 128), F32)

    for i in range(4):
        first, second = section[i, 8, 16:48], section[i, 9, 16:48]
        last, before = section[i, 15, 16:48], section[i, 14, 16:48]
        u = [wind[0, x, 16:48] for x in (6, 7, 16, 17)]
        faces[i, 0:32] = 0.5 * (u[0] * first)
        faces[i, 32:64] = 0.5 * (dd[i] * first - u[1] * (8.0 * first - second))
        faces[i, 64:96] = 0.5 * (dd[i] * last + u[2] * (8.0 * last - before))
        faces[i, 96:128] = -0.5 * (u[3] * last)

    lane32 = lanes_of(32)
    outer = jnp.where((lane32 >= 126) | (lane32 < 2), roll(zm[8, 16:48], 16), 0.0)
    rhs[...] = jnp.zeros((4, 128, 256), F32)
    for i in range(4):
        for k in range(4):
            at = slice(32 * k + 8 * i, 32 * k + 8 * i + 8)
            rhs[i, at, 0:128] = fz[8 * k : 8 * k + 8]
            rhs[i, at, 128:256] = outer[8 * k : 8 * k + 8]
    fye[0:8] = y_low(48, slice(0, 8), slice(0, 32))
    fye[8:40] = fy[...]
    fye[40:48] = y_high(48, slice(0, 8), slice(0, 32))
    total = dot(final[0], rhs[0], 1, 1)
    total_faces = dot(faces[0], rhs[0, :, 0:128], 1, 1)
    for i in range(1, 4):
        total = total + dot(final[i], rhs[i], 1, 1)
        total_faces = total_faces + dot(faces[i], rhs[i, :, 0:128], 1, 1)
    for x in range(8):
        mixed[x * 32 : x * 32 + 32] = dot(fye[...], total[x * 48 : x * 48 + 48], 0, 0)
    for x in range(4):
        mixed[256 + x * 32 : 288 + x * 32] = dot(fy[...], total_faces[x * 32 : x * 32 + 32], 0, 0)
    lane = lanes_of(4)
    for j in range(8):
        for t in range(3):
            tiles = [mixed[pl.ds(128 * t + 4 * j + b, 4, stride=32), :] for b in range(4)]
            for k in range(4):
                tile = jnp.zeros((4, 128), F32)
                for b in range(4):
                    tile = jnp.where(within(lane, 32 * b, 32), roll(tiles[b], 32 * (b - k)), tile)
                out[j * 4 + k, :, 128 * t : 128 * t + 128] = tile


def contract_x(parts, fx, e_even, e_odd, out):
    total = parts[0]
    for p in range(1, parts.shape[0]):
        total = total + parts[p]
    e_low, e_high = sides("gx", e_even, e_odd)
    outer = [e_low(33, slice(6, 8), slice(0, 32)), e_high(33, slice(0, 2), slice(0, 32))]
    outer = jnp.concatenate(outer, axis=0)
    result = dot(fx[0:4], total[:, 0:128], 0, 0) + dot(fx[4:8], total[:, 128:256], 0, 0)
    out[...] = result + dot(outer, total[:, 256:384], 0, 0)


def local(fields, velocity, diffusivity, coupling, factor_x, factor_y, factor_z):
    def swapped(axis, even, odd):
        last = lax.axis_size(axis) - 1
        pairs = [[(i, i + 1) for i in range(first, last, 2)] for first in (0, 1)]
        even_pairs, odd_pairs = ([*p, *((b, a) for a, b in p)] for p in pairs)
        even = lax.ppermute(even, axis, even_pairs)
        return even, lax.ppermute(odd, axis, odd_pairs)

    x_even, x_odd, z_even, z_odd, fields, velocity, fz = call(
        pack_xz,
        [f32(36, 32, 128)] * 2 + [f32(8, 32, 128)] * 2
        + [f32(4, 8, 32, 128), f32(3, 8, 32, 128), f32(32, 128)],
        [pl.BlockSpec(memory_space=pltpu.HBM)] * 3,
        scratch=[pltpu.SemaphoreType.DMA((3,))],
    )(*(pltpu.with_memory_space_constraint(a, pltpu.HBM) for a in (fields, velocity, factor_z.T)))
    z_even, z_odd = swapped("gz", z_even, z_odd)
    y_even, y_odd = call(pack_y, [f32(49, 8, 128)] * 2, [vmem()] * 5)(
        fields, velocity, factor_y, z_even, z_odd
    )
    y_even, y_odd = swapped("gy", y_even, y_odd)
    x_even, x_odd = swapped("gx", x_even, x_odd)
    e_even, e_odd = call(pack_x2, [f32(34, 8, 128)] * 2, [vmem()] * 5)(
        z_even, z_odd, y_even, y_odd, factor_x
    )
    e_even, e_odd = swapped("gx", e_even, e_odd)

    def tiles(*lead):
        return pltpu.VMEM((*lead, ROWS, 128), F32)

    _, _, gx = (lax.axis_size(n) for n in ("gy", "gz", "gx"))
    parts = call(
        advance,
        f32(32, 4, 384),
        [smem()] * 2 + [vmem()] * 12,
        scratch=[
            tiles(4, PLANES), tiles(4, PLANES), tiles(PLANES), tiles(PLANES),
            tiles(3, PLANES), tiles(3, PLANES), tiles(PLANES),
            pltpu.VMEM((4, 384, 256), F32), pltpu.VMEM((4, 128, 128), F32), pltpu.VMEM((384, 128), F32),
            pltpu.VMEM((4, 128, 256), F32), pltpu.VMEM((48, 32), F32),
        ],
        work=10000000,
        mib=24,
    )(
        diffusivity, coupling, fields, velocity, z_even, z_odd, x_even, x_odd, y_even, y_odd,
        e_even, e_odd, fz, factor_y,
    )
    parts = lax.all_to_all(parts, ("gy", "gz"), 0, 0, tiled=True)
    slices = call(contract_x, f32(32, 128), [vmem()] * 4)(parts, factor_x, e_even, e_odd)
    slices = lax.all_to_all(slices, "gx", 0, 0, tiled=True)
    core = jnp.sum(slices.reshape(gx, 32 // gx, 4, 4, 8), axis=0)
    return core.transpose(2, 0, 1, 3)


def solution(mesh):
    return jax.shard_map(
        local,
        mesh=mesh,
        in_specs=(
            P(None, "gx", "gy", "gz"),
            P(None, "gx", "gy", "gz"),
            P(),
            P(),
            P("gx", None),
            P("gy", None),
            P("gz", None),
        ),
        out_specs=P(None, "gx", "gy", "gz"),
        check_vma=False,
    )
```

```python
import jax
import jax.numpy as jnp
from jax import lax
from jax.experimental import pallas as pl
from jax.experimental.pallas import tpu as pltpu
from jax.sharding import PartitionSpec as P


TIME_STEP = 0.2
F32 = jnp.float32
PLANES, ROWS = 24, 64
LOW, HIGH = 8, 16


def vmem():
    return pl.BlockSpec(memory_space=pltpu.VMEM)


def smem():
    return pl.BlockSpec(memory_space=pltpu.SMEM)


def f32(*shape):
    return jax.ShapeDtypeStruct(shape, F32)


def call(kernel, out_shape, in_specs, scratch=(), work=1000000, mib=8, aliases=None):
    many = isinstance(out_shape, (list, tuple))
    return pl.pallas_call(
        kernel,
        out_shape=out_shape,
        in_specs=in_specs,
        out_specs=[vmem() for _ in out_shape] if many else vmem(),
        scratch_shapes=list(scratch),
        input_output_aliases=aliases or {},
        compiler_params=pltpu.CompilerParams(vmem_limit_bytes=mib << 20),
        cost_estimate=pl.CostEstimate(flops=work, bytes_accessed=work, transcendentals=0),
    )


def lanes_of(rows):
    return lax.broadcasted_iota(jnp.int32, (rows, 128), 1)


def within(lane, first, size):
    return (lane >= first) & (lane < first + size)


def halves(a):
    high = a.astype(jnp.bfloat16)
    return high, (a - high.astype(F32)).astype(jnp.bfloat16)


def dot(a, b, a_dim, b_dim):
    def product(p, q):
        return lax.dot_general(p, q, (((a_dim,), (b_dim,)), ((), ())), preferred_element_type=F32)

    (a_high, a_low), (b_high, b_low) = halves(a), halves(b)
    return product(a_high, b_high) + (product(a_high, b_low) + product(a_low, b_high))


def padded(rows):
    return jnp.concatenate([rows, jnp.zeros((rows.shape[0], 128 - rows.shape[1]), F32)], axis=1)


def ways(axis):
    odd = lax.rem(lax.axis_index(axis), 2)
    return 1 - odd, odd


def pack_xz(f_in, v_in, fz_in, x_even, x_odd, z_even, z_odd, f, v, fz, arrived):
    pairs = ((f_in, f), (v_in, v), (fz_in, fz))
    copies = [pltpu.make_async_copy(a, b, arrived.at[n]) for n, (a, b) in enumerate(pairs)]
    for copy in copies:
        copy.start()
    for copy in copies:
        copy.wait()
    lane = lanes_of(32)
    for out, up in zip((x_even, x_odd), ways("gx")):
        for j in range(6):
            for i in range(4):
                out[i * 6 + j] = f[i, 2 * up + j]
        for j in range(4):
            for a in range(3):
                out[24 + a * 4 + j] = v[a, 4 * up + j]
    even_up, _ = ways("gz")

    def plane_edges(x, carry):
        up = jnp.zeros((32, 128), F32)
        down = jnp.zeros((32, 128), F32)
        for i in range(4):
            plane = f[i, x]
            up = jnp.where(within(lane, 32 * i, 8), pltpu.roll(plane, (32 * i + 8) % 128, 1), up)
            down = jnp.where(within(lane, 32 * i + 24, 8), pltpu.roll(plane, 32 * i + 24, 1), down)
        for a in range(4):
            plane = pltpu.roll(v[a, x] if a < 3 else fz[...], 32 * a + 16, 1)
            up = jnp.where(within(lane, 32 * a + 8, 8), plane, up)
            down = jnp.where(within(lane, 32 * a + 16, 8), plane, down)
        z_even[x] = jnp.where(even_up == 1, up, down)
        z_odd[x] = jnp.where(even_up == 1, down, up)
        return carry

    lax.fori_loop(0, 8, plane_edges, 0)


def pack_y(f, v, fy, z_even, z_odd, y_even, y_odd):
    for out, up in zip((y_even, y_odd), ways("gy")):

        def edge_rows(high, low):
            return jnp.where(up == 1, high, low)

        for x in range(8):
            half = slice(4 * (x % 2), 4 * (x % 2) + 4)
            for i in range(4):
                out[i * 8 + x] = edge_rows(f[i, x, 24:32], f[i, x, 0:8])
            for a in range(3):
                out[32 + a * 4 + x // 2, half] = edge_rows(v[a, x, 28:32], v[a, x, 0:4])
            out[44 + x // 2, half] = edge_rows(
                z_even[x, 28:32] + z_odd[x, 28:32], z_even[x, 0:4] + z_odd[x, 0:4]
            )
        out[48] = padded(edge_rows(fy[24:32], fy[0:8]))


def sides(axis, even, odd):
    low_is_odd = ways(axis)[0] == 1

    def low(*at):
        return jnp.where(low_is_odd, odd[at], even[at])

    def high(*at):
        return jnp.where(low_is_odd, even[at], odd[at])

    return low, high


def pack_x2(z_even, z_odd, y_even, y_odd, fx, even, odd):
    y_low, y_high = sides("gy", y_even, y_odd)
    for out, up in zip((even, odd), ways("gx")):
        near, far, first = 6 * up, 2 + 2 * up, 4 * up
        for side, rows in ((0, y_low), (1, y_high)):
            four = slice(4, 8) if side == 0 else slice(0, 4)
            two = slice(6, 8) if side == 0 else slice(0, 2)
            for j in range(2):
                for i in range(4):
                    out[i * 2 + side, 4 * j : 4 * j + 4] = rows(i * 8 + near + j, four)
                    at = 4 * (i % 2) + 2 * j
                    out[8 + i // 2 * 2 + side, at : at + 2] = rows(i * 8 + far + j, two)
                at = 4 * j + (2 if side == 0 else 0)
                for a in range(3):
                    to = 4 * (a % 2) + 2 * j
                    out[12 + a // 2 * 2 + side, to : to + 2] = rows(32 + a * 4 + 3 * up, slice(at, at + 2))
                to = 4 * side + 2 * j
                out[32, to : to + 2] = rows(44 + 3 * up, slice(at, at + 2))
        for j in range(4):
            halo = z_even[first + j] + z_odd[first + j]
            for t in range(4):
                out[16 + j * 4 + t] = halo[8 * t : 8 * t + 8]
        out[33] = padded(fx[...])


FULL, OWN = (8, 24, 40), (16, 32)
SCALE = TIME_STEP / 12.0


def chunk(rows):
    lane = lanes_of(rows)
    return lane, lane % 32, lax.broadcasted_iota(jnp.int32, (rows, 128), 0)


def roll(value, by):
    return pltpu.roll(value, by % 128, 1)


def slabs(state, wind, zm, edge, edge_wind, x, r, rows, winds):
    lane, in_group, _ = chunk(rows)
    halo = zm[x, r : r + rows]
    tile = halo
    for i in range(4):
        q = state[i, x, r : r + rows]
        tile = jnp.where(within(lane, 32 * i + 8, 8), roll(q, 32 * i + 8), tile)
        tile = jnp.where(within(lane, 32 * i + 16, 8), roll(q, 32 * i + 24), tile)
    edge[x, r : r + rows] = tile
    if winds:
        halo = halo * SCALE
        packed = jnp.where(in_group < 8, roll(halo, -8), roll(halo, 8))
        for a in range(3):
            q = wind[a, x, r : r + rows]
            packed = jnp.where(within(lane, 32 * a + 8, 8), roll(q, 32 * a + 8), packed)
            packed = jnp.where(within(lane, 32 * a + 16, 8), roll(q, 32 * a + 24), packed)
        for a in range(3):
            one = jnp.where(within(lane, 32 * a, 32), packed, 0.0)
            one = one + roll(one, 32)
            edge_wind[a, x, r : r + rows] = one + roll(one, 64)


def terms(plus, minus, plus2, minus2):
    return 8.0 * (plus - minus) - (plus2 - minus2), plus + minus


def half(base, q, t):
    return 0.5 * (base + q + t)


class Stencil:
    def __init__(self, d, c, wind, edge_wind):
        self.wind, self.edge_wind = wind, edge_wind
        self.dd = [d[i] * TIME_STEP for i in range(4)]
        self.cc = [[c[i, w] * TIME_STEP for w in range(4)] for i in range(4)]
        gx, gy, self.gz = (lax.axis_index(n) for n in ("gx", "gy", "gz"))
        last_x, last_y, self.last_z = (lax.axis_size(n) - 1 for n in ("gx", "gy", "gz"))
        self.x_first, self.x_end = jnp.where(gx == 0, LOW, 0), jnp.where(gx == last_x, HIGH, PLANES)
        self.y_first, self.y_end = jnp.where(gy == 0, 16, 0), jnp.where(gy == last_y, 48, ROWS)

    def tendencies(self, src, slab, x, r, rows):
        dd, cc, wind = self.dd, self.cc, self.wind
        lane, in_group, _ = chunk(rows)
        at = slice(r, r + rows)
        u = [wind[a, x, at] for a in range(3)]
        q = [src[i, x, at] for i in range(4)]
        s = slab[x, at]
        s = jnp.where(in_group >= 24, s, roll(s, 16))
        results = []
        for i in range(4):
            ends = roll(s, -24 - 32 * i)
            gz_, lz = terms(
                roll(jnp.where(lane == 0, ends, q[i]), -1),
                roll(jnp.where(lane == 127, ends, q[i]), 1),
                roll(jnp.where(lane < 2, ends, q[i]), -2),
                roll(jnp.where(lane >= 126, ends, q[i]), 2),
            )
            gx_, lx = terms(src[i, x + 1, at], src[i, x - 1, at], src[i, x + 2, at], src[i, x - 2, at])
            gy_, ly = terms(*(src[i, x, r + o : r + o + rows] for o in (1, -1, 2, -2)))
            mix = cc[i][0] * q[0] + cc[i][1] * q[1] + (cc[i][2] * q[2] + cc[i][3] * q[3])
            moved = u[0] * gx_ + u[1] * gy_ + u[2] * gz_
            results.append(dd[i] * (lx + ly + lz) - moved + q[i] * (mix - 6.0 * dd[i]))
        return q, results

    def slab_tendency(self, slab, x, r, rows):
        dd, cc, edge_wind = self.dd, self.cc, self.edge_wind
        lane, _, _ = chunk(rows)
        group = lane // 32
        at = slice(r, r + rows)

        def by_group(values):
            return jnp.where(group < 2, jnp.where(group == 0, values[0], values[1]),
                             jnp.where(group == 2, values[2], values[3]))

        q = slab[x, at]
        gz_, lz = terms(roll(q, -1), roll(q, 1), roll(q, -2), roll(q, 2))
        gx_, lx = terms(slab[x + 1, at], slab[x - 1, at], slab[x + 2, at], slab[x - 2, at])
        gy_, ly = terms(*(slab[x, r + o : r + o + rows] for o in (1, -1, 2, -2)))
        mix = -6.0 * by_group(dd)
        for k in range(4):
            mix = mix + by_group([cc[i][(i - k) % 4] for i in range(4)]) * roll(q, 32 * k)
        moved = edge_wind[0, x, at] * gx_ + edge_wind[1, x, at] * gy_ + edge_wind[2, x, at] * gz_
        return q, by_group(dd) * (lx + ly + lz) - moved + q * mix

    def inside(self, x, r, rows):
        _, in_group, row = chunk(rows)
        first = jnp.where((x >= self.x_first) & (x < self.x_end), self.y_first, ROWS)
        ok = (row + r >= first) & (row + r < self.y_end)
        z_ok = ((in_group >= 8) | (self.gz != 0)) & ((in_group < 24) | (self.gz != self.last_z))
        return ok, z_ok

    def stage(self, x, rows_at, slab_rows, src, slab, dst, slab_dst, mean):
        for r in rows_at:
            at = slice(r, r + 16)
            ok, _ = self.inside(x, r, 16)
            q, t = self.tendencies(src, slab, x, r, 16)
            for i in range(4):
                new = half(dst[i, x, at], q[i], t[i]) if mean else q[i] + t[i]
                dst[i, x, at] = jnp.where(ok, new, 0.0)
        for r in slab_rows:
            at = slice(r, r + 16)
            ok, z_ok = self.inside(x, r, 16)
            q, t = self.slab_tendency(slab, x, r, 16)
            new = half(slab_dst[x, at], q, t) if mean else q + t
            slab_dst[x, at] = jnp.where(ok & z_ok, new, 0.0)


def prepare(
    d, c, f, v, z_even, z_odd, y_even, y_odd, fz, fy,
    state, section, edge, edge2, wind, edge_wind, zm, rhs, fye,
):
    y_low, y_high = sides("gy", y_even, y_odd)
    for i in range(4):
        for x in range(8):
            state[i, 8 + x, 16:48] = f[i, x]
            state[i, 8 + x, 8:16] = y_low(i * 8 + x)
            state[i, 8 + x, 48:56] = y_high(i * 8 + x)
    for x in range(8):
        half_tile = slice(4 * (x % 2), 4 * (x % 2) + 4)
        for a in range(3):
            wind[a, 8 + x, 16:48] = v[a, x] * SCALE
            wind[a, 8 + x, 12:16] = y_low(32 + a * 4 + x // 2, half_tile) * SCALE
            wind[a, 8 + x, 48:52] = y_high(32 + a * 4 + x // 2, half_tile) * SCALE
        zm[8 + x, 16:48] = z_even[x] + z_odd[x]
        zm[8 + x, 12:16] = y_low(44 + x // 2, half_tile)
        zm[8 + x, 48:52] = y_high(44 + x // 2, half_tile)
    lane = lanes_of(32)
    outer = jnp.where((lane >= 126) | (lane < 2), roll(zm[8, 16:48], 16), 0.0)
    rhs[...] = jnp.zeros((4, 128, 256), F32)
    for i in range(4):
        for k in range(4):
            at = slice(32 * k + 8 * i, 32 * k + 8 * i + 8)
            rhs[i, at, 0:128] = fz[8 * k : 8 * k + 8]
            rhs[i, at, 128:256] = outer[8 * k : 8 * k + 8]
    fye[0:8] = y_low(48, slice(0, 8), slice(0, 32))
    fye[8:40] = fy[...]
    fye[40:48] = y_high(48, slice(0, 8), slice(0, 32))

    @pl.loop(8, 16)
    def _(x):
        for r in FULL:
            slabs(state, wind, zm, edge, edge_wind, x, r, 16, True)

    stencil = Stencil(d, c, wind, edge_wind)

    @pl.loop(10, 14)
    def _(x):
        stencil.stage(x, FULL, FULL, state, edge, section, edge2, False)


def advance(
    d, c, x_even, x_odd, e_even, e_odd, fy, rhs, fye, *refs
):
    out, state, section, edge, edge2, wind, edge_wind, zm, final, faces, mixed = refs[7:]
    stencil = Stencil(d, c, wind, edge_wind)
    dd, cc, stage, scale = stencil.dd, stencil.cc, stencil.stage, SCALE
    full, own = FULL, OWN
    even_up, odd_up = ways("gx")
    for halo, above in ((x_even, even_up), (x_odd, odd_up)):
        for j in range(6):
            for i in range(4):
                state[i, 2 + 14 * above + j, 16:48] = halo[i * 6 + j]
        for j in range(4):
            for a in range(3):
                wind[a, 4 + 12 * above + j, 16:48] = halo[24 + a * 4 + j] * scale
    for e, above in ((e_even, even_up), (e_odd, odd_up)):
        near, far, first = 6 + 10 * above, 4 + 14 * above, 4 + 12 * above
        for j in range(2):
            for i in range(4):
                state[i, near + j, 12:16] = e[i * 2, 4 * j : 4 * j + 4]
                state[i, near + j, 48:52] = e[i * 2 + 1, 4 * j : 4 * j + 4]
                at = 4 * (i % 2) + 2 * j
                state[i, far + j, 14:16] = e[8 + i // 2 * 2, at : at + 2]
                state[i, far + j, 48:50] = e[9 + i // 2 * 2, at : at + 2]
            for a in range(3):
                at = 4 * (a % 2) + 2 * j
                wind[a, near + j, 14:16] = e[12 + a // 2 * 2, at : at + 2] * scale
                wind[a, near + j, 48:50] = e[13 + a // 2 * 2, at : at + 2] * scale
            zm[near + j, 14:16] = e[32, 2 * j : 2 * j + 2]
            zm[near + j, 48:50] = e[32, 4 + 2 * j : 6 + 2 * j]
        for j in range(4):
            for t in range(4):
                zm[first + j, 16 + 8 * t : 24 + 8 * t] = e[16 + j * 4 + t]

    @pl.loop(0, 4)
    def _(j):
        x = jnp.where(j < 2, 6 + j, 14 + j)
        for r in full:
            slabs(state, wind, zm, edge, edge_wind, x, r, 16, True)
        x = jnp.where(j < 2, 4 + j, 16 + j)
        for r in own:
            slabs(state, wind, zm, edge, edge_wind, x, r, 16, False)

    @pl.loop(0, 8)
    def _(j):
        x = jnp.where(j < 4, 6 + j, 10 + j)
        stage(x, full, full, state, edge, section, edge2, False)

    @pl.loop(0, 4)
    def _(j):
        stage(jnp.where(j < 2, 4 + j, 16 + j), own, (), state, edge, section, edge2, False)

    @pl.loop(8, 16)
    def _(x):
        stage(x, full, own, section, edge2, state, edge, True)

    @pl.loop(0, 4)
    def _(j):
        stage(jnp.where(j < 2, 6 + j, 14 + j), own, (), section, edge2, state, edge, True)

    @pl.loop(8, 16)
    def _(x):
        stage(x, own, (), state, edge, section, edge2, False)

    for i in range(4):
        for x in (6, 7, 16, 17):
            section[i, x, 16:48] = jnp.zeros((32, 128), F32)
        for x in range(8):
            section[i, 8 + x, 0:16] = jnp.zeros((16, 128), F32)
            section[i, 8 + x, 48:64] = jnp.zeros((16, 128), F32)

    @pl.loop(0, 8)
    def _(x):
        base = pl.multiple_of(x * 48, 16)
        for r in own:
            lane, _, _ = chunk(16)
            at = slice(r, r + 16)
            u = [wind[a, 8 + x, at] for a in range(3)]
            u_out = roll(zm[8 + x, at], 48) * (0.5 * scale)
            q = [section[i, 8 + x, at] for i in range(4)]
            for i in range(4):
                plus, minus, plus2, minus2 = (roll(q[i], o) for o in (-1, 1, -2, 2))
                src = section
                gz_, lz = terms(
                    jnp.where(lane == 127, 0.0, plus),
                    jnp.where(lane == 0, 0.0, minus),
                    jnp.where(lane >= 126, 0.0, plus2),
                    jnp.where(lane < 2, 0.0, minus2),
                )
                gx_, lx = terms(*(src[i, 8 + x + o, at] for o in (1, -1, 2, -2)))
                gy_, ly = terms(*(src[i, 8 + x, r + o : r + o + 16] for o in (1, -1, 2, -2)))
                mix = cc[i][0] * q[0] + cc[i][1] * q[1] + (cc[i][2] * q[2] + cc[i][3] * q[3])
                moved = u[0] * gx_ + u[1] * gy_ + u[2] * gz_
                t = dd[i] * (lx + ly + lz) - moved + q[i] * (mix - 6.0 * dd[i])
                row = pl.multiple_of(base + (r - 8), 8)
                final[i, pl.ds(row, 16), 0:128] = half(state[i, 8 + x, at], q[i], t)
                one = jnp.where(lane == 127, plus, jnp.where(lane == 0, -minus, 0.0))
                two = jnp.where(lane >= 126, plus2, jnp.where(lane < 2, -minus2, 0.0))
                spread = jnp.where(lane == 127, plus, jnp.where(lane == 0, minus, 0.0))
                beyond = (0.5 * dd[i]) * spread - u_out * (8.0 * one - two)
                final[i, pl.ds(row, 16), 128:256] = jnp.where((lane >= 126) | (lane < 2), beyond, 0.0)
        row8 = lax.broadcasted_iota(jnp.int32, (8, 128), 0)
        for r, to, kept in ((8, 0, row8 >= 6), (48, 40, row8 < 2)):
            u_y = wind[1, 8 + x, r : r + 8]
            for i in range(4):
                gy_, ly = terms(*(section[i, 8 + x, r + o : r + o + 8] for o in (1, -1, 2, -2)))
                row = pl.multiple_of(base + to, 8)
                face = jnp.where(kept, 0.5 * (dd[i] * ly - u_y * gy_), 0.0)
                final[i, pl.ds(row, 8), 0:128] = face
                final[i, pl.ds(row, 8), 128:256] = jnp.zeros((8, 128), F32)

    for i in range(4):
        first, second = section[i, 8, 16:48], section[i, 9, 16:48]
        last, before = section[i, 15, 16:48], section[i, 14, 16:48]
        u = [wind[0, x, 16:48] for x in (6, 7, 16, 17)]
        faces[i, 0:32] = 0.5 * (u[0] * first)
        faces[i, 32:64] = 0.5 * (dd[i] * first - u[1] * (8.0 * first - second))
        faces[i, 64:96] = 0.5 * (dd[i] * last + u[2] * (8.0 * last - before))
        faces[i, 96:128] = -0.5 * (u[3] * last)

    total = dot(final[0], rhs[0], 1, 1)
    total_faces = dot(faces[0], rhs[0, :, 0:128], 1, 1)
    for i in range(1, 4):
        total = total + dot(final[i], rhs[i], 1, 1)
        total_faces = total_faces + dot(faces[i], rhs[i, :, 0:128], 1, 1)
    for x in range(8):
        mixed[x * 32 : x * 32 + 32] = dot(fye[...], total[x * 48 : x * 48 + 48], 0, 0)
    for x in range(4):
        mixed[256 + x * 32 : 288 + x * 32] = dot(fy[...], total_faces[x * 32 : x * 32 + 32], 0, 0)
    lane = lanes_of(4)
    for j in range(8):
        for t in range(3):
            tiles = [mixed[pl.ds(128 * t + 4 * j + b, 4, stride=32), :] for b in range(4)]
            for k in range(4):
                tile = jnp.zeros((4, 128), F32)
                for b in range(4):
                    tile = jnp.where(within(lane, 32 * b, 32), roll(tiles[b], 32 * (b - k)), tile)
                out[j * 4 + k, :, 128 * t : 128 * t + 128] = tile


def contract_x(parts, fx, e_even, e_odd, out):
    total = parts[0]
    for p in range(1, parts.shape[0]):
        total = total + parts[p]
    e_low, e_high = sides("gx", e_even, e_odd)
    outer = [e_low(33, slice(6, 8), slice(0, 32)), e_high(33, slice(0, 2), slice(0, 32))]
    outer = jnp.concatenate(outer, axis=0)
    result = dot(fx[0:4], total[:, 0:128], 0, 0) + dot(fx[4:8], total[:, 128:256], 0, 0)
    out[...] = result + dot(outer, total[:, 256:384], 0, 0)


def local(fields, velocity, diffusivity, coupling, factor_x, factor_y, factor_z):
    def swapped(axis, even, odd):
        last = lax.axis_size(axis) - 1
        pairs = [[(i, i + 1) for i in range(first, last, 2)] for first in (0, 1)]
        even_pairs, odd_pairs = ([*p, *((b, a) for a, b in p)] for p in pairs)
        even = lax.ppermute(even, axis, even_pairs)
        return even, lax.ppermute(odd, axis, odd_pairs)

    x_even, x_odd, z_even, z_odd, fields, velocity, fz = call(
        pack_xz,
        [f32(36, 32, 128)] * 2 + [f32(8, 32, 128)] * 2
        + [f32(4, 8, 32, 128), f32(3, 8, 32, 128), f32(32, 128)],
        [pl.BlockSpec(memory_space=pltpu.HBM)] * 3,
        scratch=[pltpu.SemaphoreType.DMA((3,))],
    )(*(pltpu.with_memory_space_constraint(a, pltpu.HBM) for a in (fields, velocity, factor_z.T)))
    z_even, z_odd = swapped("gz", z_even, z_odd)
    y_even, y_odd = call(pack_y, [f32(49, 8, 128)] * 2, [vmem()] * 5)(fields, velocity, factor_y, z_even, z_odd)
    y_even, y_odd = swapped("gy", y_even, y_odd)
    x_even, x_odd = swapped("gx", x_even, x_odd)
    e_even, e_odd = call(pack_x2, [f32(34, 8, 128)] * 2, [vmem()] * 5)(z_even, z_odd, y_even, y_odd, factor_x)
    e_even, e_odd = swapped("gx", e_even, e_odd)

    def tiles(*lead):
        return f32(*lead, ROWS, 128)

    gx = lax.axis_size("gx")
    buffers = [
        tiles(4, PLANES), tiles(4, PLANES), tiles(PLANES), tiles(PLANES),
        tiles(3, PLANES), tiles(3, PLANES), tiles(PLANES),
    ]
    *filled, rhs, fye = call(
        prepare, [*buffers, f32(4, 128, 256), f32(48, 32)], [smem()] * 2 + [vmem()] * 8, work=3000000
    )(diffusivity, coupling, fields, velocity, z_even, z_odd, y_even, y_odd, fz, factor_y)
    parts, *_ = call(
        advance,
        [f32(32, 4, 384), *buffers],
        [smem()] * 2 + [vmem()] * 14,
        scratch=[
            pltpu.VMEM((4, 384, 256), F32), pltpu.VMEM((4, 128, 128), F32), pltpu.VMEM((384, 128), F32)
        ],
        work=10000000,
        aliases={9 + n: 1 + n for n in range(7)},
    )(diffusivity, coupling, x_even, x_odd, e_even, e_odd, factor_y, rhs, fye, *filled)
    parts = lax.all_to_all(parts, ("gy", "gz"), 0, 0, tiled=True)
    slices = call(contract_x, f32(32, 128), [vmem()] * 4)(
        parts, factor_x, e_even, e_odd
    )
    slices = lax.all_to_all(slices, "gx", 0, 0, tiled=True)
    core = jnp.sum(slices.reshape(gx, 32 // gx, 4, 4, 8), axis=0)
    return core.transpose(2, 0, 1, 3)


def solution(mesh):
    return jax.shard_map(
        local,
        mesh=mesh,
        in_specs=(
            P(None, "gx", "gy", "gz"),
            P(None, "gx", "gy", "gz"),
            P(),
            P(),
            P("gx", None),
            P("gy", None),
            P("gz", None),
        ),
        out_specs=P(None, "gx", "gy", "gz"),
        check_vma=False,
    )
```

```python
import jax
import jax.numpy as jnp
from jax import lax
from jax.experimental import pallas as pl
from jax.experimental.pallas import tpu as pltpu
from jax.sharding import PartitionSpec as P


TIME_STEP = 0.2
F32 = jnp.float32
PLANES, ROWS = 24, 64
LOW, HIGH = 8, 16


def vmem():
    return pl.BlockSpec(memory_space=pltpu.VMEM)


def smem():
    return pl.BlockSpec(memory_space=pltpu.SMEM)


def f32(*shape):
    return jax.ShapeDtypeStruct(shape, F32)


def call(kernel, out_shape, in_specs, scratch=(), work=1000000, mib=8, aliases=None):
    many = isinstance(out_shape, (list, tuple))
    return pl.pallas_call(
        kernel,
        out_shape=out_shape,
        in_specs=in_specs,
        out_specs=[vmem() for _ in out_shape] if many else vmem(),
        scratch_shapes=list(scratch),
        input_output_aliases=aliases or {},
        compiler_params=pltpu.CompilerParams(vmem_limit_bytes=mib << 20),
        cost_estimate=pl.CostEstimate(flops=work, bytes_accessed=work, transcendentals=0),
    )


def lanes_of(rows):
    return lax.broadcasted_iota(jnp.int32, (rows, 128), 1)


def within(lane, first, size):
    return (lane >= first) & (lane < first + size)


def halves(a):
    high = a.astype(jnp.bfloat16)
    return high, (a - high.astype(F32)).astype(jnp.bfloat16)


def dot(a, b, a_dim, b_dim):
    def product(p, q):
        return lax.dot_general(p, q, (((a_dim,), (b_dim,)), ((), ())), preferred_element_type=F32)

    (a_high, a_low), (b_high, b_low) = halves(a), halves(b)
    both = product(a_high, jnp.concatenate([b_high, b_low], axis=1 - b_dim))
    return both[:, 0:128] + (both[:, 128:256] + product(a_low, b_high))


def padded(rows):
    return jnp.concatenate([rows, jnp.zeros((rows.shape[0], 128 - rows.shape[1]), F32)], axis=1)


def ways(axis):
    odd = lax.rem(lax.axis_index(axis), 2)
    return 1 - odd, odd


def pack_xz(f_in, v_in, fz_in, fy_in, fx_in, x_even, x_odd, z_even, z_odd, f, v, fz, fy, fx, arrived):
    pairs = ((f_in, f), (v_in, v), (fz_in, fz), (fy_in, fy), (fx_in, fx))
    copies = [pltpu.make_async_copy(a, b, arrived.at[n]) for n, (a, b) in enumerate(pairs)]
    for copy in copies:
        copy.start()
    for copy in copies:
        copy.wait()
    lane = lanes_of(32)
    for out, up in zip((x_even, x_odd), ways("gx")):
        for j in range(6):
            for i in range(4):
                out[i * 6 + j] = f[i, 2 * up + j]
        for j in range(4):
            for a in range(3):
                out[24 + a * 4 + j] = v[a, 4 * up + j]
    even_up, _ = ways("gz")

    def plane_edges(x, carry):
        up = jnp.zeros((32, 128), F32)
        down = jnp.zeros((32, 128), F32)
        for i in range(4):
            plane = f[i, x]
            up = jnp.where(within(lane, 32 * i, 8), pltpu.roll(plane, (32 * i + 8) % 128, 1), up)
            down = jnp.where(within(lane, 32 * i + 24, 8), pltpu.roll(plane, 32 * i + 24, 1), down)
        for a in range(4):
            plane = pltpu.roll(v[a, x] if a < 3 else fz[...], 32 * a + 16, 1)
            up = jnp.where(within(lane, 32 * a + 8, 8), plane, up)
            down = jnp.where(within(lane, 32 * a + 16, 8), plane, down)
        z_even[x] = jnp.where(even_up == 1, up, down)
        z_odd[x] = jnp.where(even_up == 1, down, up)
        return carry

    lax.fori_loop(0, 8, plane_edges, 0)


def pack_y(f, v, fy, z_even, z_odd, y_even, y_odd):
    for out, up in zip((y_even, y_odd), ways("gy")):

        def edge_rows(high, low):
            return jnp.where(up == 1, high, low)

        for x in range(8):
            half = slice(4 * (x % 2), 4 * (x % 2) + 4)
            for i in range(4):
                out[i * 8 + x] = edge_rows(f[i, x, 24:32], f[i, x, 0:8])
            for a in range(3):
                out[32 + a * 4 + x // 2, half] = edge_rows(v[a, x, 28:32], v[a, x, 0:4])
            out[44 + x // 2, half] = edge_rows(
                z_even[x, 28:32] + z_odd[x, 28:32], z_even[x, 0:4] + z_odd[x, 0:4]
            )
        out[48] = padded(edge_rows(fy[24:32], fy[0:8]))


def sides(axis, even, odd):
    low_is_odd = ways(axis)[0] == 1

    def low(*at):
        return jnp.where(low_is_odd, odd[at], even[at])

    def high(*at):
        return jnp.where(low_is_odd, even[at], odd[at])

    return low, high


def pack_x2(z_even, z_odd, y_even, y_odd, fx, even, odd):
    y_low, y_high = sides("gy", y_even, y_odd)
    for out, up in zip((even, odd), ways("gx")):
        near, far, first = 6 * up, 2 + 2 * up, 4 * up
        for side, rows in ((0, y_low), (1, y_high)):
            four = slice(4, 8) if side == 0 else slice(0, 4)
            two = slice(6, 8) if side == 0 else slice(0, 2)
            for j in range(2):
                for i in range(4):
                    out[i * 2 + side, 4 * j : 4 * j + 4] = rows(i * 8 + near + j, four)
                    at = 4 * (i % 2) + 2 * j
                    out[8 + i // 2 * 2 + side, at : at + 2] = rows(i * 8 + far + j, two)
                at = 4 * j + (2 if side == 0 else 0)
                for a in range(3):
                    to = 4 * (a % 2) + 2 * j
                    out[12 + a // 2 * 2 + side, to : to + 2] = rows(32 + a * 4 + 3 * up, slice(at, at + 2))
                to = 4 * side + 2 * j
                out[32, to : to + 2] = rows(44 + 3 * up, slice(at, at + 2))
        for j in range(4):
            halo = z_even[first + j] + z_odd[first + j]
            for t in range(4):
                out[16 + j * 4 + t] = halo[8 * t : 8 * t + 8]
        out[33] = padded(fx[...])


FULL, OWN = (8, 24, 40), (16, 32)
SCALE = TIME_STEP / 12.0


def chunk(rows):
    lane = lanes_of(rows)
    return lane, lane % 32, lax.broadcasted_iota(jnp.int32, (rows, 128), 0)


def roll(value, by):
    return pltpu.roll(value, by % 128, 1)


def slabs(state, wind, zm, edge, edge_wind, x, r, rows, winds):
    lane, in_group, _ = chunk(rows)
    halo = zm[x, r : r + rows]
    tile = halo
    for i in range(4):
        q = state[i, x, r : r + rows]
        tile = jnp.where(within(lane, 32 * i + 8, 8), roll(q, 32 * i + 8), tile)
        tile = jnp.where(within(lane, 32 * i + 16, 8), roll(q, 32 * i + 24), tile)
    edge[x, r : r + rows] = tile
    if winds:
        halo = halo * SCALE
        packed = jnp.where(in_group < 8, roll(halo, -8), roll(halo, 8))
        for a in range(3):
            q = wind[a, x, r : r + rows]
            packed = jnp.where(within(lane, 32 * a + 8, 8), roll(q, 32 * a + 8), packed)
            packed = jnp.where(within(lane, 32 * a + 16, 8), roll(q, 32 * a + 24), packed)
        for a in range(3):
            one = jnp.where(within(lane, 32 * a, 32), packed, 0.0)
            one = one + roll(one, 32)
            edge_wind[a, x, r : r + rows] = one + roll(one, 64)


def terms(plus, minus, plus2, minus2):
    return 8.0 * (plus - minus) - (plus2 - minus2), plus + minus


def half(base, q, t):
    return 0.5 * (base + q + t)


class Stencil:
    def __init__(self, d, c, wind, edge_wind):
        self.wind, self.edge_wind = wind, edge_wind
        self.dd = [d[i] * TIME_STEP for i in range(4)]
        self.cc = [[c[i, w] * TIME_STEP for w in range(4)] for i in range(4)]
        gx, gy, self.gz = (lax.axis_index(n) for n in ("gx", "gy", "gz"))
        last_x, last_y, self.last_z = (lax.axis_size(n) - 1 for n in ("gx", "gy", "gz"))
        self.x_first, self.x_end = jnp.where(gx == 0, LOW, 0), jnp.where(gx == last_x, HIGH, PLANES)
        self.y_first, self.y_end = jnp.where(gy == 0, 16, 0), jnp.where(gy == last_y, 48, ROWS)

    def tendencies(self, src, slab, x, r, rows):
        dd, cc, wind = self.dd, self.cc, self.wind
        lane, in_group, _ = chunk(rows)
        at = slice(r, r + rows)
        u = [wind[a, x, at] for a in range(3)]
        q = [src[i, x, at] for i in range(4)]
        s = slab[x, at]
        s = jnp.where(in_group >= 24, s, roll(s, 16))
        results = []
        for i in range(4):
            ends = roll(s, -24 - 32 * i)
            gz_, lz = terms(
                roll(jnp.where(lane == 0, ends, q[i]), -1),
                roll(jnp.where(lane == 127, ends, q[i]), 1),
                roll(jnp.where(lane < 2, ends, q[i]), -2),
                roll(jnp.where(lane >= 126, ends, q[i]), 2),
            )
            gx_, lx = terms(src[i, x + 1, at], src[i, x - 1, at], src[i, x + 2, at], src[i, x - 2, at])
            gy_, ly = terms(*(src[i, x, r + o : r + o + rows] for o in (1, -1, 2, -2)))
            mix = cc[i][0] * q[0] + cc[i][1] * q[1] + (cc[i][2] * q[2] + cc[i][3] * q[3])
            moved = u[0] * gx_ + u[1] * gy_ + u[2] * gz_
            results.append(dd[i] * (lx + ly + lz) - moved + q[i] * (mix - 6.0 * dd[i]))
        return q, results

    def slab_tendency(self, slab, x, r, rows):
        dd, cc, edge_wind = self.dd, self.cc, self.edge_wind
        lane, _, _ = chunk(rows)
        group = lane // 32
        at = slice(r, r + rows)

        def by_group(values):
            return jnp.where(group < 2, jnp.where(group == 0, values[0], values[1]),
                             jnp.where(group == 2, values[2], values[3]))

        q = slab[x, at]
        gz_, lz = terms(roll(q, -1), roll(q, 1), roll(q, -2), roll(q, 2))
        gx_, lx = terms(slab[x + 1, at], slab[x - 1, at], slab[x + 2, at], slab[x - 2, at])
        gy_, ly = terms(*(slab[x, r + o : r + o + rows] for o in (1, -1, 2, -2)))
        mix = -6.0 * by_group(dd)
        for k in range(4):
            mix = mix + by_group([cc[i][(i - k) % 4] for i in range(4)]) * roll(q, 32 * k)
        moved = edge_wind[0, x, at] * gx_ + edge_wind[1, x, at] * gy_ + edge_wind[2, x, at] * gz_
        return q, by_group(dd) * (lx + ly + lz) - moved + q * mix

    def inside(self, x, r, rows):
        _, in_group, row = chunk(rows)
        first = jnp.where((x >= self.x_first) & (x < self.x_end), self.y_first, ROWS)
        ok = (row + r >= first) & (row + r < self.y_end)
        z_ok = ((in_group >= 8) | (self.gz != 0)) & ((in_group < 24) | (self.gz != self.last_z))
        return ok, z_ok

    def stage(self, x, rows_at, slab_rows, src, slab, dst, slab_dst, mean):
        for r in rows_at:
            at = slice(r, r + 16)
            ok, _ = self.inside(x, r, 16)
            q, t = self.tendencies(src, slab, x, r, 16)
            for i in range(4):
                new = half(dst[i, x, at], q[i], t[i]) if mean else q[i] + t[i]
                dst[i, x, at] = jnp.where(ok, new, 0.0)
        for r in slab_rows:
            at = slice(r, r + 16)
            ok, z_ok = self.inside(x, r, 16)
            q, t = self.slab_tendency(slab, x, r, 16)
            new = half(slab_dst[x, at], q, t) if mean else q + t
            slab_dst[x, at] = jnp.where(ok & z_ok, new, 0.0)


def prepare(
    d, c, f, v, z_even, z_odd, y_even, y_odd, fz, fy,
    state, section, edge, edge2, wind, edge_wind, zm, rhs, fye,
):
    y_low, y_high = sides("gy", y_even, y_odd)
    for i in range(4):
        for x in range(8):
            state[i, 8 + x, 16:48] = f[i, x]
            state[i, 8 + x, 8:16] = y_low(i * 8 + x)
            state[i, 8 + x, 48:56] = y_high(i * 8 + x)
    for x in range(8):
        half_tile = slice(4 * (x % 2), 4 * (x % 2) + 4)
        for a in range(3):
            wind[a, 8 + x, 16:48] = v[a, x] * SCALE
            wind[a, 8 + x, 12:16] = y_low(32 + a * 4 + x // 2, half_tile) * SCALE
            wind[a, 8 + x, 48:52] = y_high(32 + a * 4 + x // 2, half_tile) * SCALE
        zm[8 + x, 16:48] = z_even[x] + z_odd[x]
        zm[8 + x, 12:16] = y_low(44 + x // 2, half_tile)
        zm[8 + x, 48:52] = y_high(44 + x // 2, half_tile)
    lane = lanes_of(32)
    outer = jnp.where((lane >= 126) | (lane < 2), roll(zm[8, 16:48], 16), 0.0)
    rhs[...] = jnp.zeros((4, 128, 256), F32)
    for i in range(4):
        for k in range(4):
            at = slice(32 * k + 8 * i, 32 * k + 8 * i + 8)
            rhs[i, at, 0:128] = fz[8 * k : 8 * k + 8]
            rhs[i, at, 128:256] = outer[8 * k : 8 * k + 8]
    fye[0:8] = y_low(48, slice(0, 8), slice(0, 32))
    fye[8:40] = fy[...]
    fye[40:48] = y_high(48, slice(0, 8), slice(0, 32))

    @pl.loop(8, 16)
    def _(x):
        for r in FULL:
            slabs(state, wind, zm, edge, edge_wind, x, r, 16, True)

    stencil = Stencil(d, c, wind, edge_wind)

    @pl.loop(10, 14)
    def _(x):
        stencil.stage(x, FULL, FULL, state, edge, section, edge2, False)


def advance(
    d, c, x_even, x_odd, e_even, e_odd, fy, rhs, fye, *refs
):
    out, state, section, edge, edge2, wind, edge_wind, zm, final, faces, mixed = refs[7:]
    stencil = Stencil(d, c, wind, edge_wind)
    dd, cc, stage, scale = stencil.dd, stencil.cc, stencil.stage, SCALE
    full, own = FULL, OWN
    even_up, odd_up = ways("gx")
    for halo, above in ((x_even, even_up), (x_odd, odd_up)):
        for j in range(6):
            for i in range(4):
                state[i, 2 + 14 * above + j, 16:48] = halo[i * 6 + j]
        for j in range(4):
            for a in range(3):
                wind[a, 4 + 12 * above + j, 16:48] = halo[24 + a * 4 + j] * scale
    for e, above in ((e_even, even_up), (e_odd, odd_up)):
        near, far, first = 6 + 10 * above, 4 + 14 * above, 4 + 12 * above
        for j in range(2):
            for i in range(4):
                state[i, near + j, 12:16] = e[i * 2, 4 * j : 4 * j + 4]
                state[i, near + j, 48:52] = e[i * 2 + 1, 4 * j : 4 * j + 4]
                at = 4 * (i % 2) + 2 * j
                state[i, far + j, 14:16] = e[8 + i // 2 * 2, at : at + 2]
                state[i, far + j, 48:50] = e[9 + i // 2 * 2, at : at + 2]
            for a in range(3):
                at = 4 * (a % 2) + 2 * j
                wind[a, near + j, 14:16] = e[12 + a // 2 * 2, at : at + 2] * scale
                wind[a, near + j, 48:50] = e[13 + a // 2 * 2, at : at + 2] * scale
            zm[near + j, 14:16] = e[32, 2 * j : 2 * j + 2]
            zm[near + j, 48:50] = e[32, 4 + 2 * j : 6 + 2 * j]
        for j in range(4):
            for t in range(4):
                zm[first + j, 16 + 8 * t : 24 + 8 * t] = e[16 + j * 4 + t]

    @pl.loop(0, 4)
    def _(j):
        x = jnp.where(j < 2, 6 + j, 14 + j)
        for r in full:
            slabs(state, wind, zm, edge, edge_wind, x, r, 16, True)
        x = jnp.where(j < 2, 4 + j, 16 + j)
        for r in own:
            slabs(state, wind, zm, edge, edge_wind, x, r, 16, False)

    @pl.loop(0, 8)
    def _(j):
        x = jnp.where(j < 4, 6 + j, 10 + j)
        stage(x, full, full, state, edge, section, edge2, False)

    @pl.loop(0, 4, unroll=2)
    def _(j):
        stage(jnp.where(j < 2, 4 + j, 16 + j), own, (), state, edge, section, edge2, False)

    @pl.loop(8, 16)
    def _(x):
        stage(x, full, own, section, edge2, state, edge, True)

    @pl.loop(0, 4, unroll=2)
    def _(j):
        stage(jnp.where(j < 2, 6 + j, 14 + j), own, (), section, edge2, state, edge, True)

    @pl.loop(8, 16, unroll=2)
    def _(x):
        stage(x, own, (), state, edge, section, edge2, False)

    for i in range(4):
        for x in (6, 7, 16, 17):
            section[i, x, 16:48] = jnp.zeros((32, 128), F32)
        for x in range(8):
            section[i, 8 + x, 0:16] = jnp.zeros((16, 128), F32)
            section[i, 8 + x, 48:64] = jnp.zeros((16, 128), F32)

    @pl.loop(0, 8, unroll=2)
    def _(x):
        base = pl.multiple_of(x * 48, 16)
        for r in own:
            lane, _, _ = chunk(16)
            at = slice(r, r + 16)
            u = [wind[a, 8 + x, at] for a in range(3)]
            u_out = roll(zm[8 + x, at], 48) * (0.5 * scale)
            q = [section[i, 8 + x, at] for i in range(4)]
            for i in range(4):
                plus, minus, plus2, minus2 = (roll(q[i], o) for o in (-1, 1, -2, 2))
                src = section
                gz_, lz = terms(
                    jnp.where(lane == 127, 0.0, plus),
                    jnp.where(lane == 0, 0.0, minus),
                    jnp.where(lane >= 126, 0.0, plus2),
                    jnp.where(lane < 2, 0.0, minus2),
                )
                gx_, lx = terms(*(src[i, 8 + x + o, at] for o in (1, -1, 2, -2)))
                gy_, ly = terms(*(src[i, 8 + x, r + o : r + o + 16] for o in (1, -1, 2, -2)))
                mix = cc[i][0] * q[0] + cc[i][1] * q[1] + (cc[i][2] * q[2] + cc[i][3] * q[3])
                moved = u[0] * gx_ + u[1] * gy_ + u[2] * gz_
                t = dd[i] * (lx + ly + lz) - moved + q[i] * (mix - 6.0 * dd[i])
                row = pl.multiple_of(base + (r - 8), 8)
                final[i, pl.ds(row, 16), 0:128] = half(state[i, 8 + x, at], q[i], t)
                one = jnp.where(lane == 127, plus, jnp.where(lane == 0, -minus, 0.0))
                two = jnp.where(lane >= 126, plus2, jnp.where(lane < 2, -minus2, 0.0))
                spread = jnp.where(lane == 127, plus, jnp.where(lane == 0, minus, 0.0))
                beyond = (0.5 * dd[i]) * spread - u_out * (8.0 * one - two)
                final[i, pl.ds(row, 16), 128:256] = jnp.where((lane >= 126) | (lane < 2), beyond, 0.0)
        row8 = lax.broadcasted_iota(jnp.int32, (8, 128), 0)
        for r, to, kept in ((8, 0, row8 >= 6), (48, 40, row8 < 2)):
            u_y = wind[1, 8 + x, r : r + 8]
            for i in range(4):
                gy_, ly = terms(*(section[i, 8 + x, r + o : r + o + 8] for o in (1, -1, 2, -2)))
                row = pl.multiple_of(base + to, 8)
                face = jnp.where(kept, 0.5 * (dd[i] * ly - u_y * gy_), 0.0)
                final[i, pl.ds(row, 8), 0:128] = face
                final[i, pl.ds(row, 8), 128:256] = jnp.zeros((8, 128), F32)

    for i in range(4):
        first, second = section[i, 8, 16:48], section[i, 9, 16:48]
        last, before = section[i, 15, 16:48], section[i, 14, 16:48]
        u = [wind[0, x, 16:48] for x in (6, 7, 16, 17)]
        faces[i, 0:32] = 0.5 * (u[0] * first)
        faces[i, 32:64] = 0.5 * (dd[i] * first - u[1] * (8.0 * first - second))
        faces[i, 64:96] = 0.5 * (dd[i] * last + u[2] * (8.0 * last - before))
        faces[i, 96:128] = -0.5 * (u[3] * last)

    total = dot(final[0], rhs[0], 1, 1)
    total_faces = dot(faces[0], rhs[0, :, 0:128], 1, 1)
    for i in range(1, 4):
        total = total + dot(final[i], rhs[i], 1, 1)
        total_faces = total_faces + dot(faces[i], rhs[i, :, 0:128], 1, 1)
    for x in range(8):
        mixed[x * 32 : x * 32 + 32] = dot(fye[...], total[x * 48 : x * 48 + 48], 0, 0)
    for x in range(4):
        mixed[256 + x * 32 : 288 + x * 32] = dot(fy[...], total_faces[x * 32 : x * 32 + 32], 0, 0)
    for planes, first in ((8, 0), (4, 8)):
        lane = lanes_of(planes)
        for j in range(8):
            rows = [pl.ds(32 * first + 4 * j + b, planes, stride=32) for b in range(4)]
            tiles = [mixed[at, :] for at in rows]
            for k in range(4):
                tile = jnp.zeros((planes, 128), F32)
                for b in range(4):
                    tile = jnp.where(within(lane, 32 * b, 32), roll(tiles[b], 32 * (b - k)), tile)
                for t in range(planes // 4):
                    at = 32 * first + 128 * t
                    out[j * 4 + k, :, at : at + 128] = tile[4 * t : 4 * t + 4]


def contract_x(parts, fx, e_even, e_odd, out):
    total = parts[0]
    for p in range(1, parts.shape[0]):
        total = total + parts[p]
    e_low, e_high = sides("gx", e_even, e_odd)
    outer = [e_low(33, slice(6, 8), slice(0, 32)), e_high(33, slice(0, 2), slice(0, 32))]
    outer = jnp.concatenate(outer, axis=0)
    result = dot(fx[0:4], total[:, 0:128], 0, 0) + dot(fx[4:8], total[:, 128:256], 0, 0)
    out[...] = result + dot(outer, total[:, 256:384], 0, 0)


def local(fields, velocity, diffusivity, coupling, factor_x, factor_y, factor_z):
    def swapped(axis, even, odd):
        last = lax.axis_size(axis) - 1
        pairs = [[(i, i + 1) for i in range(first, last, 2)] for first in (0, 1)]
        even_pairs, odd_pairs = ([*p, *((b, a) for a, b in p)] for p in pairs)
        even = lax.ppermute(even, axis, even_pairs)
        return even, lax.ppermute(odd, axis, odd_pairs)

    inputs = (fields, velocity, factor_z.T, factor_y, factor_x)
    x_even, x_odd, z_even, z_odd, fields, velocity, fz, fy, fx = call(
        pack_xz,
        [f32(36, 32, 128)] * 2 + [f32(8, 32, 128)] * 2 + [f32(*a.shape) for a in inputs],
        [pl.BlockSpec(memory_space=pltpu.HBM)] * 5,
        scratch=[pltpu.SemaphoreType.DMA((5,))],
    )(*(pltpu.with_memory_space_constraint(a, pltpu.HBM) for a in inputs))
    z_even, z_odd = swapped("gz", z_even, z_odd)
    y_even, y_odd = call(pack_y, [f32(49, 8, 128)] * 2, [vmem()] * 5)(
        fields, velocity, fy, z_even, z_odd
    )
    y_even, y_odd = swapped("gy", y_even, y_odd)
    x_even, x_odd = swapped("gx", x_even, x_odd)
    e_even, e_odd = call(pack_x2, [f32(34, 8, 128)] * 2, [vmem()] * 5)(
        z_even, z_odd, y_even, y_odd, fx
    )
    e_even, e_odd = swapped("gx", e_even, e_odd)

    def tiles(*lead):
        return f32(*lead, ROWS, 128)

    gx = lax.axis_size("gx")
    buffers = [
        tiles(4, PLANES), tiles(4, PLANES), tiles(PLANES), tiles(PLANES),
        tiles(3, PLANES), tiles(3, PLANES), tiles(PLANES),
    ]
    *filled, rhs, fye = call(
        prepare, [*buffers, f32(4, 128, 256), f32(48, 32)], [smem()] * 2 + [vmem()] * 8, work=3000000
    )(diffusivity, coupling, fields, velocity, z_even, z_odd, y_even, y_odd, fz, fy)
    parts, *_ = call(
        advance,
        [f32(32, 4, 384), *buffers],
        [smem()] * 2 + [vmem()] * 14,
        scratch=[
            pltpu.VMEM((4, 384, 256), F32), pltpu.VMEM((4, 128, 128), F32),
            pltpu.VMEM((384, 128), F32),
        ],
        work=10000000,
        aliases={9 + n: 1 + n for n in range(7)},
    )(diffusivity, coupling, x_even, x_odd, e_even, e_odd, fy, rhs, fye, *filled)
    parts = lax.all_to_all(parts, ("gy", "gz"), 0, 0, tiled=True)
    slices = call(contract_x, f32(32, 128), [vmem()] * 4)(
        parts, fx, e_even, e_odd
    )
    slices = lax.all_to_all(slices, "gx", 0, 0, tiled=True)
    core = jnp.sum(slices.reshape(gx, 32 // gx, 4, 4, 8), axis=0)
    return core.transpose(2, 0, 1, 3)


def solution(mesh):
    return jax.shard_map(
        local,
        mesh=mesh,
        in_specs=(
            P(None, "gx", "gy", "gz"),
            P(None, "gx", "gy", "gz"),
            P(),
            P(),
            P("gx", None),
            P("gy", None),
            P("gz", None),
        ),
        out_specs=P(None, "gx", "gy", "gz"),
        check_vma=False,
    )
```

```python
import jax
import jax.numpy as jnp
from jax import lax
from jax.experimental import pallas as pl
from jax.experimental.pallas import tpu as pltpu
from jax.sharding import PartitionSpec as P


TIME_STEP = 0.2
F32 = jnp.float32
PLANES, ROWS = 24, 64
LOW, HIGH = 8, 16


def vmem():
    return pl.BlockSpec(memory_space=pltpu.VMEM)


def hbm():
    return pl.BlockSpec(memory_space=pltpu.HBM)


def in_hbm(*arrays):
    return [pltpu.with_memory_space_constraint(a, pltpu.HBM) for a in arrays]


def f32(*shape):
    return jax.ShapeDtypeStruct(shape, F32)


def call(kernel, out_shape, in_specs, scratch=(), work=1000000, mib=8, aliases=None):
    many = isinstance(out_shape, (list, tuple))
    return pl.pallas_call(
        kernel,
        out_shape=out_shape,
        in_specs=in_specs,
        out_specs=[vmem() for _ in out_shape] if many else vmem(),
        scratch_shapes=list(scratch),
        input_output_aliases=aliases or {},
        compiler_params=pltpu.CompilerParams(vmem_limit_bytes=mib << 20),
        cost_estimate=pl.CostEstimate(flops=work, bytes_accessed=work, transcendentals=0),
    )


def lanes_of(rows):
    return lax.broadcasted_iota(jnp.int32, (rows, 128), 1)


def within(lane, first, size):
    return (lane >= first) & (lane < first + size)


def halves(a):
    high = a.astype(jnp.bfloat16)
    return high, (a - high.astype(F32)).astype(jnp.bfloat16)


def dot(a, b, a_dim, b_dim):
    def product(p, q):
        return lax.dot_general(p, q, (((a_dim,), (b_dim,)), ((), ())), preferred_element_type=F32)

    (a_high, a_low), (b_high, b_low) = halves(a), halves(b)
    both = product(a_high, jnp.concatenate([b_high, b_low], axis=1 - b_dim))
    return both[:, 0:128] + (both[:, 128:256] + product(a_low, b_high))


def padded(rows):
    return jnp.concatenate([rows, jnp.zeros((rows.shape[0], 128 - rows.shape[1]), F32)], axis=1)


def ways(axis):
    odd = lax.rem(lax.axis_index(axis), 2)
    return 1 - odd, odd


def pack_xz(f_in, v_in, fz_in, fy_in, fx_in, x_even, x_odd, z_even, z_odd, f, v, fz, fy, fx, arrived):
    pairs = ((f_in, f), (v_in, v), (fz_in, fz), (fy_in, fy), (fx_in, fx))
    copies = [pltpu.make_async_copy(a, b, arrived.at[n]) for n, (a, b) in enumerate(pairs)]
    for copy in copies:
        copy.start()
    for copy in copies:
        copy.wait()
    lane = lanes_of(32)
    for out, up in zip((x_even, x_odd), ways("gx")):
        for j in range(6):
            for i in range(4):
                out[i * 6 + j] = f[i, 2 * up + j]
        for j in range(4):
            for a in range(3):
                out[24 + a * 4 + j] = v[a, 4 * up + j]
    even_up, _ = ways("gz")

    def plane_edges(x, carry):
        up = jnp.zeros((32, 128), F32)
        down = jnp.zeros((32, 128), F32)
        for i in range(4):
            plane = f[i, x]
            up = jnp.where(within(lane, 32 * i, 8), pltpu.roll(plane, (32 * i + 8) % 128, 1), up)
            down = jnp.where(within(lane, 32 * i + 24, 8), pltpu.roll(plane, 32 * i + 24, 1), down)
        for a in range(4):
            plane = pltpu.roll(v[a, x] if a < 3 else fz[...], 32 * a + 16, 1)
            up = jnp.where(within(lane, 32 * a + 8, 8), plane, up)
            down = jnp.where(within(lane, 32 * a + 16, 8), plane, down)
        z_even[x] = jnp.where(even_up == 1, up, down)
        z_odd[x] = jnp.where(even_up == 1, down, up)
        return carry

    lax.fori_loop(0, 8, plane_edges, 0)


def pack_y(f, v, fy, z_even, z_odd, y_even, y_odd):
    for out, up in zip((y_even, y_odd), ways("gy")):

        def edge_rows(high, low):
            return jnp.where(up == 1, high, low)

        for x in range(8):
            half = slice(4 * (x % 2), 4 * (x % 2) + 4)
            for i in range(4):
                out[i * 8 + x] = edge_rows(f[i, x, 24:32], f[i, x, 0:8])
            for a in range(3):
                out[32 + a * 4 + x // 2, half] = edge_rows(v[a, x, 28:32], v[a, x, 0:4])
            out[44 + x // 2, half] = edge_rows(
                z_even[x, 28:32] + z_odd[x, 28:32], z_even[x, 0:4] + z_odd[x, 0:4]
            )
        out[48] = padded(edge_rows(fy[24:32], fy[0:8]))


def sides(axis, even, odd):
    low_is_odd = ways(axis)[0] == 1

    def low(*at):
        return jnp.where(low_is_odd, odd[at], even[at])

    def high(*at):
        return jnp.where(low_is_odd, even[at], odd[at])

    return low, high


def pack_x2(z_even, z_odd, y_even, y_odd, fx, even, odd):
    y_low, y_high = sides("gy", y_even, y_odd)
    for out, up in zip((even, odd), ways("gx")):
        near, far, first = 6 * up, 2 + 2 * up, 4 * up
        for side, rows in ((0, y_low), (1, y_high)):
            four = slice(4, 8) if side == 0 else slice(0, 4)
            two = slice(6, 8) if side == 0 else slice(0, 2)
            for j in range(2):
                for i in range(4):
                    out[i * 2 + side, 4 * j : 4 * j + 4] = rows(i * 8 + near + j, four)
                    at = 4 * (i % 2) + 2 * j
                    out[8 + i // 2 * 2 + side, at : at + 2] = rows(i * 8 + far + j, two)
                at = 4 * j + (2 if side == 0 else 0)
                for a in range(3):
                    to = 4 * (a % 2) + 2 * j
                    out[12 + a // 2 * 2 + side, to : to + 2] = rows(32 + a * 4 + 3 * up, slice(at, at + 2))
                to = 4 * side + 2 * j
                out[32, to : to + 2] = rows(44 + 3 * up, slice(at, at + 2))
        for j in range(4):
            halo = z_even[first + j] + z_odd[first + j]
            for t in range(4):
                out[16 + j * 4 + t] = halo[8 * t : 8 * t + 8]
        out[33] = padded(fx[...])


FULL, OWN = (8, 24, 40), (16, 32)
SCALE = TIME_STEP / 12.0


def chunk(rows):
    lane = lanes_of(rows)
    return lane, lane % 32, lax.broadcasted_iota(jnp.int32, (rows, 128), 0)


def roll(value, by):
    return pltpu.roll(value, by % 128, 1)


def slabs(state, wind, zm, edge, edge_wind, x, r, rows, winds):
    lane, in_group, _ = chunk(rows)
    halo = zm[x, r : r + rows]
    tile = halo
    for i in range(4):
        q = state[i, x, r : r + rows]
        tile = jnp.where(within(lane, 32 * i + 8, 8), roll(q, 32 * i + 8), tile)
        tile = jnp.where(within(lane, 32 * i + 16, 8), roll(q, 32 * i + 24), tile)
    edge[x, r : r + rows] = tile
    if winds:
        halo = halo * SCALE
        packed = jnp.where(in_group < 8, roll(halo, -8), roll(halo, 8))
        for a in range(3):
            q = wind[a, x, r : r + rows]
            packed = jnp.where(within(lane, 32 * a + 8, 8), roll(q, 32 * a + 8), packed)
            packed = jnp.where(within(lane, 32 * a + 16, 8), roll(q, 32 * a + 24), packed)
        for a in range(3):
            one = jnp.where(within(lane, 32 * a, 32), packed, 0.0)
            one = one + roll(one, 32)
            edge_wind[a, x, r : r + rows] = one + roll(one, 64)


def terms(plus, minus, plus2, minus2):
    return 8.0 * (plus - minus) - (plus2 - minus2), plus + minus


def half(base, q, t):
    return 0.5 * (base + q + t)


class Stencil:
    def __init__(self, d, c, wind, edge_wind):
        self.wind, self.edge_wind = wind, edge_wind
        self.dd = [d[i] * TIME_STEP for i in range(4)]
        self.cc = [[c[i, w] * TIME_STEP for w in range(4)] for i in range(4)]
        gx, gy, self.gz = (lax.axis_index(n) for n in ("gx", "gy", "gz"))
        last_x, last_y, self.last_z = (lax.axis_size(n) - 1 for n in ("gx", "gy", "gz"))
        self.x_first, self.x_end = jnp.where(gx == 0, LOW, 0), jnp.where(gx == last_x, HIGH, PLANES)
        self.y_first, self.y_end = jnp.where(gy == 0, 16, 0), jnp.where(gy == last_y, 48, ROWS)

    def tendencies(self, src, slab, x, r, rows):
        dd, cc, wind = self.dd, self.cc, self.wind
        lane, in_group, _ = chunk(rows)
        at = slice(r, r + rows)
        u = [wind[a, x, at] for a in range(3)]
        q = [src[i, x, at] for i in range(4)]
        s = slab[x, at]
        s = jnp.where(in_group >= 24, s, roll(s, 16))
        results = []
        for i in range(4):
            ends = roll(s, -24 - 32 * i)
            gz_, lz = terms(
                roll(jnp.where(lane == 0, ends, q[i]), -1),
                roll(jnp.where(lane == 127, ends, q[i]), 1),
                roll(jnp.where(lane < 2, ends, q[i]), -2),
                roll(jnp.where(lane >= 126, ends, q[i]), 2),
            )
            gx_, lx = terms(src[i, x + 1, at], src[i, x - 1, at], src[i, x + 2, at], src[i, x - 2, at])
            gy_, ly = terms(*(src[i, x, r + o : r + o + rows] for o in (1, -1, 2, -2)))
            mix = cc[i][0] * q[0] + cc[i][1] * q[1] + (cc[i][2] * q[2] + cc[i][3] * q[3])
            moved = u[0] * gx_ + u[1] * gy_ + u[2] * gz_
            results.append(dd[i] * (lx + ly + lz) - moved + q[i] * (mix - 6.0 * dd[i]))
        return q, results

    def slab_tendency(self, slab, x, r, rows):
        dd, cc, edge_wind = self.dd, self.cc, self.edge_wind
        lane, _, _ = chunk(rows)
        group = lane // 32
        at = slice(r, r + rows)

        def by_group(values):
            return jnp.where(group < 2, jnp.where(group == 0, values[0], values[1]),
                             jnp.where(group == 2, values[2], values[3]))

        q = slab[x, at]
        gz_, lz = terms(roll(q, -1), roll(q, 1), roll(q, -2), roll(q, 2))
        gx_, lx = terms(slab[x + 1, at], slab[x - 1, at], slab[x + 2, at], slab[x - 2, at])
        gy_, ly = terms(*(slab[x, r + o : r + o + rows] for o in (1, -1, 2, -2)))
        mix = -6.0 * by_group(dd)
        for k in range(4):
            mix = mix + by_group([cc[i][(i - k) % 4] for i in range(4)]) * roll(q, 32 * k)
        moved = edge_wind[0, x, at] * gx_ + edge_wind[1, x, at] * gy_ + edge_wind[2, x, at] * gz_
        return q, by_group(dd) * (lx + ly + lz) - moved + q * mix

    def inside(self, x, r, rows):
        _, in_group, row = chunk(rows)
        first = jnp.where((x >= self.x_first) & (x < self.x_end), self.y_first, ROWS)
        ok = (row + r >= first) & (row + r < self.y_end)
        z_ok = ((in_group >= 8) | (self.gz != 0)) & ((in_group < 24) | (self.gz != self.last_z))
        return ok, z_ok

    def stage(self, x, rows_at, slab_rows, src, slab, dst, slab_dst, mean):
        for r in rows_at:
            at = slice(r, r + 16)
            ok, _ = self.inside(x, r, 16)
            q, t = self.tendencies(src, slab, x, r, 16)
            for i in range(4):
                new = half(dst[i, x, at], q[i], t[i]) if mean else q[i] + t[i]
                dst[i, x, at] = jnp.where(ok, new, 0.0)
        for r in slab_rows:
            at = slice(r, r + 16)
            ok, z_ok = self.inside(x, r, 16)
            q, t = self.slab_tendency(slab, x, r, 16)
            new = half(slab_dst[x, at], q, t) if mean else q + t
            slab_dst[x, at] = jnp.where(ok & z_ok, new, 0.0)


def fetched(d_in, c_in, d, c, arrived):
    pairs = ((d_in, d), (c_in, c))
    copies = [pltpu.make_async_copy(a, b, arrived.at[n]) for n, (a, b) in enumerate(pairs)]
    for copy in copies:
        copy.start()
    return copies


def prepare(
    d_in, c_in, f, v, z_even, z_odd, y_even, y_odd, fz, fy,
    state, section, edge, edge2, wind, edge_wind, zm, rhs, fye, d, c, arrived,
):
    copies = fetched(d_in, c_in, d, c, arrived)
    y_low, y_high = sides("gy", y_even, y_odd)
    for i in range(4):
        for x in range(8):
            state[i, 8 + x, 16:48] = f[i, x]
            state[i, 8 + x, 8:16] = y_low(i * 8 + x)
            state[i, 8 + x, 48:56] = y_high(i * 8 + x)
    for x in range(8):
        half_tile = slice(4 * (x % 2), 4 * (x % 2) + 4)
        for a in range(3):
            wind[a, 8 + x, 16:48] = v[a, x] * SCALE
            wind[a, 8 + x, 12:16] = y_low(32 + a * 4 + x // 2, half_tile) * SCALE
            wind[a, 8 + x, 48:52] = y_high(32 + a * 4 + x // 2, half_tile) * SCALE
        zm[8 + x, 16:48] = z_even[x] + z_odd[x]
        zm[8 + x, 12:16] = y_low(44 + x // 2, half_tile)
        zm[8 + x, 48:52] = y_high(44 + x // 2, half_tile)
    lane = lanes_of(32)
    outer = jnp.where((lane >= 126) | (lane < 2), roll(zm[8, 16:48], 16), 0.0)
    rhs[...] = jnp.zeros((4, 128, 256), F32)
    for i in range(4):
        for k in range(4):
            at = slice(32 * k + 8 * i, 32 * k + 8 * i + 8)
            rhs[i, at, 0:128] = fz[8 * k : 8 * k + 8]
            rhs[i, at, 128:256] = outer[8 * k : 8 * k + 8]
    fye[0:8] = y_low(48, slice(0, 8), slice(0, 32))
    fye[8:40] = fy[...]
    fye[40:48] = y_high(48, slice(0, 8), slice(0, 32))

    @pl.loop(8, 16)
    def _(x):
        for r in FULL:
            slabs(state, wind, zm, edge, edge_wind, x, r, 16, True)

    for copy in copies:
        copy.wait()
    stencil = Stencil(d, c, wind, edge_wind)

    @pl.loop(10, 14)
    def _(x):
        stencil.stage(x, FULL, FULL, state, edge, section, edge2, False)


def advance(d_in, c_in, x_even, x_odd, e_even, e_odd, fy, rhs, fye, *refs):
    out, state, section, edge, edge2, wind, edge_wind, zm, final, faces, mixed = refs[7:18]
    d, c, arrived = refs[18:]
    copies = fetched(d_in, c_in, d, c, arrived)
    scale, full, own = SCALE, FULL, OWN
    even_up, odd_up = ways("gx")
    for halo, above in ((x_even, even_up), (x_odd, odd_up)):
        for j in range(6):
            for i in range(4):
                state[i, 2 + 14 * above + j, 16:48] = halo[i * 6 + j]
        for j in range(4):
            for a in range(3):
                wind[a, 4 + 12 * above + j, 16:48] = halo[24 + a * 4 + j] * scale
    for e, above in ((e_even, even_up), (e_odd, odd_up)):
        near, far, first = 6 + 10 * above, 4 + 14 * above, 4 + 12 * above
        for j in range(2):
            for i in range(4):
                state[i, near + j, 12:16] = e[i * 2, 4 * j : 4 * j + 4]
                state[i, near + j, 48:52] = e[i * 2 + 1, 4 * j : 4 * j + 4]
                at = 4 * (i % 2) + 2 * j
                state[i, far + j, 14:16] = e[8 + i // 2 * 2, at : at + 2]
                state[i, far + j, 48:50] = e[9 + i // 2 * 2, at : at + 2]
            for a in range(3):
                at = 4 * (a % 2) + 2 * j
                wind[a, near + j, 14:16] = e[12 + a // 2 * 2, at : at + 2] * scale
                wind[a, near + j, 48:50] = e[13 + a // 2 * 2, at : at + 2] * scale
            zm[near + j, 14:16] = e[32, 2 * j : 2 * j + 2]
            zm[near + j, 48:50] = e[32, 4 + 2 * j : 6 + 2 * j]
        for j in range(4):
            for t in range(4):
                zm[first + j, 16 + 8 * t : 24 + 8 * t] = e[16 + j * 4 + t]

    @pl.loop(0, 4)
    def _(j):
        x = jnp.where(j < 2, 6 + j, 14 + j)
        for r in full:
            slabs(state, wind, zm, edge, edge_wind, x, r, 16, True)
        x = jnp.where(j < 2, 4 + j, 16 + j)
        for r in own:
            slabs(state, wind, zm, edge, edge_wind, x, r, 16, False)

    for copy in copies:
        copy.wait()
    stencil = Stencil(d, c, wind, edge_wind)
    dd, cc, stage = stencil.dd, stencil.cc, stencil.stage

    @pl.loop(0, 8)
    def _(j):
        x = jnp.where(j < 4, 6 + j, 10 + j)
        stage(x, full, full, state, edge, section, edge2, False)

    @pl.loop(0, 4, unroll=2)
    def _(j):
        stage(jnp.where(j < 2, 4 + j, 16 + j), own, (), state, edge, section, edge2, False)

    @pl.loop(8, 16)
    def _(x):
        stage(x, full, own, section, edge2, state, edge, True)

    @pl.loop(0, 4, unroll=2)
    def _(j):
        stage(jnp.where(j < 2, 6 + j, 14 + j), own, (), section, edge2, state, edge, True)

    @pl.loop(8, 16, unroll=2)
    def _(x):
        stage(x, own, (), state, edge, section, edge2, False)

    for i in range(4):
        for x in (6, 7, 16, 17):
            section[i, x, 16:48] = jnp.zeros((32, 128), F32)
        for x in range(8):
            section[i, 8 + x, 0:16] = jnp.zeros((16, 128), F32)
            section[i, 8 + x, 48:64] = jnp.zeros((16, 128), F32)

    @pl.loop(0, 8, unroll=2)
    def _(x):
        base = pl.multiple_of(x * 48, 16)
        for r in own:
            lane, _, _ = chunk(16)
            at = slice(r, r + 16)
            u = [wind[a, 8 + x, at] for a in range(3)]
            u_out = roll(zm[8 + x, at], 48) * (0.5 * scale)
            q = [section[i, 8 + x, at] for i in range(4)]
            for i in range(4):
                plus, minus, plus2, minus2 = (roll(q[i], o) for o in (-1, 1, -2, 2))
                src = section
                gz_, lz = terms(
                    jnp.where(lane == 127, 0.0, plus),
                    jnp.where(lane == 0, 0.0, minus),
                    jnp.where(lane >= 126, 0.0, plus2),
                    jnp.where(lane < 2, 0.0, minus2),
                )
                gx_, lx = terms(*(src[i, 8 + x + o, at] for o in (1, -1, 2, -2)))
                gy_, ly = terms(*(src[i, 8 + x, r + o : r + o + 16] for o in (1, -1, 2, -2)))
                mix = cc[i][0] * q[0] + cc[i][1] * q[1] + (cc[i][2] * q[2] + cc[i][3] * q[3])
                moved = u[0] * gx_ + u[1] * gy_ + u[2] * gz_
                t = dd[i] * (lx + ly + lz) - moved + q[i] * (mix - 6.0 * dd[i])
                row = pl.multiple_of(base + (r - 8), 8)
                final[i, pl.ds(row, 16), 0:128] = half(state[i, 8 + x, at], q[i], t)
                one = jnp.where(lane == 127, plus, jnp.where(lane == 0, -minus, 0.0))
                two = jnp.where(lane >= 126, plus2, jnp.where(lane < 2, -minus2, 0.0))
                spread = jnp.where(lane == 127, plus, jnp.where(lane == 0, minus, 0.0))
                beyond = (0.5 * dd[i]) * spread - u_out * (8.0 * one - two)
                final[i, pl.ds(row, 16), 128:256] = jnp.where((lane >= 126) | (lane < 2), beyond, 0.0)
        row8 = lax.broadcasted_iota(jnp.int32, (8, 128), 0)
        for r, to, kept in ((8, 0, row8 >= 6), (48, 40, row8 < 2)):
            u_y = wind[1, 8 + x, r : r + 8]
            for i in range(4):
                gy_, ly = terms(*(section[i, 8 + x, r + o : r + o + 8] for o in (1, -1, 2, -2)))
                row = pl.multiple_of(base + to, 8)
                face = jnp.where(kept, 0.5 * (dd[i] * ly - u_y * gy_), 0.0)
                final[i, pl.ds(row, 8), 0:128] = face
                final[i, pl.ds(row, 8), 128:256] = jnp.zeros((8, 128), F32)

    for i in range(4):
        first, second = section[i, 8, 16:48], section[i, 9, 16:48]
        last, before = section[i, 15, 16:48], section[i, 14, 16:48]
        u = [wind[0, x, 16:48] for x in (6, 7, 16, 17)]
        faces[i, 0:32] = 0.5 * (u[0] * first)
        faces[i, 32:64] = 0.5 * (dd[i] * first - u[1] * (8.0 * first - second))
        faces[i, 64:96] = 0.5 * (dd[i] * last + u[2] * (8.0 * last - before))
        faces[i, 96:128] = -0.5 * (u[3] * last)

    total = dot(final[0], rhs[0], 1, 1)
    total_faces = dot(faces[0], rhs[0, :, 0:128], 1, 1)
    for i in range(1, 4):
        total = total + dot(final[i], rhs[i], 1, 1)
        total_faces = total_faces + dot(faces[i], rhs[i, :, 0:128], 1, 1)
    for x in range(8):
        mixed[x * 32 : x * 32 + 32] = dot(fye[...], total[x * 48 : x * 48 + 48], 0, 0)
    for x in range(4):
        mixed[256 + x * 32 : 288 + x * 32] = dot(fy[...], total_faces[x * 32 : x * 32 + 32], 0, 0)
    for planes, first in ((8, 0), (4, 8)):
        lane = lanes_of(planes)
        for j in range(8):
            rows = [pl.ds(32 * first + 4 * j + b, planes, stride=32) for b in range(4)]
            tiles = [mixed[at, :] for at in rows]
            for k in range(4):
                tile = jnp.zeros((planes, 128), F32)
                for b in range(4):
                    tile = jnp.where(within(lane, 32 * b, 32), roll(tiles[b], 32 * (b - k)), tile)
                for t in range(planes // 4):
                    at = 32 * first + 128 * t
                    out[j * 4 + k, :, at : at + 128] = tile[4 * t : 4 * t + 4]


def contract_x(parts, fx, e_even, e_odd, out):
    total = parts[0]
    for p in range(1, parts.shape[0]):
        total = total + parts[p]
    e_low, e_high = sides("gx", e_even, e_odd)
    outer = [e_low(33, slice(6, 8), slice(0, 32)), e_high(33, slice(0, 2), slice(0, 32))]
    outer = jnp.concatenate(outer, axis=0)
    result = dot(fx[0:4], total[:, 0:128], 0, 0) + dot(fx[4:8], total[:, 128:256], 0, 0)
    out[...] = result + dot(outer, total[:, 256:384], 0, 0)


def local(fields, velocity, diffusivity, coupling, factor_x, factor_y, factor_z):
    def swapped(axis, even, odd):
        last = lax.axis_size(axis) - 1
        pairs = [[(i, i + 1) for i in range(first, last, 2)] for first in (0, 1)]
        even_pairs, odd_pairs = ([*p, *((b, a) for a, b in p)] for p in pairs)
        even = lax.ppermute(even, axis, even_pairs)
        return even, lax.ppermute(odd, axis, odd_pairs)

    inputs = (fields, velocity, factor_z.T, factor_y, factor_x)
    x_even, x_odd, z_even, z_odd, fields, velocity, fz, fy, fx = call(
        pack_xz,
        [f32(36, 32, 128)] * 2 + [f32(8, 32, 128)] * 2 + [f32(*a.shape) for a in inputs],
        [hbm()] * 5,
        scratch=[pltpu.SemaphoreType.DMA((5,))],
    )(*in_hbm(*inputs))
    z_even, z_odd = swapped("gz", z_even, z_odd)
    y_even, y_odd = call(pack_y, [f32(49, 8, 128)] * 2, [vmem()] * 5)(
        fields, velocity, fy, z_even, z_odd
    )
    y_even, y_odd = swapped("gy", y_even, y_odd)
    x_even, x_odd = swapped("gx", x_even, x_odd)
    e_even, e_odd = call(pack_x2, [f32(34, 8, 128)] * 2, [vmem()] * 5)(
        z_even, z_odd, y_even, y_odd, fx
    )
    e_even, e_odd = swapped("gx", e_even, e_odd)

    def tiles(*lead):
        return f32(*lead, ROWS, 128)

    gx = lax.axis_size("gx")
    buffers = [
        tiles(4, PLANES), tiles(4, PLANES), tiles(PLANES), tiles(PLANES),
        tiles(3, PLANES), tiles(3, PLANES), tiles(PLANES),
    ]
    scalars = [pltpu.SMEM((4,), F32), pltpu.SMEM((4, 4), F32), pltpu.SemaphoreType.DMA((2,))]
    diffusivity, coupling = in_hbm(diffusivity, coupling)
    *filled, rhs, fye = call(
        prepare,
        [*buffers, f32(4, 128, 256), f32(48, 32)],
        [hbm()] * 2 + [vmem()] * 8,
        scratch=scalars,
        work=3000000,
    )(diffusivity, coupling, fields, velocity, z_even, z_odd, y_even, y_odd, fz, fy)
    parts, *_ = call(
        advance,
        [f32(32, 4, 384), *buffers],
        [hbm()] * 2 + [vmem()] * 14,
        scratch=[
            pltpu.VMEM((4, 384, 256), F32), pltpu.VMEM((4, 128, 128), F32),
            pltpu.VMEM((384, 128), F32), *scalars,
        ],
        work=10000000,
        aliases={9 + n: 1 + n for n in range(7)},
    )(diffusivity, coupling, x_even, x_odd, e_even, e_odd, fy, rhs, fye, *filled)
    parts = lax.all_to_all(parts, ("gy", "gz"), 0, 0, tiled=True)
    slices = call(contract_x, f32(32, 128), [vmem()] * 4)(
        parts, fx, e_even, e_odd
    )
    slices = lax.all_to_all(slices, "gx", 0, 0, tiled=True)
    core = jnp.sum(slices.reshape(gx, 32 // gx, 4, 4, 8), axis=0)
    return core.transpose(2, 0, 1, 3)


def solution(mesh):
    return jax.shard_map(
        local,
        mesh=mesh,
        in_specs=(
            P(None, "gx", "gy", "gz"),
            P(None, "gx", "gy", "gz"),
            P(),
            P(),
            P("gx", None),
            P("gy", None),
            P("gz", None),
        ),
        out_specs=P(None, "gx", "gy", "gz"),
        check_vma=False,
    )
```

```python
import jax
import jax.numpy as jnp
from jax import lax
from jax.experimental import pallas as pl
from jax.experimental.pallas import tpu as pltpu
from jax.sharding import PartitionSpec as P


TIME_STEP = 0.2
F32 = jnp.float32
PLANES, ROWS = 24, 64
LOW, HIGH = 8, 16


def vmem():
    return pl.BlockSpec(memory_space=pltpu.VMEM)


def hbm():
    return pl.BlockSpec(memory_space=pltpu.HBM)


def in_hbm(*arrays):
    return [pltpu.with_memory_space_constraint(a, pltpu.HBM) for a in arrays]


def f32(*shape):
    return jax.ShapeDtypeStruct(shape, F32)


def call(kernel, out_shape, in_specs, scratch=(), work=1000000, mib=8, aliases=None):
    many = isinstance(out_shape, (list, tuple))
    return pl.pallas_call(
        kernel,
        out_shape=out_shape,
        in_specs=in_specs,
        out_specs=[vmem() for _ in out_shape] if many else vmem(),
        scratch_shapes=list(scratch),
        input_output_aliases=aliases or {},
        compiler_params=pltpu.CompilerParams(vmem_limit_bytes=mib << 20),
        cost_estimate=pl.CostEstimate(flops=work, bytes_accessed=work, transcendentals=0),
    )


def lanes_of(rows):
    return lax.broadcasted_iota(jnp.int32, (rows, 128), 1)


def within(lane, first, size):
    return (lane >= first) & (lane < first + size)


def halves(a):
    high = a.astype(jnp.bfloat16)
    return high, (a - high.astype(F32)).astype(jnp.bfloat16)


def dot(a, b, a_dim, b_dim):
    def product(p, q):
        return lax.dot_general(p, q, (((a_dim,), (b_dim,)), ((), ())), preferred_element_type=F32)

    (a_high, a_low), (b_high, b_low) = halves(a), halves(b)
    both = product(a_high, jnp.concatenate([b_high, b_low], axis=1 - b_dim))
    return both[:, 0:128] + (both[:, 128:256] + product(a_low, b_high))


def padded(rows):
    return jnp.concatenate([rows, jnp.zeros((rows.shape[0], 128 - rows.shape[1]), F32)], axis=1)


def ways(axis):
    odd = lax.rem(lax.axis_index(axis), 2)
    return 1 - odd, odd


def pack_xz(f_in, v_in, fz_in, fy_in, fx_in, x_even, x_odd, z_even, z_odd, f, v, fz, fy, fx, arrived):
    pairs = ((f_in, f), (v_in, v), (fz_in, fz), (fy_in, fy), (fx_in, fx))
    copies = [pltpu.make_async_copy(a, b, arrived.at[n]) for n, (a, b) in enumerate(pairs)]
    for copy in copies:
        copy.start()
    for copy in copies:
        copy.wait()
    lane = lanes_of(32)
    for out, up in zip((x_even, x_odd), ways("gx")):
        for j in range(6):
            for i in range(4):
                out[i * 6 + j] = f[i, 2 * up + j]
        for j in range(4):
            for a in range(3):
                out[24 + a * 4 + j] = v[a, 4 * up + j]
    even_up, _ = ways("gz")

    def plane_edges(x, carry):
        up = jnp.zeros((32, 128), F32)
        down = jnp.zeros((32, 128), F32)
        for i in range(4):
            plane = f[i, x]
            up = jnp.where(within(lane, 32 * i, 8), pltpu.roll(plane, (32 * i + 8) % 128, 1), up)
            down = jnp.where(within(lane, 32 * i + 24, 8), pltpu.roll(plane, 32 * i + 24, 1), down)
        for a in range(4):
            plane = pltpu.roll(v[a, x] if a < 3 else fz[...], 32 * a + 16, 1)
            up = jnp.where(within(lane, 32 * a + 8, 8), plane, up)
            down = jnp.where(within(lane, 32 * a + 16, 8), plane, down)
        z_even[x] = jnp.where(even_up == 1, up, down)
        z_odd[x] = jnp.where(even_up == 1, down, up)
        return carry

    lax.fori_loop(0, 8, plane_edges, 0)


def pack_y(f, v, fy, z_even, z_odd, y_even, y_odd):
    for out, up in zip((y_even, y_odd), ways("gy")):

        def edge_rows(high, low):
            return jnp.where(up == 1, high, low)

        for x in range(8):
            half = slice(4 * (x % 2), 4 * (x % 2) + 4)
            for i in range(4):
                out[i * 8 + x] = edge_rows(f[i, x, 24:32], f[i, x, 0:8])
            for a in range(3):
                out[32 + a * 4 + x // 2, half] = edge_rows(v[a, x, 28:32], v[a, x, 0:4])
            out[44 + x // 2, half] = edge_rows(
                z_even[x, 28:32] + z_odd[x, 28:32], z_even[x, 0:4] + z_odd[x, 0:4]
            )
        out[48] = padded(edge_rows(fy[24:32], fy[0:8]))


def sides(axis, even, odd):
    low_is_odd = ways(axis)[0] == 1

    def low(*at):
        return jnp.where(low_is_odd, odd[at], even[at])

    def high(*at):
        return jnp.where(low_is_odd, even[at], odd[at])

    return low, high


def pack_x2(z_even, z_odd, y_even, y_odd, fx, even, odd):
    y_low, y_high = sides("gy", y_even, y_odd)
    for out, up in zip((even, odd), ways("gx")):
        near, far, first = 6 * up, 2 + 2 * up, 4 * up
        for side, rows in ((0, y_low), (1, y_high)):
            four = slice(4, 8) if side == 0 else slice(0, 4)
            two = slice(6, 8) if side == 0 else slice(0, 2)
            for j in range(2):
                for i in range(4):
                    out[i * 2 + side, 4 * j : 4 * j + 4] = rows(i * 8 + near + j, four)
                    at = 4 * (i % 2) + 2 * j
                    out[8 + i // 2 * 2 + side, at : at + 2] = rows(i * 8 + far + j, two)
                at = 4 * j + (2 if side == 0 else 0)
                for a in range(3):
                    to = 4 * (a % 2) + 2 * j
                    out[12 + a // 2 * 2 + side, to : to + 2] = rows(32 + a * 4 + 3 * up, slice(at, at + 2))
                to = 4 * side + 2 * j
                out[32, to : to + 2] = rows(44 + 3 * up, slice(at, at + 2))
        for j in range(4):
            halo = z_even[first + j] + z_odd[first + j]
            for t in range(4):
                out[16 + j * 4 + t] = halo[8 * t : 8 * t + 8]
        out[33] = padded(fx[...])


FULL, OWN = (8, 24, 40), (16, 32)
SCALE = TIME_STEP / 12.0


def chunk(rows):
    lane = lanes_of(rows)
    return lane, lane % 32, lax.broadcasted_iota(jnp.int32, (rows, 128), 0)


def roll(value, by):
    return pltpu.roll(value, by % 128, 1)


def slabs(state, wind, zm, edge, edge_wind, x, r, rows, winds):
    lane, in_group, _ = chunk(rows)
    halo = zm[x, r : r + rows]
    tile = halo
    for i in range(4):
        q = state[i, x, r : r + rows]
        tile = jnp.where(within(lane, 32 * i + 8, 8), roll(q, 32 * i + 8), tile)
        tile = jnp.where(within(lane, 32 * i + 16, 8), roll(q, 32 * i + 24), tile)
    edge[x, r : r + rows] = tile
    if winds:
        halo = halo * SCALE
        packed = jnp.where(in_group < 8, roll(halo, -8), roll(halo, 8))
        for a in range(3):
            q = wind[a, x, r : r + rows]
            packed = jnp.where(within(lane, 32 * a + 8, 8), roll(q, 32 * a + 8), packed)
            packed = jnp.where(within(lane, 32 * a + 16, 8), roll(q, 32 * a + 24), packed)
        for a in range(3):
            one = jnp.where(within(lane, 32 * a, 32), packed, 0.0)
            one = one + roll(one, 32)
            edge_wind[a, x, r : r + rows] = one + roll(one, 64)


def terms(plus, minus, plus2, minus2):
    return 8.0 * (plus - minus) - (plus2 - minus2), plus + minus


def half(base, q, t):
    return 0.5 * (base + q + t)


class Stencil:
    def __init__(self, d, c, wind, edge_wind):
        self.wind, self.edge_wind = wind, edge_wind
        self.dd = [d[i] * TIME_STEP for i in range(4)]
        self.cc = [[c[i, w] * TIME_STEP for w in range(4)] for i in range(4)]
        gx, gy, self.gz = (lax.axis_index(n) for n in ("gx", "gy", "gz"))
        last_x, last_y, self.last_z = (lax.axis_size(n) - 1 for n in ("gx", "gy", "gz"))
        self.x_first, self.x_end = jnp.where(gx == 0, LOW, 0), jnp.where(gx == last_x, HIGH, PLANES)
        self.y_first, self.y_end = jnp.where(gy == 0, 16, 0), jnp.where(gy == last_y, 48, ROWS)

    def tendencies(self, src, slab, x, r, rows):
        dd, cc, wind = self.dd, self.cc, self.wind
        lane, in_group, _ = chunk(rows)
        at = slice(r, r + rows)
        u = [wind[a, x, at] for a in range(3)]
        q = [src[i, x, at] for i in range(4)]
        s = slab[x, at]
        s = jnp.where(in_group >= 24, s, roll(s, 16))
        results = []
        for i in range(4):
            ends = roll(s, -24 - 32 * i)
            gz_, lz = terms(
                roll(jnp.where(lane == 0, ends, q[i]), -1),
                roll(jnp.where(lane == 127, ends, q[i]), 1),
                roll(jnp.where(lane < 2, ends, q[i]), -2),
                roll(jnp.where(lane >= 126, ends, q[i]), 2),
            )
            gx_, lx = terms(src[i, x + 1, at], src[i, x - 1, at], src[i, x + 2, at], src[i, x - 2, at])
            gy_, ly = terms(*(src[i, x, r + o : r + o + rows] for o in (1, -1, 2, -2)))
            mix = cc[i][0] * q[0] + cc[i][1] * q[1] + (cc[i][2] * q[2] + cc[i][3] * q[3])
            moved = u[0] * gx_ + u[1] * gy_ + u[2] * gz_
            results.append(dd[i] * (lx + ly + lz) - moved + q[i] * (mix - 6.0 * dd[i]))
        return q, results

    def slab_tendency(self, slab, x, r, rows):
        dd, cc, edge_wind = self.dd, self.cc, self.edge_wind
        lane, _, _ = chunk(rows)
        group = lane // 32
        at = slice(r, r + rows)

        def by_group(values):
            return jnp.where(group < 2, jnp.where(group == 0, values[0], values[1]),
                             jnp.where(group == 2, values[2], values[3]))

        q = slab[x, at]
        gz_, lz = terms(roll(q, -1), roll(q, 1), roll(q, -2), roll(q, 2))
        gx_, lx = terms(slab[x + 1, at], slab[x - 1, at], slab[x + 2, at], slab[x - 2, at])
        gy_, ly = terms(*(slab[x, r + o : r + o + rows] for o in (1, -1, 2, -2)))
        mix = -6.0 * by_group(dd)
        for k in range(4):
            mix = mix + by_group([cc[i][(i - k) % 4] for i in range(4)]) * roll(q, 32 * k)
        moved = edge_wind[0, x, at] * gx_ + edge_wind[1, x, at] * gy_ + edge_wind[2, x, at] * gz_
        return q, by_group(dd) * (lx + ly + lz) - moved + q * mix

    def inside(self, x, r, rows):
        _, in_group, row = chunk(rows)
        first = jnp.where((x >= self.x_first) & (x < self.x_end), self.y_first, ROWS)
        ok = (row + r >= first) & (row + r < self.y_end)
        z_ok = ((in_group >= 8) | (self.gz != 0)) & ((in_group < 24) | (self.gz != self.last_z))
        return ok, z_ok

    def stage(self, x, rows_at, slab_rows, src, slab, dst, slab_dst, mean):
        for r in rows_at:
            at = slice(r, r + 16)
            ok, _ = self.inside(x, r, 16)
            q, t = self.tendencies(src, slab, x, r, 16)
            for i in range(4):
                new = half(dst[i, x, at], q[i], t[i]) if mean else q[i] + t[i]
                dst[i, x, at] = jnp.where(ok, new, 0.0)
        for r in slab_rows:
            at = slice(r, r + 16)
            ok, z_ok = self.inside(x, r, 16)
            q, t = self.slab_tendency(slab, x, r, 16)
            new = half(slab_dst[x, at], q, t) if mean else q + t
            slab_dst[x, at] = jnp.where(ok & z_ok, new, 0.0)


def fetched(d_in, c_in, d, c, arrived):
    pairs = ((d_in, d), (c_in, c))
    copies = [pltpu.make_async_copy(a, b, arrived.at[n]) for n, (a, b) in enumerate(pairs)]
    for copy in copies:
        copy.start()
    return copies


def prepare_own(
    d_in, c_in, f, v, z_even, z_odd, fz,
    state, section, edge, edge2, wind, edge_wind, zm, rhs, d, c, arrived,
):
    copies = fetched(d_in, c_in, d, c, arrived)
    for x in range(8):
        for i in range(4):
            state[i, 8 + x, 16:48] = f[i, x]
        for a in range(3):
            wind[a, 8 + x, 16:48] = v[a, x] * SCALE
        zm[8 + x, 16:48] = z_even[x] + z_odd[x]
    lane = lanes_of(32)
    outer = jnp.where((lane >= 126) | (lane < 2), roll(zm[8, 16:48], 16), 0.0)
    rhs[...] = jnp.zeros((4, 128, 256), F32)
    for i in range(4):
        for k in range(4):
            at = slice(32 * k + 8 * i, 32 * k + 8 * i + 8)
            rhs[i, at, 0:128] = fz[8 * k : 8 * k + 8]
            rhs[i, at, 128:256] = outer[8 * k : 8 * k + 8]

    @pl.loop(8, 16)
    def _(x):
        for r in OWN:
            slabs(state, wind, zm, edge, edge_wind, x, r, 16, True)

    for copy in copies:
        copy.wait()
    stencil = Stencil(d, c, wind, edge_wind)

    @pl.loop(10, 14)
    def _(x):
        stencil.stage(x, (24,), (24,), state, edge, section, edge2, False)


def prepare(d_in, c_in, y_even, y_odd, fy, *refs):
    state, section, edge, edge2, wind, edge_wind, zm, fye, d, c, arrived = refs[7:]
    copies = fetched(d_in, c_in, d, c, arrived)
    y_low, y_high = sides("gy", y_even, y_odd)
    for x in range(8):
        half_tile = slice(4 * (x % 2), 4 * (x % 2) + 4)
        for i in range(4):
            state[i, 8 + x, 8:16] = y_low(i * 8 + x)
            state[i, 8 + x, 48:56] = y_high(i * 8 + x)
        for a in range(3):
            wind[a, 8 + x, 12:16] = y_low(32 + a * 4 + x // 2, half_tile) * SCALE
            wind[a, 8 + x, 48:52] = y_high(32 + a * 4 + x // 2, half_tile) * SCALE
        zm[8 + x, 12:16] = y_low(44 + x // 2, half_tile)
        zm[8 + x, 48:52] = y_high(44 + x // 2, half_tile)
    fye[0:8] = y_low(48, slice(0, 8), slice(0, 32))
    fye[8:40] = fy[...]
    fye[40:48] = y_high(48, slice(0, 8), slice(0, 32))

    @pl.loop(8, 16)
    def _(x):
        for r in (8, 48):
            slabs(state, wind, zm, edge, edge_wind, x, r, 8, True)

    for copy in copies:
        copy.wait()
    stencil = Stencil(d, c, wind, edge_wind)

    @pl.loop(10, 14)
    def _(x):
        stencil.stage(x, (8, 40), (8, 40), state, edge, section, edge2, False)


def advance(d_in, c_in, x_even, x_odd, e_even, e_odd, fy, rhs, fye, *refs):
    out, state, section, edge, edge2, wind, edge_wind, zm, final, faces, mixed = refs[7:18]
    d, c, arrived = refs[18:]
    copies = fetched(d_in, c_in, d, c, arrived)
    scale, full, own = SCALE, FULL, OWN
    even_up, odd_up = ways("gx")
    for halo, above in ((x_even, even_up), (x_odd, odd_up)):
        for j in range(6):
            for i in range(4):
                state[i, 2 + 14 * above + j, 16:48] = halo[i * 6 + j]
        for j in range(4):
            for a in range(3):
                wind[a, 4 + 12 * above + j, 16:48] = halo[24 + a * 4 + j] * scale
    for e, above in ((e_even, even_up), (e_odd, odd_up)):
        near, far, first = 6 + 10 * above, 4 + 14 * above, 4 + 12 * above
        for j in range(2):
            for i in range(4):
                state[i, near + j, 12:16] = e[i * 2, 4 * j : 4 * j + 4]
                state[i, near + j, 48:52] = e[i * 2 + 1, 4 * j : 4 * j + 4]
                at = 4 * (i % 2) + 2 * j
                state[i, far + j, 14:16] = e[8 + i // 2 * 2, at : at + 2]
                state[i, far + j, 48:50] = e[9 + i // 2 * 2, at : at + 2]
            for a in range(3):
                at = 4 * (a % 2) + 2 * j
                wind[a, near + j, 14:16] = e[12 + a // 2 * 2, at : at + 2] * scale
                wind[a, near + j, 48:50] = e[13 + a // 2 * 2, at : at + 2] * scale
            zm[near + j, 14:16] = e[32, 2 * j : 2 * j + 2]
            zm[near + j, 48:50] = e[32, 4 + 2 * j : 6 + 2 * j]
        for j in range(4):
            for t in range(4):
                zm[first + j, 16 + 8 * t : 24 + 8 * t] = e[16 + j * 4 + t]

    @pl.loop(0, 4)
    def _(j):
        x = jnp.where(j < 2, 6 + j, 14 + j)
        for r in full:
            slabs(state, wind, zm, edge, edge_wind, x, r, 16, True)
        x = jnp.where(j < 2, 4 + j, 16 + j)
        for r in own:
            slabs(state, wind, zm, edge, edge_wind, x, r, 16, False)

    for copy in copies:
        copy.wait()
    stencil = Stencil(d, c, wind, edge_wind)
    dd, cc, stage = stencil.dd, stencil.cc, stencil.stage

    @pl.loop(0, 8)
    def _(j):
        x = jnp.where(j < 4, 6 + j, 10 + j)
        stage(x, full, full, state, edge, section, edge2, False)

    @pl.loop(0, 4, unroll=2)
    def _(j):
        stage(jnp.where(j < 2, 4 + j, 16 + j), own, (), state, edge, section, edge2, False)

    @pl.loop(8, 16)
    def _(x):
        stage(x, full, own, section, edge2, state, edge, True)

    @pl.loop(0, 4, unroll=2)
    def _(j):
        stage(jnp.where(j < 2, 6 + j, 14 + j), own, (), section, edge2, state, edge, True)

    @pl.loop(8, 16, unroll=2)
    def _(x):
        stage(x, own, (), state, edge, section, edge2, False)

    for i in range(4):
        for x in (6, 7, 16, 17):
            section[i, x, 16:48] = jnp.zeros((32, 128), F32)
        for x in range(8):
            section[i, 8 + x, 0:16] = jnp.zeros((16, 128), F32)
            section[i, 8 + x, 48:64] = jnp.zeros((16, 128), F32)

    @pl.loop(0, 8, unroll=2)
    def _(x):
        base = pl.multiple_of(x * 48, 16)
        for r in own:
            lane, _, _ = chunk(16)
            at = slice(r, r + 16)
            u = [wind[a, 8 + x, at] for a in range(3)]
            u_out = roll(zm[8 + x, at], 48) * (0.5 * scale)
            q = [section[i, 8 + x, at] for i in range(4)]
            for i in range(4):
                plus, minus, plus2, minus2 = (roll(q[i], o) for o in (-1, 1, -2, 2))
                src = section
                gz_, lz = terms(
                    jnp.where(lane == 127, 0.0, plus),
                    jnp.where(lane == 0, 0.0, minus),
                    jnp.where(lane >= 126, 0.0, plus2),
                    jnp.where(lane < 2, 0.0, minus2),
                )
                gx_, lx = terms(*(src[i, 8 + x + o, at] for o in (1, -1, 2, -2)))
                gy_, ly = terms(*(src[i, 8 + x, r + o : r + o + 16] for o in (1, -1, 2, -2)))
                mix = cc[i][0] * q[0] + cc[i][1] * q[1] + (cc[i][2] * q[2] + cc[i][3] * q[3])
                moved = u[0] * gx_ + u[1] * gy_ + u[2] * gz_
                t = dd[i] * (lx + ly + lz) - moved + q[i] * (mix - 6.0 * dd[i])
                row = pl.multiple_of(base + (r - 8), 8)
                final[i, pl.ds(row, 16), 0:128] = half(state[i, 8 + x, at], q[i], t)
                one = jnp.where(lane == 127, plus, jnp.where(lane == 0, -minus, 0.0))
                two = jnp.where(lane >= 126, plus2, jnp.where(lane < 2, -minus2, 0.0))
                spread = jnp.where(lane == 127, plus, jnp.where(lane == 0, minus, 0.0))
                beyond = (0.5 * dd[i]) * spread - u_out * (8.0 * one - two)
                final[i, pl.ds(row, 16), 128:256] = jnp.where((lane >= 126) | (lane < 2), beyond, 0.0)
        row8 = lax.broadcasted_iota(jnp.int32, (8, 128), 0)
        for r, to, kept in ((8, 0, row8 >= 6), (48, 40, row8 < 2)):
            u_y = wind[1, 8 + x, r : r + 8]
            for i in range(4):
                gy_, ly = terms(*(section[i, 8 + x, r + o : r + o + 8] for o in (1, -1, 2, -2)))
                row = pl.multiple_of(base + to, 8)
                face = jnp.where(kept, 0.5 * (dd[i] * ly - u_y * gy_), 0.0)
                final[i, pl.ds(row, 8), 0:128] = face
                final[i, pl.ds(row, 8), 128:256] = jnp.zeros((8, 128), F32)

    for i in range(4):
        first, second = section[i, 8, 16:48], section[i, 9, 16:48]
        last, before = section[i, 15, 16:48], section[i, 14, 16:48]
        u = [wind[0, x, 16:48] for x in (6, 7, 16, 17)]
        faces[i, 0:32] = 0.5 * (u[0] * first)
        faces[i, 32:64] = 0.5 * (dd[i] * first - u[1] * (8.0 * first - second))
        faces[i, 64:96] = 0.5 * (dd[i] * last + u[2] * (8.0 * last - before))
        faces[i, 96:128] = -0.5 * (u[3] * last)

    total = dot(final[0], rhs[0], 1, 1)
    total_faces = dot(faces[0], rhs[0, :, 0:128], 1, 1)
    for i in range(1, 4):
        total = total + dot(final[i], rhs[i], 1, 1)
        total_faces = total_faces + dot(faces[i], rhs[i, :, 0:128], 1, 1)
    for x in range(8):
        mixed[x * 32 : x * 32 + 32] = dot(fye[...], total[x * 48 : x * 48 + 48], 0, 0)
    for x in range(4):
        mixed[256 + x * 32 : 288 + x * 32] = dot(fy[...], total_faces[x * 32 : x * 32 + 32], 0, 0)
    for planes, first in ((8, 0), (4, 8)):
        lane = lanes_of(planes)
        for j in range(8):
            rows = [pl.ds(32 * first + 4 * j + b, planes, stride=32) for b in range(4)]
            tiles = [mixed[at, :] for at in rows]
            for k in range(4):
                tile = jnp.zeros((planes, 128), F32)
                for b in range(4):
                    tile = jnp.where(within(lane, 32 * b, 32), roll(tiles[b], 32 * (b - k)), tile)
                for t in range(planes // 4):
                    at = 32 * first + 128 * t
                    out[j * 4 + k, :, at : at + 128] = tile[4 * t : 4 * t + 4]


def contract_x(parts, fx, e_even, e_odd, out):
    total = parts[0]
    for p in range(1, parts.shape[0]):
        total = total + parts[p]
    e_low, e_high = sides("gx", e_even, e_odd)
    outer = [e_low(33, slice(6, 8), slice(0, 32)), e_high(33, slice(0, 2), slice(0, 32))]
    outer = jnp.concatenate(outer, axis=0)
    result = dot(fx[0:4], total[:, 0:128], 0, 0) + dot(fx[4:8], total[:, 128:256], 0, 0)
    out[...] = result + dot(outer, total[:, 256:384], 0, 0)


def local(fields, velocity, diffusivity, coupling, factor_x, factor_y, factor_z):
    def swapped(axis, even, odd):
        last = lax.axis_size(axis) - 1
        pairs = [[(i, i + 1) for i in range(first, last, 2)] for first in (0, 1)]
        even_pairs, odd_pairs = ([*p, *((b, a) for a, b in p)] for p in pairs)
        even = lax.ppermute(even, axis, even_pairs)
        return even, lax.ppermute(odd, axis, odd_pairs)

    inputs = (fields, velocity, factor_z.T, factor_y, factor_x)
    x_even, x_odd, z_even, z_odd, fields, velocity, fz, fy, fx = call(
        pack_xz,
        [f32(36, 32, 128)] * 2 + [f32(8, 32, 128)] * 2 + [f32(*a.shape) for a in inputs],
        [hbm()] * 5,
        scratch=[pltpu.SemaphoreType.DMA((5,))],
    )(*in_hbm(*inputs))
    z_even, z_odd = swapped("gz", z_even, z_odd)
    y_even, y_odd = call(pack_y, [f32(49, 8, 128)] * 2, [vmem()] * 5)(
        fields, velocity, fy, z_even, z_odd
    )
    y_even, y_odd = swapped("gy", y_even, y_odd)
    x_even, x_odd = swapped("gx", x_even, x_odd)
    e_even, e_odd = call(pack_x2, [f32(34, 8, 128)] * 2, [vmem()] * 5)(
        z_even, z_odd, y_even, y_odd, fx
    )
    e_even, e_odd = swapped("gx", e_even, e_odd)

    def tiles(*lead):
        return f32(*lead, ROWS, 128)

    gx = lax.axis_size("gx")
    buffers = [
        tiles(4, PLANES), tiles(4, PLANES), tiles(PLANES), tiles(PLANES),
        tiles(3, PLANES), tiles(3, PLANES), tiles(PLANES),
    ]
    scalars = [pltpu.SMEM((4,), F32), pltpu.SMEM((4, 4), F32), pltpu.SemaphoreType.DMA((2,))]
    diffusivity, coupling = in_hbm(diffusivity, coupling)
    *filled, rhs = call(
        prepare_own, [*buffers, f32(4, 128, 256)], [hbm()] * 2 + [vmem()] * 5, scratch=scalars, work=2000000
    )(diffusivity, coupling, fields, velocity, z_even, z_odd, fz)
    *filled, fye = call(
        prepare,
        [*buffers, f32(48, 32)],
        [hbm()] * 2 + [vmem()] * 10,
        scratch=scalars,
        work=2000000,
        aliases={5 + n: n for n in range(7)},
    )(diffusivity, coupling, y_even, y_odd, fy, *filled)
    parts, *_ = call(
        advance,
        [f32(32, 4, 384), *buffers],
        [hbm()] * 2 + [vmem()] * 14,
        scratch=[
            pltpu.VMEM((4, 384, 256), F32), pltpu.VMEM((4, 128, 128), F32),
            pltpu.VMEM((512, 128), F32), *scalars,
        ],
        work=10000000,
        aliases={9 + n: 1 + n for n in range(7)},
    )(diffusivity, coupling, x_even, x_odd, e_even, e_odd, fy, rhs, fye, *filled)
    parts = lax.all_to_all(parts, ("gy", "gz"), 0, 0, tiled=True)
    slices = call(contract_x, f32(32, 128), [vmem()] * 4)(
        parts, fx, e_even, e_odd
    )
    slices = lax.all_to_all(slices, "gx", 0, 0, tiled=True)
    core = jnp.sum(slices.reshape(gx, 32 // gx, 4, 4, 8), axis=0)
    return core.transpose(2, 0, 1, 3)


def solution(mesh):
    return jax.shard_map(
        local,
        mesh=mesh,
        in_specs=(
            P(None, "gx", "gy", "gz"),
            P(None, "gx", "gy", "gz"),
            P(),
            P(),
            P("gx", None),
            P("gy", None),
            P("gz", None),
        ),
        out_specs=P(None, "gx", "gy", "gz"),
        check_vma=False,
    )
```
